32 devices in a mesh: wide: 8 (over z, y), narrow: 4 (over x, core).
Axes of the slice: x: 2, y: 2, z: 4, core: 2. Of those that a mesh axis runs over, the one named last changes fastest.
Arguments:
- block_input: bfloat16 [16384, 1024], P(('wide', 'narrow')), may hold values from -6 to 6
- doc_lengths: int32 [8, 4], P('wide'), may hold values from 1 to 1024, 2048 in all within a row
- mixer_gain: bfloat16 [1024], replicated, may hold values from 0.5 to 1.5
- query_proj: bfloat16 [1024, 512], P(None, 'narrow'), may hold values from -0.1875 to 0.1875
- key_proj: bfloat16 [1024, 512], P(None, 'narrow'), may hold values from -0.1875 to 0.1875
- value_proj: bfloat16 [1024, 1024], P(None, 'narrow'), may hold values from -0.1875 to 0.1875
- outgate_proj: bfloat16 [1024, 1024], P(None, 'narrow'), may hold values from -0.1875 to 0.1875
- decay_down: bfloat16 [1024, 16], replicated, may hold values from -0.1875 to 0.1875
- decay_up: bfloat16 [16, 512], P(None, 'narrow'), may hold values from -1.5 to 1.5
- decay_bias: bfloat16 [512], P('narrow'), may hold values from -6 to 6
- group_gain: bfloat16 [256], replicated, may hold values from 0.5 to 1.5
- output_proj: bfloat16 [1024, 1024], P('narrow'), may hold values from -0.1875 to 0.1875
- ffn_gain: bfloat16 [1024], replicated, may hold values from 0.5 to 1.5
- gate_proj: bfloat16 [1024, 2816], P(None, 'narrow'), may hold values from -0.1875 to 0.1875
- up_proj: bfloat16 [1024, 2816], P(None, 'narrow'), may hold values from -0.1875 to 0.1875
- down_proj: bfloat16 [2816, 1024], P('narrow'), may hold values from -0.109375 to 0.109375
- cotangent: bfloat16 [16384, 1024], P(('wide', 'narrow')), may hold values from -6 to 6
Outputs:
- block_output: bfloat16 [16384, 1024], P(('wide', 'narrow'))
- input_grad: bfloat16 [16384, 1024], P(('wide', 'narrow'))
- grad_mixer_gain: float32 [1024], replicated
- grad_query: float32 [1024, 512], P(None, 'narrow')
- grad_key: float32 [1024, 512], P(None, 'narrow')
- grad_value: float32 [1024, 1024], P(None, 'narrow')
- grad_outgate: float32 [1024, 1024], P(None, 'narrow')
- grad_decay_down: float32 [1024, 16], replicated
- grad_decay_up: float32 [16, 512], P(None, 'narrow')
- grad_decay_bias: float32 [512], P('narrow')
- grad_group_gain: float32 [256], replicated
- grad_output: float32 [1024, 1024], P('narrow')
- grad_ffn_gain: float32 [1024], replicated
- grad_gate: float32 [1024, 2816], P(None, 'narrow')
- grad_up: float32 [1024, 2816], P(None, 'narrow')
- grad_down: float32 [2816, 1024], P('narrow')
The draws below stay inside these ranges and needn't reach their ends.
Inputs may be any that keep to these rules, and one draw needn't show every extreme that they name: Row w of doc_lengths holds the lengths of the 4 documents packed in order into group w; they sum to 2048.
All inputs are finite; a program needn't handle non-finite values.
Results may differ from the reference program's by a relative error of at most 0.025.
Values may be sent and summed in bfloat16 or wider, within the bound.
No kernel may reach another device: no remote copies, remote signals or barrier semaphores. Data moves between devices by JAX's collectives and lax.ppermute only.
A program may use at most 192 MiB of HBM per device.

```python
import math
import jax
import jax.numpy as jnp
import numpy as np
from jax import lax

D = 1024
HEADS = 4
HK = 128
HV = 256
FF = 2816
RANK = 16
SPAN = 64
DOCS = 4
GROUP_TOK = 2048
TOKENS = 16384
N_WIDE = 8


def block_scale(own_key, dims, pieces, least, largest):
    factor_of, own = 1.0, jax.random.fold_in(own_key, 6)
    for dim, parts in pieces:
        heights = jnp.exp(jax.random.uniform(jax.random.fold_in(own, dim), (parts,), jnp.float32, least / len(pieces), largest / len(pieces)))
        factor_of = factor_of * jnp.repeat(heights, dims[dim] // parts).reshape([-1 if axis == dim else 1 for axis in range(len(dims))])
    return factor_of


def split_up(amount, total, bound, lean):
    loads = [(1 << 20) // math.isqrt(standing ** lean) + 1 for standing in range(2, amount + 1)]
    surplus, holding = total - bound - (amount - 1), [1] * (amount - 1)
    while surplus > 0:
        candidates = [i for i in range(amount - 1) if holding[i] < bound]
        pool, remaining = sum([loads[i] for i in candidates]), surplus
        for i in candidates:
            addition = min(bound - holding[i], max(1, remaining * loads[i] // pool), surplus)
            holding[i] = holding[i] + addition
            surplus = surplus - addition
    return np.array([bound] + holding)


def ragged(own_key, count, total, most, slope):
    if count == 2:
        one = jax.random.randint(own_key, (), max(1, total - most), min(most, total - 1) + 1)
        return jnp.stack([one, total - one])
    tallies = jnp.asarray(split_up(count, total, most, slope), jnp.int32)
    couples = (count - 1) // 2
    giver, receiver = tallies[1:1 + 2 * couples:2], tallies[2:2 + 2 * couples:2]
    slack = jnp.minimum(giver - 1, most - receiver)
    shifted = jax.random.randint(jax.random.fold_in(own_key, 1), (couples,), 0, 1 << 20) % (slack + 1)
    tallies = tallies.at[1:1 + 2 * couples:2].set(giver - shifted).at[2:2 + 2 * couples:2].set(receiver + shifted)
    return tallies[jax.random.permutation(jax.random.fold_in(own_key, 2), count)]


def scatter_about(rng, shape, spread, limit, pieces=(), held_as=jnp.bfloat16):
    result = jax.random.normal(rng, shape, jnp.float32) * spread
    if len(pieces) > 0:
        result = block_scale(rng, shape, pieces, -0.22, 0.18) * result
    return jnp.clip(result, min=-limit, max=limit).astype(held_as)


def setup_inputs(seed: int = 0) -> dict:
    arg_keys = jax.random.split(jax.random.key(seed), 18)
    return {
        "block_input": scatter_about(arg_keys[0], (TOKENS, D), 1.0, 6.0, ((0, 32),)),
        "doc_lengths": jax.vmap(lambda own: ragged(own, DOCS, GROUP_TOK, GROUP_TOK // 2, 2))(jax.random.split(arg_keys[1], N_WIDE)).reshape((N_WIDE, DOCS)).astype(jnp.int32),
        "mixer_gain": jnp.clip(1.0 + 0.1 * jax.random.normal(arg_keys[2], (D,), jnp.float32), 0.5, 1.5).astype(jnp.bfloat16),
        "query_proj": scatter_about(arg_keys[3], (D, HEADS * HK), D ** -0.5, 0.1875, ((1, 4),)),
        "key_proj": scatter_about(arg_keys[4], (D, HEADS * HK), D ** -0.5, 0.1875, ((1, 4),)),
        "value_proj": scatter_about(arg_keys[5], (D, HEADS * HV), D ** -0.5, 0.1875, ((1, 4),)),
        "outgate_proj": scatter_about(arg_keys[6], (D, HEADS * HV), D ** -0.5, 0.1875, ((1, 4),)),
        "decay_down": scatter_about(arg_keys[7], (D, RANK), D ** -0.5, 0.1875),
        "decay_up": scatter_about(arg_keys[8], (RANK, HEADS * HK), RANK ** -0.5, 1.5, ((1, 4),)),
        "decay_bias": scatter_about(arg_keys[9], (HEADS * HK,), 1.5, 6.0, ((0, 4),)),
        "group_gain": jnp.clip(1.0 + 0.1 * jax.random.normal(arg_keys[10], (HV,), jnp.float32), 0.5, 1.5).astype(jnp.bfloat16),
        "output_proj": scatter_about(arg_keys[11], (HEADS * HV, D), (HEADS * HV) ** -0.5, 0.1875, ((0, 4),)),
        "ffn_gain": jnp.clip(1.0 + 0.1 * jax.random.normal(arg_keys[12], (D,), jnp.float32), 0.5, 1.5).astype(jnp.bfloat16),
        "gate_proj": scatter_about(arg_keys[13], (D, FF), D ** -0.5, 0.1875, ((1, 4),)),
        "up_proj": scatter_about(arg_keys[14], (D, FF), D ** -0.5, 0.1875, ((1, 4),)),
        "down_proj": scatter_about(arg_keys[15], (FF, D), FF ** -0.5, 0.109375, ((0, 4),)),
        "cotangent": scatter_about(arg_keys[16], (TOKENS, D), 1.0, 6.0, ((0, 32),)),
    }


@jax.custom_vjp
def low(v):
    return lax.optimization_barrier(v.astype(jnp.bfloat16)).astype(jnp.float32)

@jax.custom_vjp
def low_back(v):
    return v

def low_keep(v):
    return (low(v), None)

def low_pass(kept, grad):
    return (grad,)

def back_keep(v):
    return (v, None)

def back_low(kept, grad):
    return (low(grad),)
low.defvjp(low_keep, low_pass)
low_back.defvjp(back_keep, back_low)
epsilon = 1e-06
group_floor = 0.25
highest = lax.Precision.HIGHEST

def product(left, right):
    return jnp.dot(left, right, precision=highest, preferred_element_type=jnp.float32)

def segment_ids(length_row, count):
    ends = jnp.cumsum(length_row).astype(jnp.int32)
    places = jnp.arange(count, dtype=jnp.int32)
    return lax.optimization_barrier(jnp.sum((places[:, None] >= ends[None, :]).astype(jnp.int32), axis=1)).astype(jnp.int32)

def span_step(carry, block):
    state, previous = carry
    query, key, value, decay, seg = block
    width = query.shape[0]
    places = jnp.arange(width, dtype=jnp.int32)
    allowed = ((places[:, None] >= places[None, :]) & (seg[:, None] == seg[None, :])).astype(state.dtype)
    csum = jnp.cumsum(decay, axis=0)
    centre = csum[width // 2][None, :]
    scores = lax.dot_general(query * jnp.exp(csum - centre), key * jnp.exp(centre - csum), (((1,), (1,)), ((), ())), precision=highest) * allowed
    inside = product(scores, value)
    living = (seg == previous).astype(state.dtype)
    carried = product(query * jnp.exp(csum), state) * living[:, None]
    final = seg[width - 1]
    alive = (final == previous).astype(state.dtype)
    tail = jnp.exp(csum[width - 1][None, :] - csum) * (seg == final).astype(state.dtype)[:, None]
    added = lax.dot_general(key * tail, value, (((0,), (0,)), ((), ())), precision=highest)
    new_state = jnp.exp(csum[width - 1])[:, None] * state * alive + added
    return ((new_state, final), inside + carried)

def decay_scan(query, key, value, decay, seg):
    count = query.shape[0] // SPAN
    blocks = (query.reshape(count, SPAN, query.shape[1]), key.reshape(count, SPAN, key.shape[1]), value.reshape(count, SPAN, value.shape[1]), decay.reshape(count, SPAN, decay.shape[1]), seg.reshape(count, SPAN))
    start = (jnp.zeros((query.shape[1], value.shape[1]), query.dtype), jnp.array(-1, jnp.int32))
    unused, outputs = lax.scan(jax.checkpoint(span_step), start, blocks)
    return outputs.reshape(query.shape[0], value.shape[1])

def block_group(params, inputs, seg):
    mixer_gain, query_proj, key_proj, value_proj, outgate_proj, decay_down, decay_up, decay_bias, group_gain, output_proj, ffn_gain, gate_proj, up_proj, down_proj = params
    token_count = inputs.shape[0]
    scale_one = lax.rsqrt(lax.optimization_barrier(jnp.mean(inputs * inputs, axis=-1, keepdims=True)) + epsilon)
    normed = low(inputs * scale_one * mixer_gain)
    query = low(low_back(product(normed, query_proj)))
    key = low(low_back(product(normed, key_proj)))
    value = low(low_back(product(normed, value_proj)))
    gate_out = low_back(product(normed, outgate_proj))
    raw = product(product(normed, decay_down), decay_up) + decay_bias
    decay = jax.nn.log_sigmoid(raw) / 16.0
    mixed = jax.vmap(decay_scan, in_axes=(1, 1, 1, 1, None), out_axes=1)((query * HK ** (-0.5)).reshape(token_count, HEADS, HK), key.reshape(token_count, HEADS, HK), value.reshape(token_count, HEADS, HV), decay.reshape(token_count, HEADS, HK), seg)
    inverse = lax.rsqrt(lax.optimization_barrier(jnp.mean(mixed * mixed, axis=-1, keepdims=True)) + group_floor)
    gated = (mixed * inverse * group_gain).reshape(token_count, HEADS * HV) * jax.nn.silu(gate_out)
    merged = low(low_back(gated))
    resid = inputs + low_back(product(merged, output_proj))
    scale_two = lax.rsqrt(lax.optimization_barrier(jnp.mean(resid * resid, axis=-1, keepdims=True)) + epsilon)
    normed_two = low(resid * scale_two * ffn_gain)
    gate = low_back(product(normed_two, gate_proj))
    upper = low_back(product(normed_two, up_proj))
    hidden = low(low_back(jax.nn.silu(gate) * upper))
    return resid + low_back(product(hidden, down_proj))

def reference(block_input, doc_lengths, mixer_gain, query_proj, key_proj, value_proj, outgate_proj, decay_down, decay_up, decay_bias, group_gain, output_proj, ffn_gain, gate_proj, up_proj, down_proj, cotangent):
    params = (mixer_gain.astype(jnp.float32), query_proj.astype(jnp.float32), key_proj.astype(jnp.float32), value_proj.astype(jnp.float32), outgate_proj.astype(jnp.float32), decay_down.astype(jnp.float32), decay_up.astype(jnp.float32), decay_bias.astype(jnp.float32), group_gain.astype(jnp.float32), output_proj.astype(jnp.float32), ffn_gain.astype(jnp.float32), gate_proj.astype(jnp.float32), up_proj.astype(jnp.float32), down_proj.astype(jnp.float32))
    inputs = block_input.astype(jnp.float32).reshape(N_WIDE, GROUP_TOK, D)

    def one_segs(length_row):
        return segment_ids(length_row, GROUP_TOK)
    segs = jax.vmap(one_segs)(doc_lengths)

    def forward(values, weights):

        def one_group(pair):
            return block_group(weights, pair[0], pair[1])
        return lax.map(one_group, (values, segs))
    outputs, pullback = jax.vjp(forward, inputs, params)
    input_grad, grads = pullback(cotangent.astype(jnp.float32).reshape(N_WIDE, GROUP_TOK, D))
    return (outputs.reshape(TOKENS, D).astype(jnp.bfloat16), input_grad.reshape(TOKENS, D).astype(jnp.bfloat16), grads[0], grads[1], grads[2], grads[3], grads[4], grads[5], grads[6], grads[7], grads[8], grads[9], grads[10], grads[11], grads[12], grads[13])
```

```python
import functools

import jax
import jax.numpy as jnp
from jax import lax
from jax.experimental import pallas as pl
from jax.experimental.pallas import tpu as pltpu
from jax.sharding import PartitionSpec as P

HK = 128
HV = 256
SPAN = 64
ROWS = 256
NB = ROWS // SPAN

epsilon = 1e-06
group_floor = 0.25
highest = lax.Precision.HIGHEST
f32 = jnp.float32
bf16 = jnp.bfloat16
scale_q = HK ** (-0.5)


def nn(a, b, precision=None):
    return lax.dot_general(
        a, b, (((1,), (0,)), ((), ())), precision=precision, preferred_element_type=f32
    )


def nt(a, b, precision=None):
    return lax.dot_general(
        a, b, (((1,), (1,)), ((), ())), precision=precision, preferred_element_type=f32
    )


def tn(a, b, precision=None):
    return lax.dot_general(
        a, b, (((0,), (0,)), ((), ())), precision=precision, preferred_element_type=f32
    )


def sigmoid(v):
    return 1.0 / (1.0 + jnp.exp(-v))


def rows_cols():
    i = lax.broadcasted_iota(jnp.int32, (ROWS, ROWS), 0)
    j = lax.broadcasted_iota(jnp.int32, (ROWS, ROWS), 1)
    return i, j


def block_low():
    i, j = rows_cols()
    return (i >= j) & (i // SPAN == j // SPAN)


def doc_start(info, pos):
    e1, e2, e3 = info[2], info[3], info[4]
    start = jnp.where(pos >= e1, e1, 0)
    start = jnp.where(pos >= e2, e2, start)
    return jnp.where(pos >= e3, e3, start)


def scalar_start(info, pos):
    e1, e2, e3 = info[2], info[3], info[4]
    start = jnp.where(pos >= e1, e1, 0)
    start = jnp.where(pos >= e2, e2, start)
    return jnp.where(pos >= e3, e3, start)


def spread(v, row):
    return jnp.concatenate(
        [
            jnp.broadcast_to(v[b * SPAN + row : b * SPAN + row + 1], (SPAN, v.shape[1]))
            for b in range(NB)
        ],
        axis=0,
    )


def pick(info, s, own, sib):
    use_own = (s // 2) == info[0]
    return jnp.where(use_own, own[...], sib[...])


def both(own, par):
    return jnp.concatenate([own[...], par[...]], axis=1)


def project_kernel(
    info, own, sib, k_own, v_own, u_own, kvu, down, key, value, raw, csum, state, acc
):
    s = pl.program_id(0)
    x = pick(info, s, own, sib)
    width = x.shape[1]
    k_par, v_par, u_par = kvu.at[:width, :HK], kvu.at[:width, HK:], kvu.at[width:, :HK]
    ko = nn(x, both(k_own, k_par))
    k = ko.astype(bf16)
    key[...] = k
    v0 = nn(x, v_own[...]).astype(bf16)
    v1 = nn(x, v_par[...]).astype(bf16)
    value[:, :HV] = v0
    value[:, HV:] = v1
    low = nt(x, down[...])
    up = both(u_own, u_par).astype(f32)
    raws = nn(low, up[:16], highest) + up[16:17]
    raw[...] = raws
    decay = (jnp.minimum(raws, 0.0) - jnp.log1p(jnp.exp(-jnp.abs(raws)))) * (1.0 / 16.0)
    i, j = rows_cols()
    csum[...] = nn(block_low().astype(f32), decay, highest)
    rest = nn((j > i).astype(f32), decay, highest)
    total = rest[0:1] + decay[0:1]
    base = info[1] + s * ROWS
    last = scalar_start(info, base + ROWS - 1)
    pos = base + lax.broadcasted_iota(jnp.int32, (ROWS, 1), 0)
    tail = jnp.where(pos >= last, 1.0, 0.0)
    alive = jnp.where((last < base) & (s > 0), 1.0, 0.0)
    ks = (k.astype(f32) * jnp.exp(rest) * tail).astype(bf16)
    keep = jnp.exp(total) * alive

    @pl.when(s == 0)
    def _():
        acc[...] = jnp.zeros_like(acc)

    for h, v in enumerate((v0, v1)):
        hs = slice(h * HK, (h + 1) * HK)
        acc[h] = acc[h] * keep[:, hs] + tn(v, ks[:, hs])

    @pl.when(s == 3)
    def _():
        state[0] = acc[1].astype(bf16)
        state[1] = acc[0].astype(bf16)


def factors(info, s, cs):
    base = info[1] + s * ROWS
    row = lax.broadcasted_iota(jnp.int32, (ROWS, 1), 0)
    pos = base + row
    start = doc_start(info, pos)
    living = jnp.where(start < base + (row // SPAN) * SPAN, 1.0, 0.0)
    final = doc_start(info, base + (row // SPAN) * SPAN + SPAN - 1)
    tail = jnp.where(pos >= final, 1.0, 0.0)
    alive = []
    for b in range(NB):
        first = base + b * SPAN
        alive.append(jnp.where(scalar_start(info, first + SPAN - 1) < first, 1.0, 0.0))
    i, j = rows_cols()
    mask = block_low() & (base + j >= start)
    return living, tail, alive, mask


def forward_kernel(
    info, own, sib, q_own, o_own, qo, gain, key, value, csum, entering,
    query, gate_out, mixed, merged, states, acc,
):
    s = pl.program_id(0)
    x = pick(info, s, own, sib)
    q_par, o_par = qo.at[:, :HK], qo.at[:, HK:]
    q = nn(x, both(q_own, q_par)).astype(bf16)
    query[...] = q
    living, tail, alive, mask = factors(info, s, None)

    @pl.when(s == 0)
    def _():
        acc[...] = entering[...].astype(f32)

    for h in range(2):
        w = o_own if h == 0 else o_par
        hs, vs = slice(h * HK, (h + 1) * HK), slice(h * HV, (h + 1) * HV)
        go = nn(x, w[...])
        gate_out[:, vs] = go
        cs = csum[:, hs]
        centre, last = spread(cs, SPAN // 2), spread(cs, SPAN - 1)
        qt = q[:, hs].astype(f32) * scale_q
        k = key[:, hs].astype(f32)
        v = value[:, vs]
        qe = (qt * jnp.exp(cs - centre)).astype(bf16)
        ke = (k * jnp.exp(centre - cs)).astype(bf16)
        qc = (qt * jnp.exp(cs) * living).astype(bf16)
        kt = (k * jnp.exp(last - cs) * tail).astype(bf16)
        scores = jnp.where(mask, nt(qe, ke), 0.0).astype(bf16)
        inside = nn(scores, v)
        st = acc[h]
        carried = []
        for b in range(NB):
            r = slice(b * SPAN, (b + 1) * SPAN)
            stb = st.astype(bf16)
            states[0, h, b] = stb
            carried.append(nt(qc[r], stb))
            f = jnp.exp(cs[(b + 1) * SPAN - 1 : (b + 1) * SPAN]) * alive[b]
            st = st * f + tn(v[r], kt[r])
        acc[h] = st
        mix = inside + jnp.concatenate(carried, axis=0)
        mixed[:, vs] = mix
        inv = lax.rsqrt(jnp.mean(mix * mix, axis=-1, keepdims=True) + group_floor)
        mer = (mix * inv * gain[...] * (go * sigmoid(go))).astype(bf16)
        merged[:, vs] = mer


def gate_back_kernel(
    info, own, sib, out_own, out_par, gain, mixed, gate_out, query, csum,
    mixed_grad, gate_grad, gate_own, gate_par, gain_grad, enter_grad, acc, carry,
):
    s = pl.program_id(0)
    g = pick(info, s, own, sib)

    @pl.when(s == 0)
    def _():
        acc[...] = jnp.zeros_like(acc)
        carry[...] = jnp.zeros_like(carry)
        gain_grad[...] = jnp.zeros_like(gain_grad)

    base = info[1] + s * ROWS
    pos = base + lax.broadcasted_iota(jnp.int32, (ROWS, 1), 0)
    living = jnp.where(doc_start(info, pos) < info[1], 1.0, 0.0)
    for h in range(2):
        wo = out_own if h == 0 else out_par
        hs, vs = slice(h * HK, (h + 1) * HK), slice(h * HV, (h + 1) * HV)
        mg = nt(g, wo[...]).astype(bf16).astype(f32)
        mix = mixed[:, vs]
        go = gate_out[:, vs]
        gn = gain[...]
        inv = lax.rsqrt(jnp.mean(mix * mix, axis=-1, keepdims=True) + group_floor)
        n = mix * inv
        sg = sigmoid(go)
        silu = go * sg
        ng = mg * n
        dgo = (ng * gn * (sg + silu * (1.0 - sg))).astype(bf16)
        gate_grad[:, vs] = dgo
        (gate_own if h == 0 else gate_par)[...] = dgo
        gain_grad[...] += jnp.sum(ng * silu, axis=0, keepdims=True)
        dn = mg * gn * silu
        do = (inv * (dn - n * jnp.mean(dn * n, axis=-1, keepdims=True))).astype(bf16)
        mixed_grad[:, vs] = do
        cs = csum[:, hs]
        offset = carry[:, hs]
        parts = []
        for b in range(NB):
            parts.append(cs[b * SPAN : (b + 1) * SPAN] + offset)
            offset = offset + cs[(b + 1) * SPAN - 1 : (b + 1) * SPAN]
        carry[:, hs] = offset
        qcc = query[:, hs].astype(f32) * scale_q * jnp.exp(jnp.concatenate(parts, axis=0)) * living
        acc[h] += tn(do, qcc.astype(bf16))

    @pl.when(s == 3)
    def _():
        enter_grad[0] = acc[1].astype(bf16)
        enter_grad[1] = acc[0].astype(bf16)


def backward_kernel(
    info, own, sib, q_w, o_w, k_w, v_w, u_w, down,
    query, key, value, csum, raw, mixed_grad, gate_grad, states, leaving, *rest,
):
    given, rest = (rest[:1], rest[1:]) if len(rest) == 8 else ((), rest)
    kvq_grad, up_grad, bias_grad, down_grad, *outs, acc = rest
    step = pl.program_id(0)
    s = 3 - step
    x = pick(info, s, own, sib)

    @pl.when(step == 0)
    def _():
        acc[...] = leaving[0].astype(f32)
        up_grad[...] = jnp.zeros_like(up_grad)
        bias_grad[...] = jnp.zeros_like(bias_grad)
        down_grad[...] = jnp.zeros_like(down_grad)

    living, tail, alive, mask = factors(info, s, None)
    lower = block_low().astype(f32)
    cs = csum[...]
    centre, last = spread(cs, SPAN // 2), spread(cs, SPAN - 1)
    qt = query[...].astype(f32) * scale_q
    k = key[...].astype(f32)
    v = value[...]
    do = mixed_grad[...]
    eq, ek = jnp.exp(cs - centre), jnp.exp(centre - cs)
    ec, et = jnp.exp(cs) * living, jnp.exp(last - cs) * tail
    qe, ke = (qt * eq).astype(bf16), (k * ek).astype(bf16)
    qcf, ktf = qt * ec, k * et
    qc, kt = qcf.astype(bf16), ktf.astype(bf16)
    scores = jnp.where(mask, nt(qe, ke), 0.0).astype(bf16)
    ds = jnp.where(mask, nt(do, v), 0.0).astype(bf16)
    dqe = nn(ds, ke)
    dke = tn(ds, qe)
    dv = tn(scores, do)
    gt = acc[...]
    dqc, dkt, dvt, dlast = [None] * NB, [None] * NB, [None] * NB, [None] * NB
    for b in reversed(range(NB)):
        r = slice(b * SPAN, (b + 1) * SPAN)
        gtb = gt.astype(bf16)
        st = states[0, 0, b]
        dvt[b] = nt(kt[r], gtb)
        dkt[b] = nn(v[r], gtb)
        dqc[b] = nn(do[r], st)
        f = jnp.exp(cs[(b + 1) * SPAN - 1 : (b + 1) * SPAN]) * alive[b]
        moved = f * jnp.sum(st.astype(f32) * gt, axis=0, keepdims=True)
        tails = jnp.sum(ktf[r] * dkt[b], axis=0, keepdims=True)
        dlast[b] = jnp.broadcast_to(moved + tails, (SPAN, HK))
        gt = gt * f + tn(do[r], qc[r])
    acc[...] = gt
    dqc = jnp.concatenate(dqc, axis=0)
    dkt = jnp.concatenate(dkt, axis=0)
    dv = (dv + jnp.concatenate(dvt, axis=0)).astype(bf16)
    dq = ((dqe * eq + dqc * ec) * scale_q).astype(bf16)
    dk = (dke * ek + dkt * et).astype(bf16)
    dc = qe.astype(f32) * dqe - ke.astype(f32) * dke + qcf * dqc - ktf * dkt
    ddecay = tn(lower, dc, highest) + jnp.concatenate(dlast, axis=0)
    raw_grad = ddecay * sigmoid(-raw[...]) * (1.0 / 16.0)
    kvq_grad[:, :HK] = dk
    kvq_grad[:, HK : HK + HV] = dv
    kvq_grad[:, HK + HV :] = dq
    up = u_w[:16].astype(f32)
    rank_low = nt(raw_grad, up, highest).astype(bf16)
    low = nt(x, down[...])
    up_grad[...] += tn(low, raw_grad, highest)
    bias_grad[...] += jnp.sum(raw_grad, axis=0, keepdims=True)
    down_grad[...] += tn(rank_low, x)
    back = nt(dv, v_w[...]) + nt(gate_grad[...], o_w[...]) + nn(rank_low, down[...])
    back = back + nt(
        jnp.concatenate([dq, dk], axis=1), jnp.concatenate([q_w[...], k_w[...]], axis=1)
    )
    if not given:
        outs[0][...] = back
        return
    back = back + given[0][...]
    use_own = (s // 2) == info[0]

    @pl.when(use_own)
    def _():
        outs[0][...] = back.astype(bf16)

    @pl.when(jnp.logical_not(use_own))
    def _():
        outs[1][...] = back.astype(bf16)


def ffn_kernel(
    place, n_a, n_b, g_ref, gate_w, up_w, down_w, *rest,
):
    hidden, gate_grad, up_grad, n_cat, g_cat, back_a, back_b, feed_a, feed_b = rest[-9:]
    i = pl.program_id(0)
    first = i < pl.num_programs(0) // 2
    n = jnp.where(first, n_a[...], n_b[...])
    g = g_ref[...]
    n_cat[...] = n
    g_cat[...] = g
    gate = nt(n, gate_w[...])
    up = nt(n, up_w[...])
    gh = nt(g, down_w[...]).astype(bf16).astype(f32)
    sg = sigmoid(gate)
    silu = gate * sg
    hid = (silu * up).astype(bf16)
    gg = (gh * up * (sg + silu * (1.0 - sg))).astype(bf16)
    ug = (gh * silu).astype(bf16)
    hidden[...] = hid
    gate_grad[...] = gg
    up_grad[...] = ug
    feed = nn(hid, down_w[...]).astype(bf16)
    back = (nn(gg, gate_w[...]) + nn(ug, up_w[...])).astype(bf16)

    @pl.when(first)
    def _():
        feed_a[...] = feed
        back_a[...] = back

    @pl.when(jnp.logical_not(first))
    def _():
        feed_b[...] = feed
        back_b[...] = back


def ffn_grad_kernel(*refs):
    outs, accs = refs[-6:-3], refs[-3:]
    i = pl.program_id(0)

    @pl.when(i == 0)
    def _():
        for acc in accs:
            acc[...] = jnp.zeros_like(acc)

    def add(h, gg, ug, n, g):
        for acc, left, right in zip(accs, (gg, ug, h), (n, n, g)):
            acc[...] += tn(left[...], right[...])

    pl.when(i < 2)(lambda: add(*refs[:5]))
    pl.when(i == 2)(lambda: add(*refs[5:10]))
    pl.when(i == 3)(lambda: add(*refs[10:15]))

    @pl.when(i == 3)
    def _():
        for out, acc in zip(outs, accs):
            out[...] = acc[...].astype(out.dtype)


def ffn_grad_call(groups, dtype, name, us):
    step, units = groups[1][0].shape
    width = groups[1][3].shape[1]
    out = jax.ShapeDtypeStruct((units, width), dtype)
    specs = []
    for k, group in enumerate(groups):
        for a in group:
            index = (lambda i: (jnp.minimum(i, 1), 0)) if k == 0 else (lambda i: (0, 0))
            specs.append(pl.BlockSpec((step, a.shape[1]), index))
    return pl.pallas_call(
        ffn_grad_kernel,
        out_shape=[out] * 3,
        grid=(4,),
        in_specs=specs,
        out_specs=[whole(out)] * 3,
        scratch_shapes=[pltpu.VMEM((units, width), f32)] * 3,
        compiler_params=params(44),
        cost_estimate=cost(us),
        name=name,
    )(*[a for group in groups for a in group])


def params(mib):
    return pltpu.CompilerParams(
        dimension_semantics=("arbitrary",), vmem_limit_bytes=mib * 1024 * 1024
    )


def cost(us):
    return pl.CostEstimate(flops=us * 1_000_000_000, transcendentals=0, bytes_accessed=us * 1_000_000)


def whole(a):
    zero = (0,) * a.ndim
    return pl.BlockSpec(a.shape, lambda *_: zero)


def resident():
    return pl.BlockSpec(memory_space=pltpu.VMEM)


def own_index(s, info):
    return jnp.where(info[0] == 0, jnp.minimum(s, 1), jnp.maximum(s - 2, 0))


def sib_index(s, info):
    return jnp.where(info[0] == 0, jnp.maximum(s - 2, 0), jnp.minimum(s, 1))


def phys_index(s, info):
    return jnp.where(info[0] == 0, s, (s + 2) % 4)


def mixer_call(kernel, info, ins, outs, scratch, name, us, mib, reverse=False):
    def at(s):
        return 3 - s if reverse else s

    def spec(a, kind):
        if isinstance(kind, tuple) and kind[0] == "col":
            cols = kind[2]
            return pl.BlockSpec((ROWS, cols), lambda s, info: (at(s), kind[1]))
        if isinstance(kind, tuple) and kind[0] == "head":
            return pl.BlockSpec((1, 1, *a.shape[2:]), lambda s, info: (at(s), kind[1], 0, 0, 0))
        if isinstance(kind, tuple) and kind[0] == "one":
            return pl.BlockSpec((1, *a.shape[1:]), lambda s, info: (kind[1], 0, 0))
        if kind == "own":
            return pl.BlockSpec((ROWS, a.shape[1]), lambda s, info: (own_index(at(s), info), 0))
        if kind == "sib":
            return pl.BlockSpec((ROWS, a.shape[1]), lambda s, info: (sib_index(at(s), info), 0))
        if kind == "seq":
            return pl.BlockSpec((ROWS, a.shape[1]), lambda s, info: (at(s), 0))
        if kind == "phy":
            return pl.BlockSpec((ROWS, a.shape[1]), lambda s, info: (phys_index(at(s), info), 0))
        if kind == "blk":
            zero = (0,) * (a.ndim - 1)
            return pl.BlockSpec((1, *a.shape[1:]), lambda s, info: (at(s), *zero))
        return resident() if kind == "vmem" else whole(a)

    return pl.pallas_call(
        kernel,
        out_shape=[a for a, _ in outs],
        grid_spec=pltpu.PrefetchScalarGridSpec(
            num_scalar_prefetch=1,
            grid=(4,),
            in_specs=[spec(a, kind) for a, kind in ins],
            out_specs=[spec(a, kind) for a, kind in outs],
            scratch_shapes=scratch,
        ),
        compiler_params=params(mib),
        cost_estimate=cost(us),
        name=name,
    )(info, *[a for a, _ in ins])


def ffn_call(place, n_a, n_b, g_all, gate_w, up_w, down_w, name, flip, part=0, feeds=()):
    rows, width = n_a.shape
    units = gate_w.shape[0]
    steps = 2 * rows // ROWS
    half = steps // 2
    per = g_all.shape[0] // 4 // ROWS

    def g_index(i, place):
        return (place[0] ^ (flip + i // half)) * per + part + i % half, 0

    lo = pl.BlockSpec((ROWS, width), lambda i, place: (jnp.minimum(i, half - 1), 0))
    hi = pl.BlockSpec((ROWS, width), lambda i, place: (jnp.maximum(i - half, 0), 0))
    at = part + (flip // 2) * per
    feed_lo = pl.BlockSpec((ROWS, width), lambda i, place: (jnp.minimum(i, half - 1) + at, 0))
    feed_hi = pl.BlockSpec((ROWS, width), lambda i, place: (jnp.maximum(i - half, 0) + at, 0))
    hbm = pl.BlockSpec(memory_space=pl.ANY)
    cat = pl.BlockSpec((ROWS, width), lambda i, place: (i, 0))
    mid = pl.BlockSpec((ROWS, units), lambda i, place: (i, 0))
    sds = jax.ShapeDtypeStruct
    return pl.pallas_call(
        ffn_kernel,
        out_shape=[sds((2 * rows, units), bf16)] * 3
        + [sds((2 * rows, width), bf16)] * 2
        + [sds((rows, width), bf16)] * 2
        + [sds((2 * per * ROWS, width), bf16)] * 2,
        grid_spec=pltpu.PrefetchScalarGridSpec(
            num_scalar_prefetch=1,
            grid=(steps,),
            in_specs=[lo, hi, pl.BlockSpec((ROWS, width), g_index), whole(gate_w), whole(up_w), whole(down_w)]
            + [hbm] * len(feeds),
            out_specs=[mid, mid, mid, cat, cat, lo, hi, feed_lo, feed_hi],
        ),
        input_output_aliases={7 + k: 7 + k for k in range(len(feeds))},
        compiler_params=params(32),
        cost_estimate=cost(3 * steps + 2),
        name=name,
    )(place, n_a, n_b, g_all, gate_w, up_w, down_w, *feeds)


def across(v, bit):
    return lax.ppermute(v, "narrow", [(i, i ^ bit) for i in range(4)])


def forth(v):
    return lax.ppermute(v, "narrow", [(0, 2), (1, 3)])


def back_to(v):
    return lax.ppermute(v, "narrow", [(2, 0), (3, 1)])


def after(v, *others):
    return lax.optimization_barrier((v, *others))[0]


def pairs(count, bit):
    return [(i, i ^ bit) for i in range(count)]


def wide_send(v, bit, count):
    half = v.shape[0] // 2
    high = (lax.axis_index("wide") // bit) % 2
    keep = lax.dynamic_slice_in_dim(v, high * half, half, 0)
    send = lax.dynamic_slice_in_dim(v, (1 - high) * half, half, 0)
    return keep, lax.ppermute(send, "wide", pairs(count, bit))


def wide_add(keep, got, *earlier):
    got = after(got, *earlier) if earlier else got
    return (keep.astype(f32) + got.astype(f32)).astype(bf16)


def wide_start(v, order, count):
    for bit in order:
        v = wide_add(*wide_send(v, bit, count))
    return v


def wide_end(v, gone, order, count):
    place = lax.axis_index("wide")
    v = wide_start(v, order[gone:], count)
    for bit in reversed(order):
        high = (place // bit) % 2
        got = lax.ppermute(v, "wide", pairs(count, bit))
        v = jnp.where(high == 0, jnp.concatenate([v, got], 0), jnp.concatenate([got, v], 0))
    return v


def wide_sum(v, order, count):
    return wide_end(v, 0, order, count)


def body(
    count, block_input, doc_lengths, mixer_gain, query_proj, key_proj, value_proj, outgate_proj,
    decay_down, decay_up, decay_bias, group_gain, output_proj, ffn_gain, gate_proj, up_proj,
    down_proj, cotangent,
):
    sds = jax.ShapeDtypeStruct
    rows, width = block_input.shape
    chip = 2 * rows
    place = lax.axis_index("narrow")
    lengths = doc_lengths[0]
    e1 = lengths[0]
    e2 = e1 + lengths[1]
    e3 = e2 + lengths[2]
    info = jnp.stack([place % 2, (place // 2) * chip, e1, e2, e3]).astype(jnp.int32)

    u_own = jnp.concatenate(
        [decay_up, decay_bias[None, :], jnp.zeros((15, decay_up.shape[1]), bf16)], axis=0
    )
    kvu_own = jnp.concatenate(
        [
            jnp.concatenate([key_proj, value_proj], axis=1),
            jnp.pad(u_own, ((0, 0), (0, HV))),
        ],
        axis=0,
    )
    kvu = across(kvu_own, 2)
    inputs = after(block_input, kvu_own).astype(f32)
    scale_one = lax.rsqrt(jnp.mean(inputs * inputs, axis=-1, keepdims=True) + epsilon)
    unit_one = inputs * scale_one
    gain_one = mixer_gain.astype(f32)
    n_own = (unit_one * gain_one).astype(bf16)
    n_sib = across(n_own, 1)
    qo = across(after(jnp.concatenate([query_proj, outgate_proj], axis=1), n_own), 2)
    out_par = across(after(output_proj, n_own), 2)
    down_t = decay_down.T

    group = group_gain.astype(f32)[None, :]
    key, value, raw, csum, state = mixer_call(
        project_kernel, info,
        [(n_own, "own"), (n_sib, "sib"), (key_proj, "vmem"), (value_proj, "vmem"), (u_own, "vmem"),
         (kvu, "vmem"), (down_t, "vmem")],
        [(sds((chip, 2 * HK), bf16), "seq"), (sds((chip, 2 * HV), bf16), "seq"),
         (sds((chip, 2 * HK), f32), "seq"), (sds((chip, 2 * HK), f32), "seq"),
         (sds((2, HV, HK), bf16), "all")],
        [pltpu.VMEM((2, HV, HK), f32)], "project", 10, 24,
    )
    entering = forth(state)
    g_all = lax.all_gather(after(cotangent, qo, state), "narrow", axis=0, tiled=True)
    query, gate_out, mixed, merged, states = mixer_call(
        forward_kernel, info,
        [(n_own, "own"), (n_sib, "sib"), (query_proj, "vmem"), (outgate_proj, "vmem"), (qo, "vmem"), (group, "vmem"), (key, "seq"), (value, "seq"), (csum, "seq"), (entering, "vmem")],
        [(sds((chip, 2 * HK), bf16), "seq"), (sds((chip, 2 * HV), f32), "seq"),
         (sds((chip, 2 * HV), f32), "seq"), (sds((chip, 2 * HV), bf16), "phy"),
         (sds((4, 2, NB, HV, HK), bf16), "blk")],
        [pltpu.VMEM((2, HV, HK), f32)], "mixer_forward", 11, 32,
    )
    out_w = jnp.concatenate([output_proj, out_par], axis=0)
    att_sib = across(nn(merged[rows:], out_w).astype(bf16), 1)
    resid = inputs + nn(merged[:rows], out_w) + att_sib.astype(f32)
    scale_two = lax.rsqrt(jnp.mean(resid * resid, axis=-1, keepdims=True) + epsilon)
    unit_two = resid * scale_two
    gain_two = ffn_gain.astype(f32)
    m_own = (unit_two * gain_two).astype(bf16)
    m_sib = across(m_own, 1)
    m_x0 = across(m_own[: rows // 2], 2)
    m_x1 = across(m_own[rows // 2 :], 2)
    gate_t, up_t = gate_proj.T, up_proj.T
    spot = place.astype(jnp.int32)[None]
    near = ffn_call(spot, m_own, m_sib, g_all, gate_t, up_t, down_proj, "ffn_near", 0)
    m_s0 = across(after(m_x0, near[0]), 1)
    m_s1 = across(after(m_x1, near[0]), 1)
    far0 = ffn_call(
        spot, m_x0, m_s0, g_all, gate_t, up_t, down_proj, "ffn_far", 2, 0, near[7:]
    )
    far1 = ffn_call(
        spot, after(m_x1, far0[0]), m_s1, g_all, gate_t, up_t, down_proj, "ffn_far", 2, 1, far0[7:]
    )
    near_got = across(near[6], 1)
    back_x = [far[5] + across(far[6], 1) for far in (far0, far1)]
    back_got = [across(v, 2) for v in back_x]
    parts = [after(v, back_x[1]) for v in near[:5]]
    ffn_grads = ffn_grad_call((parts, far0[:5], far1[:5]), bf16, "ffn_grads", 1)
    back_two = (
        near[5].astype(f32) + near_got.astype(f32)
        + after(jnp.concatenate(back_got, axis=0), ffn_grads[0]).astype(f32)
    )
    scaled_two = back_two * gain_two
    grad_ffn_gain = jnp.sum(back_two * unit_two, axis=0)
    resid_grad = cotangent.astype(f32) + scale_two * (
        scaled_two - unit_two * jnp.mean(scaled_two * unit_two, axis=-1, keepdims=True)
    )
    r_own = resid_grad.astype(bf16)
    r_sib = across(r_own, 1)

    bits = [1 << b for b in range(count.bit_length() - 1)]
    turned = bits[1:2] + bits[:1] + bits[2:]
    wide_ffn = lax.psum(tuple(ffn_grads[:2]), "wide")
    grad_gate = wide_ffn[0].astype(f32).T
    grad_up = wide_ffn[1].astype(f32).T
    down_keep, down_got = wide_send(ffn_grads[2], turned[0], count)

    feed_a, feed_b = far1[7:]

    mixed_grad, gate_grad, gate_grad_own, gate_grad_par, gain_grad, enter_grad = mixer_call(
        gate_back_kernel, info,
        [(r_own, "own"), (r_sib, "sib"), (output_proj, "vmem"), (out_par, "vmem"), (group, "vmem"),
         (mixed, "seq"), (gate_out, "seq"), (query, "seq"), (csum, "seq")],
        [(sds((chip, 2 * HV), bf16), "seq"), (sds((chip, 2 * HV), bf16), "seq"),
         (sds((chip, HV), bf16), "phy"), (sds((chip, HV), bf16), "phy"),
         (sds((1, HV), f32), "all"), (sds((2, HV, HK), bf16), "all")],
        [pltpu.VMEM((2, HV, HK), f32), pltpu.VMEM((1, 2 * HK), f32)], "gate_backward", 1, 32,
    )
    leaving = back_to(enter_grad)
    n_cat = jnp.concatenate([n_own, n_sib], axis=0)
    r_cat = after(jnp.concatenate([r_own, r_sib], axis=0), enter_grad)
    out_grad = tn(merged, r_cat)
    early = jnp.concatenate([out_grad[HV:], tn(gate_grad_par, n_cat)], axis=0).astype(bf16)
    early_got = across(early, 2)
    k_par, v_par, u_par = kvu[:width, :HK], kvu[:width, HK:], kvu[width:, :HK]
    q_par, o_par = qo[:, :HK], qo[:, HK:]

    def backward(h, q_w, o_w, k_w, v_w, u_w, given, name):
        outs = [(sds((chip, 2 * HK + HV), bf16), "phy"), (sds((16, HK), f32), "all"),
                (sds((1, HK), f32), "all"), (sds((16, width), f32), "all")]
        if given:
            outs += [(sds((rows, width), bf16), "own"), (sds((rows, width), bf16), "sib")]
        else:
            outs += [(sds((chip, width), f32), "seq")]
        return mixer_call(
            backward_kernel, info,
            [(n_own, "own"), (n_sib, "sib"), (q_w, "vmem"), (o_w, "vmem"), (k_w, "vmem"),
             (v_w, "vmem"), (u_w, "vmem"), (down_t, "vmem"), (query, ("col", h, HK)),
             (key, ("col", h, HK)), (value, ("col", h, HV)), (csum, ("col", h, HK)),
             (raw, ("col", h, HK)), (mixed_grad, ("col", h, HV)), (gate_grad, ("col", h, HV)),
             (states, ("head", h)), (leaving, ("one", h))] + [(a, "seq") for a in given],
            outs, [pltpu.VMEM((HV, HK), f32)], name, 1, 32, reverse=True,
        )

    grad_down = wide_add(down_keep, down_got, enter_grad)
    leaving, grad_down = lax.optimization_barrier((leaving, grad_down))
    down_keep, down_got = wide_send(grad_down, turned[1], count)
    kvq_grad_par, up_par_grad, bias_par_grad, down_par_grad, back_part = backward(
        1, q_par, o_par, k_par, v_par, u_par, (), "mixer_backward_par"
    )
    kvq_par = tn(kvq_grad_par, n_cat).astype(bf16)
    kvq_got = across(kvq_par, 2)
    feed_got = across(after(feed_b, back_part), 1)
    feed_far = across(feed_a[rows:] + feed_got[rows:], 2)
    feed = feed_a[:rows].astype(f32) + feed_got[:rows].astype(f32) + feed_far.astype(f32)
    block_output = (resid + feed).astype(bf16)
    grad_down = wide_add(down_keep, down_got, back_part)
    early_sum = jnp.concatenate(
        [out_grad[:HV] + after(early_got, back_part)[:HV].astype(f32),
         tn(gate_grad_own, n_cat) + after(early_got, back_part)[HV:].astype(f32)], axis=0
    ).astype(bf16)
    back_part, kvq_par, grad_down, early_sum = lax.optimization_barrier(
        (back_part, kvq_par, grad_down, early_sum)
    )
    down_keep, down_got = wide_send(grad_down, turned[2], count)
    early_keep, early_kept = wide_send(early_sum, turned[0], count)
    kvq_grad_own, up_own_grad, bias_own_grad, down_own_grad, back_own, back_s = backward(
        0, query_proj, outgate_proj, key_proj, value_proj, u_own, (back_part,), "mixer_backward_own"
    )
    back_one = back_own.astype(f32) + across(back_s, 1).astype(f32)
    scaled_one = back_one * gain_one
    grad_mixer_gain = jnp.sum(back_one * unit_one, axis=0)
    input_grad = (
        resid_grad
        + scale_one
        * (scaled_one - unit_one * jnp.mean(scaled_one * unit_one, axis=-1, keepdims=True))
    ).astype(bf16)

    kvq_sum = (tn(kvq_grad_own, n_cat) + kvq_got.astype(f32)).astype(bf16)
    decay_own = jnp.concatenate([up_own_grad, bias_own_grad], axis=0)
    decay_par = jnp.concatenate([up_par_grad, bias_par_grad], axis=0)
    small = jnp.concatenate(
        [down_own_grad + down_par_grad, grad_mixer_gain[None], grad_ffn_gain[None],
         jnp.pad(gain_grad, ((0, 0), (0, width - HV)))], axis=0
    )
    small = small + across(small, 1)

    def wide_rows(v):
        return jnp.pad(v, ((0, 0), (0, width - HK)))

    got = across(jnp.concatenate([small, wide_rows(decay_par)], axis=0), 2)
    few = got + jnp.concatenate([small, wide_rows(decay_own)], axis=0)
    few = jnp.pad(few, ((0, 28), (0, 0))).astype(bf16)
    early_sum = wide_add(early_keep, early_kept, back_s)
    second = wide_end(early_sum, 1, turned, count).astype(f32)
    first = wide_sum(jnp.concatenate([kvq_sum, few], axis=0), bits, count).astype(f32)
    grad_down = wide_add(down_keep, down_got, back_s)
    grad_down = wide_end(grad_down, 3, turned, count).astype(f32)
    kvq, few = first[: 2 * HK + HV], first[2 * HK + HV :]
    return (
        block_output,
        input_grad,
        few[16],
        kvq[HK + HV :].T,
        kvq[:HK].T,
        kvq[HK : HK + HV].T,
        second[HV:].T,
        few[:16].T,
        few[19:35, :HK],
        few[35, :HK],
        few[18, :HV],
        second[:HV],
        few[17],
        grad_gate,
        grad_up,
        grad_down,
    )


def solution(mesh):
    placed = (
        P(("wide", "narrow"), None),
        P("wide", None),
        P(),
        P(None, "narrow"),
        P(None, "narrow"),
        P(None, "narrow"),
        P(None, "narrow"),
        P(),
        P(None, "narrow"),
        P("narrow"),
        P(),
        P("narrow", None),
        P(),
        P(None, "narrow"),
        P(None, "narrow"),
        P("narrow", None),
        P(("wide", "narrow"), None),
    )
    return jax.shard_map(
        functools.partial(body, mesh.shape["wide"]),
        mesh=mesh,
        in_specs=placed,
        out_specs=(
            P(("wide", "narrow"), None),
            P(("wide", "narrow"), None),
            P(),
            P(None, "narrow"),
            P(None, "narrow"),
            P(None, "narrow"),
            P(None, "narrow"),
            P(),
            P(None, "narrow"),
            P("narrow"),
            P(),
            P("narrow", None),
            P(),
            P(None, "narrow"),
            P(None, "narrow"),
            P("narrow", None),
        ),
        check_vma=False,
    )
```

```python
import functools

import jax
import jax.numpy as jnp
from jax import lax
from jax.experimental import pallas as pl
from jax.experimental.pallas import tpu as pltpu
from jax.sharding import PartitionSpec as P

HK = 128
HV = 256
SPAN = 64
ROWS = 256
NB = ROWS // SPAN

epsilon = 1e-06
group_floor = 0.25
highest = lax.Precision.HIGHEST
f32 = jnp.float32
bf16 = jnp.bfloat16
scale_q = HK ** (-0.5)


def nn(a, b, precision=None):
    return lax.dot_general(
        a, b, (((1,), (0,)), ((), ())), precision=precision, preferred_element_type=f32
    )


def nt(a, b, precision=None):
    return lax.dot_general(
        a, b, (((1,), (1,)), ((), ())), precision=precision, preferred_element_type=f32
    )


def tn(a, b, precision=None):
    return lax.dot_general(
        a, b, (((0,), (0,)), ((), ())), precision=precision, preferred_element_type=f32
    )


def sigmoid(v):
    return 1.0 / (1.0 + jnp.exp(-v))


def rows_cols():
    i = lax.broadcasted_iota(jnp.int32, (ROWS, ROWS), 0)
    j = lax.broadcasted_iota(jnp.int32, (ROWS, ROWS), 1)
    return i, j


def block_low():
    i, j = rows_cols()
    return (i >= j) & (i // SPAN == j // SPAN)


def doc_start(info, pos):
    e1, e2, e3 = info[2], info[3], info[4]
    start = jnp.where(pos >= e1, e1, 0)
    start = jnp.where(pos >= e2, e2, start)
    return jnp.where(pos >= e3, e3, start)


def scalar_start(info, pos):
    e1, e2, e3 = info[2], info[3], info[4]
    start = jnp.where(pos >= e1, e1, 0)
    start = jnp.where(pos >= e2, e2, start)
    return jnp.where(pos >= e3, e3, start)


def spread(v, row):
    return jnp.concatenate(
        [
            jnp.broadcast_to(v[b * SPAN + row : b * SPAN + row + 1], (SPAN, v.shape[1]))
            for b in range(NB)
        ],
        axis=0,
    )


def pick(info, s, own, sib):
    use_own = (s // 2) == info[0]
    return jnp.where(use_own, own[...], sib[...])


def both(own, par):
    return jnp.concatenate([own[...], par[...]], axis=1)


def project_kernel(
    info, own, sib, k_own, v_own, u_own, kvu, down, key, value, raw, csum, state, acc
):
    s = pl.program_id(0)
    x = pick(info, s, own, sib)
    width = x.shape[1]
    k_par, v_par, u_par = kvu.at[:width, :HK], kvu.at[:width, HK:], kvu.at[width:, :HK]
    ko = nn(x, both(k_own, k_par))
    k = ko.astype(bf16)
    key[...] = k
    v0 = nn(x, v_own[...]).astype(bf16)
    v1 = nn(x, v_par[...]).astype(bf16)
    value[:, :HV] = v0
    value[:, HV:] = v1
    low = nt(x, down[...])
    up = both(u_own, u_par).astype(f32)
    raws = nn(low, up[:16], highest) + up[16:17]
    raw[...] = raws
    decay = (jnp.minimum(raws, 0.0) - jnp.log1p(jnp.exp(-jnp.abs(raws)))) * (1.0 / 16.0)
    i, j = rows_cols()
    csum[...] = nn(block_low().astype(f32), decay, highest)
    rest = nn((j > i).astype(f32), decay, highest)
    total = rest[0:1] + decay[0:1]
    base = info[1] + s * ROWS
    last = scalar_start(info, base + ROWS - 1)
    pos = base + lax.broadcasted_iota(jnp.int32, (ROWS, 1), 0)
    tail = jnp.where(pos >= last, 1.0, 0.0)
    alive = jnp.where((last < base) & (s > 0), 1.0, 0.0)
    ks = (k.astype(f32) * jnp.exp(rest) * tail).astype(bf16)
    keep = jnp.exp(total) * alive

    @pl.when(s == 0)
    def _():
        acc[...] = jnp.zeros_like(acc)

    for h, v in enumerate((v0, v1)):
        hs = slice(h * HK, (h + 1) * HK)
        acc[h] = acc[h] * keep[:, hs] + tn(v, ks[:, hs])

    @pl.when(s == 3)
    def _():
        state[0] = acc[1].astype(bf16)
        state[1] = acc[0].astype(bf16)


def factors(info, s, cs):
    base = info[1] + s * ROWS
    row = lax.broadcasted_iota(jnp.int32, (ROWS, 1), 0)
    pos = base + row
    start = doc_start(info, pos)
    living = jnp.where(start < base + (row // SPAN) * SPAN, 1.0, 0.0)
    final = doc_start(info, base + (row // SPAN) * SPAN + SPAN - 1)
    tail = jnp.where(pos >= final, 1.0, 0.0)
    alive = []
    for b in range(NB):
        first = base + b * SPAN
        alive.append(jnp.where(scalar_start(info, first + SPAN - 1) < first, 1.0, 0.0))
    i, j = rows_cols()
    mask = block_low() & (base + j >= start)
    return living, tail, alive, mask


def forward_kernel(
    info, own, sib, q_own, o_own, qo, gain, key, value, csum, entering,
    query, gate_out, mixed, merged, states, acc,
):
    s = pl.program_id(0)
    x = pick(info, s, own, sib)
    q_par, o_par = qo.at[:, :HK], qo.at[:, HK : HK + HV]
    q = nn(x, both(q_own, q_par)).astype(bf16)
    query[...] = q
    living, tail, alive, mask = factors(info, s, None)

    @pl.when(s == 0)
    def _():
        acc[...] = entering[...].astype(f32)

    for h in range(2):
        w = o_own if h == 0 else o_par
        hs, vs = slice(h * HK, (h + 1) * HK), slice(h * HV, (h + 1) * HV)
        go = nn(x, w[...])
        gate_out[:, vs] = go
        cs = csum[:, hs]
        centre, last = spread(cs, SPAN // 2), spread(cs, SPAN - 1)
        qt = q[:, hs].astype(f32) * scale_q
        k = key[:, hs].astype(f32)
        v = value[:, vs]
        qe = (qt * jnp.exp(cs - centre)).astype(bf16)
        ke = (k * jnp.exp(centre - cs)).astype(bf16)
        qc = (qt * jnp.exp(cs) * living).astype(bf16)
        kt = (k * jnp.exp(last - cs) * tail).astype(bf16)
        scores = jnp.where(mask, nt(qe, ke), 0.0).astype(bf16)
        inside = nn(scores, v)
        st = acc[h]
        carried = []
        for b in range(NB):
            r = slice(b * SPAN, (b + 1) * SPAN)
            stb = st.astype(bf16)
            states[0, h, b] = stb
            carried.append(nt(qc[r], stb))
            f = jnp.exp(cs[(b + 1) * SPAN - 1 : (b + 1) * SPAN]) * alive[b]
            st = st * f + tn(v[r], kt[r])
        acc[h] = st
        mix = inside + jnp.concatenate(carried, axis=0)
        mixed[:, vs] = mix
        inv = lax.rsqrt(jnp.mean(mix * mix, axis=-1, keepdims=True) + group_floor)
        mer = (mix * inv * gain[...] * (go * sigmoid(go))).astype(bf16)
        merged[:, vs] = mer


def gate_back_kernel(
    info, own, sib, out_own, out_par, gain, mixed, gate_out, query, csum,
    mixed_grad, gate_grad, gate_own, gate_par, gain_grad, enter_grad, acc, carry,
):
    s = pl.program_id(0)
    g = pick(info, s, own, sib)

    @pl.when(s == 0)
    def _():
        acc[...] = jnp.zeros_like(acc)
        carry[...] = jnp.zeros_like(carry)
        gain_grad[...] = jnp.zeros_like(gain_grad)

    base = info[1] + s * ROWS
    pos = base + lax.broadcasted_iota(jnp.int32, (ROWS, 1), 0)
    living = jnp.where(doc_start(info, pos) < info[1], 1.0, 0.0)
    for h in range(2):
        wo = out_own if h == 0 else out_par
        hs, vs = slice(h * HK, (h + 1) * HK), slice(h * HV, (h + 1) * HV)
        mg = nt(g, wo[...]).astype(bf16).astype(f32)
        mix = mixed[:, vs]
        go = gate_out[:, vs]
        gn = gain[...]
        inv = lax.rsqrt(jnp.mean(mix * mix, axis=-1, keepdims=True) + group_floor)
        n = mix * inv
        sg = sigmoid(go)
        silu = go * sg
        ng = mg * n
        dgo = (ng * gn * (sg + silu * (1.0 - sg))).astype(bf16)
        gate_grad[:, vs] = dgo
        (gate_own if h == 0 else gate_par)[...] = dgo
        gain_grad[...] += jnp.sum(ng * silu, axis=0, keepdims=True)
        dn = mg * gn * silu
        do = (inv * (dn - n * jnp.mean(dn * n, axis=-1, keepdims=True))).astype(bf16)
        mixed_grad[:, vs] = do
        cs = csum[:, hs]
        offset = carry[:, hs]
        parts = []
        for b in range(NB):
            parts.append(cs[b * SPAN : (b + 1) * SPAN] + offset)
            offset = offset + cs[(b + 1) * SPAN - 1 : (b + 1) * SPAN]
        carry[:, hs] = offset
        qcc = query[:, hs].astype(f32) * scale_q * jnp.exp(jnp.concatenate(parts, axis=0)) * living
        acc[h] += tn(do, qcc.astype(bf16))

    @pl.when(s == 3)
    def _():
        enter_grad[0] = acc[1].astype(bf16)
        enter_grad[1] = acc[0].astype(bf16)


def backward_kernel(
    info, own, sib, *rest,
):
    width = own.shape[1]
    if len(rest) == 18:
        kvu, qo, *rest = rest
        q_w, o_w = qo.at[:, :HK], qo.at[:, HK : HK + HV]
        k_w, v_w, u_w = kvu.at[:width, :HK], kvu.at[:width, HK:], kvu.at[width:, :HK]
    else:
        q_w, o_w, k_w, v_w, u_w, *rest = rest
    down, query, key, value, csum, raw, mixed_grad, gate_grad, states, leaving, *rest = rest
    given, rest = (rest[:1], rest[1:]) if len(rest) == 8 else ((), rest)
    kvq_grad, up_grad, bias_grad, down_grad, *outs, acc = rest
    step = pl.program_id(0)
    s = 3 - step
    x = pick(info, s, own, sib)

    @pl.when(step == 0)
    def _():
        acc[...] = leaving[0].astype(f32)
        up_grad[...] = jnp.zeros_like(up_grad)
        bias_grad[...] = jnp.zeros_like(bias_grad)
        down_grad[...] = jnp.zeros_like(down_grad)

    living, tail, alive, mask = factors(info, s, None)
    lower = block_low().astype(f32)
    cs = csum[...]
    centre, last = spread(cs, SPAN // 2), spread(cs, SPAN - 1)
    qt = query[...].astype(f32) * scale_q
    k = key[...].astype(f32)
    v = value[...]
    do = mixed_grad[...]
    eq, ek = jnp.exp(cs - centre), jnp.exp(centre - cs)
    ec, et = jnp.exp(cs) * living, jnp.exp(last - cs) * tail
    qe, ke = (qt * eq).astype(bf16), (k * ek).astype(bf16)
    qcf, ktf = qt * ec, k * et
    qc, kt = qcf.astype(bf16), ktf.astype(bf16)
    scores = jnp.where(mask, nt(qe, ke), 0.0).astype(bf16)
    ds = jnp.where(mask, nt(do, v), 0.0).astype(bf16)
    dqe = nn(ds, ke)
    dke = tn(ds, qe)
    dv = tn(scores, do)
    gt = acc[...]
    dqc, dkt, dvt, dlast = [None] * NB, [None] * NB, [None] * NB, [None] * NB
    for b in reversed(range(NB)):
        r = slice(b * SPAN, (b + 1) * SPAN)
        gtb = gt.astype(bf16)
        st = states[0, 0, b]
        dvt[b] = nt(kt[r], gtb)
        dkt[b] = nn(v[r], gtb)
        dqc[b] = nn(do[r], st)
        f = jnp.exp(cs[(b + 1) * SPAN - 1 : (b + 1) * SPAN]) * alive[b]
        moved = f * jnp.sum(st.astype(f32) * gt, axis=0, keepdims=True)
        tails = jnp.sum(ktf[r] * dkt[b], axis=0, keepdims=True)
        dlast[b] = jnp.broadcast_to(moved + tails, (SPAN, HK))
        gt = gt * f + tn(do[r], qc[r])
    acc[...] = gt
    dqc = jnp.concatenate(dqc, axis=0)
    dkt = jnp.concatenate(dkt, axis=0)
    dv = (dv + jnp.concatenate(dvt, axis=0)).astype(bf16)
    dq = ((dqe * eq + dqc * ec) * scale_q).astype(bf16)
    dk = (dke * ek + dkt * et).astype(bf16)
    dc = qe.astype(f32) * dqe - ke.astype(f32) * dke + qcf * dqc - ktf * dkt
    ddecay = tn(lower, dc, highest) + jnp.concatenate(dlast, axis=0)
    raw_grad = ddecay * sigmoid(-raw[...]) * (1.0 / 16.0)
    kvq_grad[:, :HK] = dk
    kvq_grad[:, HK : HK + HV] = dv
    kvq_grad[:, HK + HV :] = dq
    up = u_w[:16].astype(f32)
    rank_low = nt(raw_grad, up, highest).astype(bf16)
    low = nt(x, down[...])
    up_grad[...] += tn(low, raw_grad, highest)
    bias_grad[...] += jnp.sum(raw_grad, axis=0, keepdims=True)
    down_grad[...] += tn(rank_low, x)
    back = nt(dv, v_w[...]) + nt(gate_grad[...], o_w[...]) + nn(rank_low, down[...])
    back = back + nt(
        jnp.concatenate([dq, dk], axis=1), jnp.concatenate([q_w[...], k_w[...]], axis=1)
    )
    if not given:
        outs[0][...] = back
        return
    back = back + given[0][...]
    use_own = (s // 2) == info[0]

    @pl.when(use_own)
    def _():
        outs[0][...] = back.astype(bf16)

    @pl.when(jnp.logical_not(use_own))
    def _():
        outs[1][...] = back.astype(bf16)


def ffn_kernel(
    place, n_a, n_b, g_a, g_b, gate_w, up_w, down_w, *rest,
):
    hidden, gate_grad, up_grad, n_cat, g_cat, back_a, back_b, feed_a, feed_b = rest[-9:]
    i = pl.program_id(0)
    first = i < pl.num_programs(0) // 2
    n = jnp.where(first, n_a[...], n_b[...])
    g = jnp.where(first, g_a[...], g_b[...])
    n_cat[...] = n
    g_cat[...] = g
    gate = nt(n, gate_w[...])
    up = nt(n, up_w[...])
    gh = nt(g, down_w[...]).astype(bf16).astype(f32)
    sg = sigmoid(gate)
    silu = gate * sg
    hid = (silu * up).astype(bf16)
    gg = (gh * up * (sg + silu * (1.0 - sg))).astype(bf16)
    ug = (gh * silu).astype(bf16)
    hidden[...] = hid
    gate_grad[...] = gg
    up_grad[...] = ug
    feed = nn(hid, down_w[...]).astype(bf16)
    back = (nn(gg, gate_w[...]) + nn(ug, up_w[...])).astype(bf16)

    @pl.when(first)
    def _():
        feed_a[...] = feed
        back_a[...] = back

    @pl.when(jnp.logical_not(first))
    def _():
        feed_b[...] = feed
        back_b[...] = back


def ffn_grad_kernel(*refs):
    out, acc = refs[-2:]
    units = refs[0].shape[1]
    i = pl.program_id(0)

    @pl.when(i == 0)
    def _():
        acc[...] = jnp.zeros_like(acc)

    def add(h, gg, ug, n, g):
        for k, (left, right) in enumerate(((gg, n), (ug, n), (h, g))):
            acc[k * units : (k + 1) * units] += tn(left[...], right[...])

    pl.when(i < 2)(lambda: add(*refs[:5]))
    pl.when(i == 2)(lambda: add(*refs[5:10]))
    pl.when(i == 3)(lambda: add(*refs[10:15]))

    @pl.when(i == 3)
    def _():
        out[...] = acc[...].astype(out.dtype)


def ffn_grad_call(groups, dtype, name, us):
    step, units = groups[1][0].shape
    width = groups[1][3].shape[1]
    out = jax.ShapeDtypeStruct((3 * units, width), dtype)
    specs = []
    for k, group in enumerate(groups):
        for a in group:
            index = (lambda i: (jnp.minimum(i, 1), 0)) if k == 0 else (lambda i: (0, 0))
            specs.append(pl.BlockSpec((step, a.shape[1]), index))
    return pl.pallas_call(
        ffn_grad_kernel,
        out_shape=out_hbm(out),
        grid=(4,),
        in_specs=specs,
        out_specs=whole(out),
        scratch_shapes=[pltpu.VMEM((3 * units, width), f32)],
        compiler_params=params(44),
        cost_estimate=cost(us),
        name=name,
    )(*[in_hbm(a) for group in groups for a in group])


def resid_back_kernel(info, own, sib, got0, got1, resid, g, gain, resid_grad, low, gain_grad):
    i = pl.program_id(0)
    got = jnp.where(i == 0, got0[...], got1[...])
    back = own[...].astype(f32) + sib[...].astype(f32) + got.astype(f32)
    res = resid[...]
    scale = lax.rsqrt(jnp.mean(res * res, axis=-1, keepdims=True) + epsilon)
    unit = res * scale
    scaled = back * gain[...]
    grad = g[...].astype(f32) + scale * (
        scaled - unit * jnp.mean(scaled * unit, axis=-1, keepdims=True)
    )
    resid_grad[...] = grad
    low[...] = grad.astype(bf16)
    part = jnp.sum(back * unit, axis=0, keepdims=True)

    @pl.when(i == 0)
    def _():
        gain_grad[...] = part

    @pl.when(i > 0)
    def _():
        gain_grad[...] += part


def input_back_kernel(info, own, sib, x, resid_grad, gain, input_grad, gain_grad):
    i = pl.program_id(0)
    back = own[...].astype(f32) + sib[...].astype(f32)
    values = x[...].astype(f32)
    scale = lax.rsqrt(jnp.mean(values * values, axis=-1, keepdims=True) + epsilon)
    unit = values * scale
    scaled = back * gain[...]
    grad = resid_grad[...] + scale * (
        scaled - unit * jnp.mean(scaled * unit, axis=-1, keepdims=True)
    )
    input_grad[...] = grad.astype(bf16)
    part = jnp.sum(back * unit, axis=0, keepdims=True)

    @pl.when(i == 0)
    def _():
        gain_grad[...] = part

    @pl.when(i > 0)
    def _():
        gain_grad[...] += part


def params(mib):
    return pltpu.CompilerParams(
        dimension_semantics=("arbitrary",), vmem_limit_bytes=mib * 1024 * 1024
    )


def cost(us):
    return pl.CostEstimate(flops=us * 1_000_000_000, transcendentals=0, bytes_accessed=us * 1_000_000)


def in_hbm(a):
    return pltpu.with_memory_space_constraint(a, pltpu.HBM)


def out_hbm(a):
    return pltpu.HBM(a.shape, a.dtype)


def whole(a):
    zero = (0,) * a.ndim
    return pl.BlockSpec(a.shape, lambda *_: zero)


def resident():
    return pl.BlockSpec(memory_space=pltpu.VMEM)


def own_index(s, info):
    return jnp.where(info[0] == 0, jnp.minimum(s, 1), jnp.maximum(s - 2, 0))


def sib_index(s, info):
    return jnp.where(info[0] == 0, jnp.maximum(s - 2, 0), jnp.minimum(s, 1))


def phys_index(s, info):
    return jnp.where(info[0] == 0, s, (s + 2) % 4)


def mixer_call(kernel, info, ins, outs, scratch, name, us, mib, reverse=False, steps=4):
    def at(s):
        return 3 - s if reverse else s

    def spec(a, kind):
        if isinstance(kind, tuple) and kind[0] == "col":
            cols = kind[2]
            return pl.BlockSpec((ROWS, cols), lambda s, info: (at(s), kind[1]))
        if isinstance(kind, tuple) and kind[0] == "head":
            return pl.BlockSpec((1, 1, *a.shape[2:]), lambda s, info: (at(s), kind[1], 0, 0, 0))
        if isinstance(kind, tuple) and kind[0] == "one":
            return pl.BlockSpec((1, *a.shape[1:]), lambda s, info: (kind[1], 0, 0))
        if kind == "own":
            return pl.BlockSpec((ROWS, a.shape[1]), lambda s, info: (own_index(at(s), info), 0))
        if kind == "sib":
            return pl.BlockSpec((ROWS, a.shape[1]), lambda s, info: (sib_index(at(s), info), 0))
        if kind == "seq":
            return pl.BlockSpec((ROWS, a.shape[1]), lambda s, info: (at(s), 0))
        if kind == "phy":
            return pl.BlockSpec((ROWS, a.shape[1]), lambda s, info: (phys_index(at(s), info), 0))
        if kind == "blk":
            zero = (0,) * (a.ndim - 1)
            return pl.BlockSpec((1, *a.shape[1:]), lambda s, info: (at(s), *zero))
        return whole(a)

    return pl.pallas_call(
        kernel,
        out_shape=[out_hbm(a) for a, _ in outs],
        grid_spec=pltpu.PrefetchScalarGridSpec(
            num_scalar_prefetch=1,
            grid=(steps,),
            in_specs=[spec(a, kind) for a, kind in ins],
            out_specs=[spec(a, kind) for a, kind in outs],
            scratch_shapes=scratch,
        ),
        compiler_params=params(mib),
        cost_estimate=cost(us),
        name=name,
    )(info, *[in_hbm(a) for a, _ in ins])


def ffn_call(place, n_a, n_b, g_a, g_b, gate_w, up_w, down_w, name, flip, part=0, feeds=()):
    rows, width = n_a.shape
    units = gate_w.shape[0]
    steps = 2 * rows // ROWS
    half = steps // 2
    per = 2

    def g_low(i, place):
        here = (place[0] ^ flip) * per + part if flip else 0
        return here + jnp.minimum(i, half - 1), 0

    def g_high(i, place):
        here = (place[0] ^ (flip + 1)) * per + part if flip else 0
        return here + jnp.maximum(i - half, 0), 0

    lo = pl.BlockSpec((ROWS, width), lambda i, place: (jnp.minimum(i, half - 1), 0))
    hi = pl.BlockSpec((ROWS, width), lambda i, place: (jnp.maximum(i - half, 0), 0))
    at = part + (flip // 2) * per
    feed_lo = pl.BlockSpec((ROWS, width), lambda i, place: (jnp.minimum(i, half - 1) + at, 0))
    feed_hi = pl.BlockSpec((ROWS, width), lambda i, place: (jnp.maximum(i - half, 0) + at, 0))
    hbm = pl.BlockSpec(memory_space=pl.ANY)
    cat = pl.BlockSpec((ROWS, width), lambda i, place: (i, 0))
    mid = pl.BlockSpec((ROWS, units), lambda i, place: (i, 0))
    sds = jax.ShapeDtypeStruct
    return pl.pallas_call(
        ffn_kernel,
        out_shape=[out_hbm(sds((2 * rows, units), bf16))] * 3
        + [out_hbm(sds((2 * rows, width), bf16))] * 2
        + [out_hbm(sds((rows, width), bf16))] * 2
        + [out_hbm(sds((2 * per * ROWS, width), bf16))] * 2,
        grid_spec=pltpu.PrefetchScalarGridSpec(
            num_scalar_prefetch=1,
            grid=(steps,),
            in_specs=[lo, hi, pl.BlockSpec((ROWS, width), g_low), pl.BlockSpec((ROWS, width), g_high), whole(gate_w), whole(up_w), whole(down_w)]
            + [hbm] * len(feeds),
            out_specs=[mid, mid, mid, cat, cat, lo, hi, feed_lo, feed_hi],
        ),
        input_output_aliases={8 + k: 7 + k for k in range(len(feeds))},
        compiler_params=params(32),
        cost_estimate=cost(3 * steps + 2),
        name=name,
    )(place, *[in_hbm(a) for a in (n_a, n_b, g_a, g_b, gate_w, up_w, down_w, *feeds)])


def across(v, bit):
    return lax.ppermute(v, "narrow", [(i, i ^ bit) for i in range(4)])


def forth(v):
    return lax.ppermute(v, "narrow", [(0, 2), (1, 3)])


def back_to(v):
    return lax.ppermute(v, "narrow", [(2, 0), (3, 1)])


def after(v, *others):
    return lax.optimization_barrier((v, *others))[0]


def pairs(count, bit):
    return [(i, i ^ bit) for i in range(count)]


def wide_send(v, bit, count):
    half = v.shape[0] // 2
    high = (lax.axis_index("wide") // bit) % 2
    keep = lax.dynamic_slice_in_dim(v, high * half, half, 0)
    send = lax.dynamic_slice_in_dim(v, (1 - high) * half, half, 0)
    return keep, lax.ppermute(send, "wide", pairs(count, bit))


def wide_add(keep, got, *earlier):
    got = after(got, *earlier) if earlier else got
    return (keep.astype(f32) + got.astype(f32)).astype(bf16)


class Exchange:
    def __init__(self, arrays, orders, count):
        self.arrays, self.orders, self.count, self.step = arrays, orders, count, 0

    def begin(self, keeps, sends):
        self.sent = [
            (keep, lax.ppermute(send, "wide", pairs(self.count, order[0])))
            for keep, send, order in zip(keeps, sends, self.orders)
        ]

    def send(self):
        n = len(self.orders[0])
        self.sent = []
        for v, order in zip(self.arrays, self.orders):
            if self.step < n:
                self.sent.append(wide_send(v, order[self.step], self.count))
            else:
                got = lax.ppermute(v, "wide", pairs(self.count, order[2 * n - 1 - self.step]))
                self.sent.append((v, got))

    def take(self, *earlier):
        n = len(self.orders[0])
        arrays = []
        for (keep, got), order in zip(self.sent, self.orders):
            if self.step < n:
                arrays.append(wide_add(keep, got, *earlier))
            else:
                got = after(got, *earlier) if earlier else got
                high = (lax.axis_index("wide") // order[2 * n - 1 - self.step]) % 2
                arrays.append(
                    jnp.where(
                        high == 0,
                        jnp.concatenate([keep, got], 0),
                        jnp.concatenate([got, keep], 0),
                    )
                )
        self.arrays = arrays
        self.step += 1

    def tie(self, v):
        v, *self.arrays = lax.optimization_barrier((v, *self.arrays))
        return v

    def finish(self, fresh=False):
        if not fresh:
            self.take()
        while self.step < 2 * len(self.orders[0]):
            self.send()
            self.take()
        return self.arrays


def wide_pieces(v, count):
    return lax.all_to_all(
        v.reshape(count, v.shape[0] // count, v.shape[1]), "wide", 0, 0, tiled=True
    )


def added(pieces):
    return jnp.sum(pieces.astype(f32), axis=0).astype(bf16)


def wide_copies(v, count):
    spread_out = jnp.broadcast_to(v[None], (count, *v.shape))
    got = lax.all_to_all(spread_out, "wide", 0, 0, tiled=True)
    return got.reshape(count * v.shape[0], v.shape[1])


def body(
    count, block_input, doc_lengths, mixer_gain, query_proj, key_proj, value_proj, outgate_proj,
    decay_down, decay_up, decay_bias, group_gain, output_proj, ffn_gain, gate_proj, up_proj,
    down_proj, cotangent,
):
    sds = jax.ShapeDtypeStruct
    rows, width = block_input.shape
    chip = 2 * rows
    place = lax.axis_index("narrow")
    lengths = doc_lengths[0]
    e1 = lengths[0]
    e2 = e1 + lengths[1]
    e3 = e2 + lengths[2]
    info = jnp.stack([place % 2, (place // 2) * chip, e1, e2, e3]).astype(jnp.int32)

    u_own = jnp.concatenate(
        [decay_up, decay_bias[None, :], jnp.zeros((15, decay_up.shape[1]), bf16)], axis=0
    )
    kvu_own = jnp.concatenate(
        [
            jnp.concatenate([key_proj, value_proj], axis=1),
            jnp.pad(u_own, ((0, 0), (0, HV))),
        ],
        axis=0,
    )
    kvu = across(kvu_own, 2)
    inputs = after(block_input, kvu_own).astype(f32)
    scale_one = lax.rsqrt(jnp.mean(inputs * inputs, axis=-1, keepdims=True) + epsilon)
    unit_one = inputs * scale_one
    gain_one = mixer_gain.astype(f32)
    n_own = (unit_one * gain_one).astype(bf16)
    n_sib = across(n_own, 1)
    out_flat = output_proj.reshape(width, HV)
    qo = across(
        after(jnp.concatenate([query_proj, outgate_proj, out_flat], axis=1), n_own), 2
    )
    out_par = qo[:, HK + HV :].reshape(HV, width)
    down_t = decay_down.T

    group = group_gain.astype(f32)[None, :]
    key, value, raw, csum, state = mixer_call(
        project_kernel, info,
        [(n_own, "own"), (n_sib, "sib"), (key_proj, "vmem"), (value_proj, "vmem"), (u_own, "vmem"),
         (kvu, "vmem"), (down_t, "vmem")],
        [(sds((chip, 2 * HK), bf16), "seq"), (sds((chip, 2 * HV), bf16), "seq"),
         (sds((chip, 2 * HK), f32), "seq"), (sds((chip, 2 * HK), f32), "seq"),
         (sds((2, HV, HK), bf16), "all")],
        [pltpu.VMEM((2, HV, HK), f32)], "project", 10, 24,
    )
    entering = forth(state)
    g_sib = across(after(cotangent, state), 1)
    g_all = lax.all_gather(after(cotangent, qo, state), "narrow", axis=0, tiled=True)
    query, gate_out, mixed, merged, states = mixer_call(
        forward_kernel, info,
        [(n_own, "own"), (n_sib, "sib"), (query_proj, "vmem"), (outgate_proj, "vmem"), (qo, "vmem"), (group, "vmem"), (key, "seq"), (value, "seq"), (csum, "seq"), (entering, "vmem")],
        [(sds((chip, 2 * HK), bf16), "seq"), (sds((chip, 2 * HV), f32), "seq"),
         (sds((chip, 2 * HV), f32), "seq"), (sds((chip, 2 * HV), bf16), "phy"),
         (sds((4, 2, NB, HV, HK), bf16), "blk")],
        [pltpu.VMEM((2, HV, HK), f32)], "mixer_forward", 11, 32,
    )
    out_w = jnp.concatenate([output_proj, out_par], axis=0)
    att_sib = across(nn(merged[rows:], out_w).astype(bf16), 1)
    resid = inputs + nn(merged[:rows], out_w) + att_sib.astype(f32)
    scale_two = lax.rsqrt(jnp.mean(resid * resid, axis=-1, keepdims=True) + epsilon)
    gain_two = ffn_gain.astype(f32)[None, :]
    m_own = (resid * scale_two * gain_two).astype(bf16)
    m_0, m_1 = m_own[: rows // 2], m_own[rows // 2 :]
    m_sib = across(m_own, 1)
    m_x0 = across(m_0, 2)
    m_x1 = across(m_1, 2)
    gate_t, up_t = gate_proj.T, up_proj.T
    spot = place.astype(jnp.int32)[None]
    near = ffn_call(spot, m_own, m_sib, cotangent, g_sib, gate_t, up_t, down_proj, "ffn_near", 0)
    m_s0 = across(after(m_x0, near[0]), 1)
    far0 = ffn_call(
        spot, m_x0, m_s0, g_all, g_all, gate_t, up_t, down_proj, "ffn_far", 2, 0, near[7:]
    )
    m_s1 = across(after(m_x1, far0[0]), 1)
    far1 = ffn_call(
        spot, after(m_x1, far0[0]), m_s1, g_all, g_all, gate_t, up_t, down_proj, "ffn_far", 2, 1, far0[7:]
    )
    near_got = across(near[6], 1)
    back_x = [far[5] + across(far[6], 1) for far in (far0, far1)]
    back_got = [across(v, 2) for v in back_x]
    parts = [after(v, *back_x) for v in near[:5]]
    bits = [1 << b for b in range(count.bit_length() - 1)]
    turned = bits[1:2] + bits[:1] + bits[2:]
    ffn_grads = ffn_grad_call((parts, far0[:5], far1[:5]), bf16, "ffn_grads", 18)
    ffn_part = lax.psum_scatter(ffn_grads, "wide", scatter_dimension=0, tiled=True)
    resid_grad, r_own, grad_ffn_gain = mixer_call(
        resid_back_kernel, info,
        [(near[5], "seq"), (near_got, "seq"), (after(back_got[0], ffn_grads), "all"),
         (back_got[1], "all"), (resid, "seq"), (cotangent, "seq"), (gain_two, "all")],
        [(sds((rows, width), f32), "seq"), (sds((rows, width), bf16), "seq"),
         (sds((1, width), f32), "all")],
        [], "resid_back", 3, 24, steps=2,
    )
    r_sib = across(r_own, 1)


    mixed_grad, gate_grad, gate_grad_own, gate_grad_par, gain_grad, enter_grad = mixer_call(
        gate_back_kernel, info,
        [(r_own, "own"), (r_sib, "sib"), (output_proj, "vmem"), (out_par, "vmem"), (group, "vmem"),
         (mixed, "seq"), (gate_out, "seq"), (query, "seq"), (csum, "seq")],
        [(sds((chip, 2 * HV), bf16), "seq"), (sds((chip, 2 * HV), bf16), "seq"),
         (sds((chip, HV), bf16), "phy"), (sds((chip, HV), bf16), "phy"),
         (sds((1, HV), f32), "all"), (sds((2, HV, HK), bf16), "all")],
        [pltpu.VMEM((2, HV, HK), f32), pltpu.VMEM((1, 2 * HK), f32)], "gate_backward", 6, 32,
    )
    leaving = back_to(enter_grad)
    n_cat = jnp.concatenate([n_own, n_sib], axis=0)
    r_cat = after(jnp.concatenate([r_own, r_sib], axis=0), enter_grad)
    out_grad = tn(merged, r_cat)
    early = jnp.concatenate([out_grad[HV:], tn(gate_grad_par, n_cat)], axis=0).astype(bf16)
    early_got = across(after(early, leaving), 2)
    def backward(h, weights, given, name):
        outs = [(sds((chip, 2 * HK + HV), bf16), "phy"), (sds((16, HK), f32), "all"),
                (sds((1, HK), f32), "all"), (sds((16, width), f32), "all")]
        if given:
            outs += [(sds((rows, width), bf16), "own"), (sds((rows, width), bf16), "sib")]
        else:
            outs += [(sds((chip, width), f32), "seq")]
        return mixer_call(
            backward_kernel, info,
            [(n_own, "own"), (n_sib, "sib"), *[(w, "vmem") for w in weights],
             (down_t, "vmem"), (query, ("col", h, HK)),
             (key, ("col", h, HK)), (value, ("col", h, HV)), (csum, ("col", h, HK)),
             (raw, ("col", h, HK)), (mixed_grad, ("col", h, HV)), (gate_grad, ("col", h, HV)),
             (states, ("head", h)), (leaving, ("one", h))] + [(a, "seq") for a in given],
            outs, [pltpu.VMEM((HV, HK), f32)], name, 10, 32, reverse=True,
        )

    kvq_grad_par, up_par_grad, bias_par_grad, down_par_grad, back_part = backward(
        1, (kvu, qo), (), "mixer_backward_par"
    )
    kvq_par = tn(kvq_grad_par, n_cat).astype(bf16)
    kvq_got = across(kvq_par, 2)
    feed_a, feed_b = far1[7:]
    feed_got = across(after(feed_b, back_part), 1)
    feed_far = across(feed_a[rows:] + feed_got[rows:], 2)
    feed = feed_a[:rows].astype(f32) + feed_got[:rows].astype(f32) + feed_far.astype(f32)
    block_output = (resid + feed).astype(bf16)
    early_got = after(early_got, back_part)
    early_sum = jnp.concatenate(
        [out_grad[:HV] + early_got[:HV].astype(f32),
         tn(gate_grad_own, n_cat) + early_got[HV:].astype(f32)], axis=0
    ).astype(bf16)
    second = Exchange([early_sum], [turned], count)
    back_part = second.tie(back_part)
    second.send()
    kvq_grad_own, up_own_grad, bias_own_grad, down_own_grad, back_own, back_s = backward(
        0, (query_proj, outgate_proj, key_proj, value_proj, u_own), (back_part,),
        "mixer_backward_own",
    )
    input_grad, grad_mixer_gain = mixer_call(
        input_back_kernel, info,
        [(after(back_own, kvq_got), "seq"), (across(back_s, 1), "seq"), (block_input, "seq"),
         (resid_grad, "seq"), (gain_one[None, :], "all")],
        [(sds((rows, width), bf16), "seq"), (sds((1, width), f32), "all")],
        [], "input_back", 5, 24, steps=2,
    )

    kvq_sum = (tn(kvq_grad_own, n_cat) + kvq_got.astype(f32)).astype(bf16)
    decay_own = jnp.concatenate([up_own_grad, bias_own_grad], axis=0)
    decay_par = jnp.concatenate([up_par_grad, bias_par_grad], axis=0)
    small = jnp.concatenate(
        [down_own_grad + down_par_grad, grad_mixer_gain, grad_ffn_gain,
         jnp.pad(gain_grad, ((0, 0), (0, width - HV)))], axis=0
    )
    small = small + across(small, 1)

    def wide_rows(v):
        return jnp.pad(v, ((0, 0), (0, width - HK)))

    got = across(jnp.concatenate([small, wide_rows(decay_par)], axis=0), 2)
    few = got + jnp.concatenate([small, wide_rows(decay_own)], axis=0)
    few = jnp.pad(few, ((0, 28), (0, 0))).astype(bf16)
    second.take(back_s)
    second.send()
    [second] = second.finish()
    second = second.astype(f32)
    packed = jnp.concatenate([kvq_sum, few], axis=0)
    ffn_sum = lax.all_gather(after(ffn_part, packed), "wide", axis=0, tiled=True).astype(f32)
    first = Exchange([packed], [bits], count)
    for step in range(2 * len(bits)):
        first.send()
        if step == 2 * len(bits) - 2:
            first.take(ffn_sum)
        else:
            first.take()
    first = first.arrays[0].astype(f32)
    kvq, few = first[: 2 * HK + HV], first[2 * HK + HV :]
    grad_gate, grad_up, grad_down = jnp.split(ffn_sum, 3, axis=0)
    grad_gate, grad_up = grad_gate.T, grad_up.T
    return (
        block_output,
        input_grad,
        few[16],
        kvq[HK + HV :].T,
        kvq[:HK].T,
        kvq[HK : HK + HV].T,
        second[HV:].T,
        few[:16].T,
        few[19:35, :HK],
        few[35, :HK],
        few[18, :HV],
        second[:HV],
        few[17],
        grad_gate,
        grad_up,
        grad_down,
    )


def solution(mesh):
    placed = (
        P(("wide", "narrow"), None),
        P("wide", None),
        P(),
        P(None, "narrow"),
        P(None, "narrow"),
        P(None, "narrow"),
        P(None, "narrow"),
        P(),
        P(None, "narrow"),
        P("narrow"),
        P(),
        P("narrow", None),
        P(),
        P(None, "narrow"),
        P(None, "narrow"),
        P("narrow", None),
        P(("wide", "narrow"), None),
    )
    return jax.shard_map(
        functools.partial(body, mesh.shape["wide"]),
        mesh=mesh,
        in_specs=placed,
        out_specs=(
            P(("wide", "narrow"), None),
            P(("wide", "narrow"), None),
            P(),
            P(None, "narrow"),
            P(None, "narrow"),
            P(None, "narrow"),
            P(None, "narrow"),
            P(),
            P(None, "narrow"),
            P("narrow"),
            P(),
            P("narrow", None),
            P(),
            P(None, "narrow"),
            P(None, "narrow"),
            P("narrow", None),
        ),
        check_vma=False,
    )
```

```python
import functools

import jax
import jax.numpy as jnp
from jax import lax
from jax.experimental import pallas as pl
from jax.experimental.pallas import tpu as pltpu
from jax.sharding import PartitionSpec as P

HK = 128
HV = 256
SPAN = 64
ROWS = 256
NB = ROWS // SPAN
PER = 2
HALVES = 2
GRAD_ROWS = 512

epsilon = 1e-06
group_floor = 0.25
highest = lax.Precision.HIGHEST
f32 = jnp.float32
bf16 = jnp.bfloat16
scale_q = HK ** (-0.5)


def nn(a, b, precision=None):
    return lax.dot_general(
        a, b, (((1,), (0,)), ((), ())), precision=precision, preferred_element_type=f32
    )


def nt(a, b, precision=None):
    return lax.dot_general(
        a, b, (((1,), (1,)), ((), ())), precision=precision, preferred_element_type=f32
    )


def tn(a, b, precision=None):
    return lax.dot_general(
        a, b, (((0,), (0,)), ((), ())), precision=precision, preferred_element_type=f32
    )


def sigmoid(v):
    return 1.0 / (1.0 + jnp.exp(-v))


def rows_cols():
    i = lax.broadcasted_iota(jnp.int32, (ROWS, ROWS), 0)
    j = lax.broadcasted_iota(jnp.int32, (ROWS, ROWS), 1)
    return i, j


def block_low():
    i, j = rows_cols()
    return (i >= j) & (i // SPAN == j // SPAN)


def doc_start(info, pos):
    e1, e2, e3 = info[2], info[3], info[4]
    start = jnp.where(pos >= e1, e1, 0)
    start = jnp.where(pos >= e2, e2, start)
    return jnp.where(pos >= e3, e3, start)


def scalar_start(info, pos):
    e1, e2, e3 = info[2], info[3], info[4]
    start = jnp.where(pos >= e1, e1, 0)
    start = jnp.where(pos >= e2, e2, start)
    return jnp.where(pos >= e3, e3, start)


def spread(v, row):
    return jnp.concatenate(
        [
            jnp.broadcast_to(v[b * SPAN + row : b * SPAN + row + 1], (SPAN, v.shape[1]))
            for b in range(NB)
        ],
        axis=0,
    )


def pick(info, half, own, sib, r):
    return jnp.where(half == info[0], own[r], sib[r])


def ones_times(mask, v):
    ones = jnp.where(mask, 1.0, 0.0).astype(bf16)
    high = v.astype(bf16)
    rest = v - high.astype(f32)
    middle = rest.astype(bf16)
    low = (rest - middle.astype(f32)).astype(bf16)
    return nn(ones, high) + (nn(ones, middle) + nn(ones, low))


def both(own, par):
    return jnp.concatenate([own[...], par[...]], axis=1)


def project_kernel(
    info, own, sib, k_own, v_own, u_own, kvu, down, key, value, raw, csum, state, acc
):
    half = pl.program_id(0)
    width = own.shape[1]
    k_par, v_par, u_par = kvu.at[:width, :HK], kvu.at[:width, HK:], kvu.at[width:, :HK]
    i, j = rows_cols()
    up = both(u_own, u_par).astype(f32)

    @pl.when(half == 0)
    def _():
        acc[...] = jnp.zeros_like(acc)

    for t in range(PER):
        r = slice(t * ROWS, (t + 1) * ROWS)
        x = pick(info, half, own, sib, r)
        low = nt(x, down[...])
        raws = nn(low, up[:16], highest) + up[16:17]
        raw[r] = raws
        decay = (jnp.minimum(raws, 0.0) - jnp.log1p(jnp.exp(-jnp.abs(raws)))) * (1.0 / 16.0)
        k = nn(x, both(k_own, k_par)).astype(bf16)
        key[r] = k
        v0 = nn(x, v_own[...]).astype(bf16)
        v1 = nn(x, v_par[...]).astype(bf16)
        value[r, :HV] = v0
        value[r, HV:] = v1
        csum[r] = ones_times(block_low(), decay)
        rest = ones_times(j > i, decay)
        total = rest[0:1] + decay[0:1]
        base = info[1] + (half * PER + t) * ROWS
        last = scalar_start(info, base + ROWS - 1)
        pos = base + lax.broadcasted_iota(jnp.int32, (ROWS, 1), 0)
        tail = jnp.where(pos >= last, 1.0, 0.0)
        alive = jnp.where((last < base) & (half + t > 0), 1.0, 0.0)
        ks = (k.astype(f32) * jnp.exp(rest) * tail).astype(bf16)
        keep = jnp.exp(total) * alive
        for h, v in enumerate((v0, v1)):
            hs = slice(h * HK, (h + 1) * HK)
            acc[h] = acc[h] * keep[:, hs] + tn(v, ks[:, hs])

    @pl.when(half == HALVES - 1)
    def _():
        state[0] = acc[1].astype(bf16)
        state[1] = acc[0].astype(bf16)


def factors(info, s, cs):
    base = info[1] + s * ROWS
    row = lax.broadcasted_iota(jnp.int32, (ROWS, 1), 0)
    pos = base + row
    start = doc_start(info, pos)
    living = jnp.where(start < base + (row // SPAN) * SPAN, 1.0, 0.0)
    final = doc_start(info, base + (row // SPAN) * SPAN + SPAN - 1)
    tail = jnp.where(pos >= final, 1.0, 0.0)
    alive = []
    for b in range(NB):
        first = base + b * SPAN
        alive.append(jnp.where(scalar_start(info, first + SPAN - 1) < first, 1.0, 0.0))
    i, j = rows_cols()
    mask = block_low() & (base + j >= start)
    return living, tail, alive, mask


def forward_kernel(
    info, own, sib, q_own, o_own, qo, gain, key, value, csum, entering,
    query, gate_out, mixed, merged, states, acc,
):
    half = pl.program_id(0)
    q_par, o_par = qo.at[:, :HK], qo.at[:, HK : HK + HV]

    @pl.when(half == 0)
    def _():
        acc[...] = entering[...].astype(f32)

    sts = [acc[0], acc[1]]
    for t in range(PER):
        r = slice(t * ROWS, (t + 1) * ROWS)
        x = pick(info, half, own, sib, r)
        living, tail, alive, mask = factors(info, half * PER + t, None)
        q = nn(x, both(q_own, q_par)).astype(bf16)
        query[r] = q
        for h in range(2):
            w = o_own if h == 0 else o_par
            hs, vs = slice(h * HK, (h + 1) * HK), slice(h * HV, (h + 1) * HV)
            go = nn(x, w[...])
            gate_out[r, vs] = go.astype(bf16)
            cs = csum[r, hs]
            centre, last = spread(cs, SPAN // 2), spread(cs, SPAN - 1)
            qt = q[:, hs].astype(f32) * scale_q
            k = key[r, hs].astype(f32)
            v = value[r, vs]
            qe = (qt * jnp.exp(cs - centre)).astype(bf16)
            ke = (k * jnp.exp(centre - cs)).astype(bf16)
            qc = (qt * jnp.exp(cs) * living).astype(bf16)
            kt = (k * jnp.exp(last - cs) * tail).astype(bf16)
            scores = jnp.where(mask, nt(qe, ke), 0.0).astype(bf16)
            inside = nn(scores, v)
            st = sts[h]
            carried = []
            for b in range(NB):
                rb = slice(b * SPAN, (b + 1) * SPAN)
                stb = st.astype(bf16)
                states[t, h, b] = stb
                carried.append(nt(qc[rb], stb))
                f = jnp.exp(cs[(b + 1) * SPAN - 1 : (b + 1) * SPAN]) * alive[b]
                st = st * f + tn(v[rb], kt[rb])
            sts[h] = st
            mix = inside + jnp.concatenate(carried, axis=0)
            mixed[r, vs] = mix.astype(bf16)
            inv = lax.rsqrt(jnp.mean(mix * mix, axis=-1, keepdims=True) + group_floor)
            merged[r, vs] = (mix * inv * gain[...] * (go * sigmoid(go))).astype(bf16)
    acc[0] = sts[0]
    acc[1] = sts[1]


def gate_back_kernel(
    info, own, sib, out_own, out_par, gain, mixed, gate_out, query, csum,
    mixed_grad, gate_grad, gain_grad, enter_grad, acc, carry,
):
    half = pl.program_id(0)

    @pl.when(half == 0)
    def _():
        acc[...] = jnp.zeros_like(acc)
        carry[...] = jnp.zeros_like(carry)
        gain_grad[...] = jnp.zeros_like(gain_grad)

    gn = gain[...]
    total = jnp.zeros_like(gn)
    for h in range(2):
        hs, vs = slice(h * HK, (h + 1) * HK), slice(h * HV, (h + 1) * HV)
        offset = carry[:, hs]
        for t in range(PER):
            r = slice(t * ROWS, (t + 1) * ROWS)
            g = pick(info, half, own, sib, r)
            base = info[1] + (half * PER + t) * ROWS
            pos = base + lax.broadcasted_iota(jnp.int32, (ROWS, 1), 0)
            living = jnp.where(doc_start(info, pos) < info[1], 1.0, 0.0)
            wo = out_own if h == 0 else out_par
            mg = nt(g, wo[...]).astype(bf16).astype(f32)
            mix = mixed[r, vs].astype(f32)
            go = gate_out[r, vs].astype(f32)
            inv = lax.rsqrt(jnp.mean(mix * mix, axis=-1, keepdims=True) + group_floor)
            n = mix * inv
            sg = sigmoid(go)
            silu = go * sg
            ng = mg * n
            dgo = (ng * gn * (sg + silu * (1.0 - sg))).astype(bf16)
            gate_grad[r, vs] = dgo
            total = total + jnp.sum(ng * silu, axis=0, keepdims=True)
            dn = mg * gn * silu
            do = (inv * (dn - n * jnp.mean(dn * n, axis=-1, keepdims=True))).astype(bf16)
            mixed_grad[r, vs] = do
            cs = csum[r, hs]
            parts = []
            for b in range(NB):
                parts.append(cs[b * SPAN : (b + 1) * SPAN] + offset)
                offset = offset + cs[(b + 1) * SPAN - 1 : (b + 1) * SPAN]
            qcc = (
                query[r, hs].astype(f32) * scale_q * jnp.exp(jnp.concatenate(parts, axis=0)) * living
            )
            acc[h] += tn(do, qcc.astype(bf16))
        carry[:, hs] = offset
    gain_grad[...] += total

    @pl.when(half == HALVES - 1)
    def _():
        enter_grad[0] = acc[1].astype(bf16)
        enter_grad[1] = acc[0].astype(bf16)


def backward_kernel(
    info, own, sib, *rest,
):
    width = own.shape[1]
    if len(rest) == 18:
        kvu, qo, *rest = rest
        q_w, o_w = qo.at[:, :HK], qo.at[:, HK : HK + HV]
        k_w, v_w, u_w = kvu.at[:width, :HK], kvu.at[:width, HK:], kvu.at[width:, :HK]
    else:
        q_w, o_w, k_w, v_w, u_w, *rest = rest
    down, query, key, value, csum, raw, mixed_grad, gate_grad, states, leaving, *rest = rest
    given, rest = (rest[:1], rest[1:]) if len(rest) == 8 else ((), rest)
    kvq_grad, up_grad, bias_grad, down_grad, *outs, acc = rest
    step = pl.program_id(0)
    half = HALVES - 1 - step

    @pl.when(step == 0)
    def _():
        acc[...] = leaving[0].astype(f32)
        up_grad[...] = jnp.zeros_like(up_grad)
        bias_grad[...] = jnp.zeros_like(bias_grad)
        down_grad[...] = jnp.zeros_like(down_grad)

    i, j = rows_cols()
    upper = (i <= j) & (i // SPAN == j // SPAN)
    up = u_w[:16].astype(f32)
    w_qk = jnp.concatenate([q_w[...], k_w[...]], axis=1)
    gt = acc[...]
    lows, ranks, grads, backs = [None] * PER, [None] * PER, [None] * PER, [None] * PER
    for t in reversed(range(PER)):
        r = slice(t * ROWS, (t + 1) * ROWS)
        x = pick(info, half, own, sib, r)
        living, tail, alive, mask = factors(info, half * PER + t, None)
        cs = csum[r]
        centre, last = spread(cs, SPAN // 2), spread(cs, SPAN - 1)
        qt = query[r].astype(f32) * scale_q
        k = key[r].astype(f32)
        v = value[r]
        do = mixed_grad[r]
        eq, ek = jnp.exp(cs - centre), jnp.exp(centre - cs)
        ec, et = jnp.exp(cs) * living, jnp.exp(last - cs) * tail
        qe, ke = (qt * eq).astype(bf16), (k * ek).astype(bf16)
        qcf, ktf = qt * ec, k * et
        qc, kt = qcf.astype(bf16), ktf.astype(bf16)
        scores = jnp.where(mask, nt(qe, ke), 0.0).astype(bf16)
        ds = jnp.where(mask, nt(do, v), 0.0).astype(bf16)
        dqe = nn(ds, ke)
        dke = tn(ds, qe)
        dv = tn(scores, do)
        dqc, dkt, dvt, dlast = [None] * NB, [None] * NB, [None] * NB, [None] * NB
        for b in reversed(range(NB)):
            rb = slice(b * SPAN, (b + 1) * SPAN)
            gtb = gt.astype(bf16)
            st = states[t, 0, b]
            dvt[b] = nt(kt[rb], gtb)
            dkt[b] = nn(v[rb], gtb)
            dqc[b] = nn(do[rb], st)
            f = jnp.exp(cs[(b + 1) * SPAN - 1 : (b + 1) * SPAN]) * alive[b]
            moved = f * jnp.sum(st.astype(f32) * gt, axis=0, keepdims=True)
            tails = jnp.sum(ktf[rb] * dkt[b], axis=0, keepdims=True)
            dlast[b] = jnp.broadcast_to(moved + tails, (SPAN, HK))
            gt = gt * f + tn(do[rb], qc[rb])
        dqc = jnp.concatenate(dqc, axis=0)
        dkt = jnp.concatenate(dkt, axis=0)
        dv = (dv + jnp.concatenate(dvt, axis=0)).astype(bf16)
        dq = ((dqe * eq + dqc * ec) * scale_q).astype(bf16)
        dk = (dke * ek + dkt * et).astype(bf16)
        dc = qe.astype(f32) * dqe - ke.astype(f32) * dke + qcf * dqc - ktf * dkt
        ddecay = ones_times(upper, dc) + jnp.concatenate(dlast, axis=0)
        raw_grad = ddecay * sigmoid(-raw[r]) * (1.0 / 16.0)
        kvq_grad[r, :HK] = dk
        kvq_grad[r, HK : HK + HV] = dv
        kvq_grad[r, HK + HV :] = dq
        rank_low = nt(raw_grad, up, highest).astype(bf16)
        lows[t] = nt(x, down[...])
        ranks[t], grads[t] = rank_low, raw_grad
        back = nt(dv, v_w[...]) + nt(gate_grad[r], o_w[...]) + nn(rank_low, down[...])
        back = back + nt(jnp.concatenate([dq, dk], axis=1), w_qk)
        if given:
            backs[t] = (back + given[0][r].astype(f32)).astype(bf16)
        else:
            outs[0][r] = back.astype(bf16)
    acc[...] = gt
    raw_grad = jnp.concatenate(grads, axis=0)
    up_grad[...] += tn(jnp.concatenate(lows, axis=0), raw_grad, highest)
    bias_grad[...] += jnp.sum(raw_grad, axis=0, keepdims=True)
    down_grad[...] += tn(
        jnp.concatenate(ranks, axis=0), jnp.where(half == info[0], own[...], sib[...])
    )
    if not given:
        return
    use_own = half == info[0]
    back = jnp.concatenate(backs, axis=0)

    @pl.when(use_own)
    def _():
        outs[0][...] = back

    @pl.when(jnp.logical_not(use_own))
    def _():
        outs[1][...] = back


def ffn_kernel(
    place, n_a, n_b, g_a, g_b, gate_w, up_w, down_w, *rest,
):
    hidden, gate_grad, up_grad, n_cat, g_cat, feed_a, feed_b, back_a, back_b = rest[-9:]
    i = pl.program_id(0)
    first = i < pl.num_programs(0) // 2
    n = jnp.where(first, n_a[...], n_b[...])
    g = jnp.where(first, g_a[...], g_b[...])
    n_cat[...] = n
    g_cat[...] = g
    gate = nt(n, gate_w[...])
    up = nt(n, up_w[...])
    gh = nt(g, down_w[...]).astype(bf16).astype(f32)
    sg = sigmoid(gate)
    silu = gate * sg
    hid = (silu * up).astype(bf16)
    gg = (gh * up * (sg + silu * (1.0 - sg))).astype(bf16)
    ug = (gh * silu).astype(bf16)
    hidden[...] = hid
    gate_grad[...] = gg
    up_grad[...] = ug
    feed = nn(hid, down_w[...]).astype(bf16)
    back = (nn(gg, gate_w[...]) + nn(ug, up_w[...])).astype(bf16)

    @pl.when(first)
    def _():
        feed_a[...] = feed
        back_a[...] = back

    @pl.when(jnp.logical_not(first))
    def _():
        feed_b[...] = feed
        back_b[...] = back


def ffn_grad_kernel(h, gg, ug, n, g, out, acc):
    units = h.shape[1]
    i = pl.program_id(0)

    @pl.when(i == 0)
    def _():
        acc[...] = jnp.zeros_like(acc)

    for k, (left, right) in enumerate(((gg, n), (ug, n), (h, g))):
        rows = slice(k * units, (k + 1) * units)
        acc[rows] += tn(left[...], right[...])

    @pl.when(i == pl.num_programs(0) - 1)
    def _():
        out[...] = acc[...].astype(out.dtype)


def ffn_grad_call(arrays, dtype, name, us):
    rows, units = arrays[0].shape
    width = arrays[3].shape[1]
    step = GRAD_ROWS
    out = jax.ShapeDtypeStruct((3 * units, width), dtype)
    return pl.pallas_call(
        ffn_grad_kernel,
        out_shape=out_hbm(out),
        grid=(rows // step,),
        in_specs=[pl.BlockSpec((step, a.shape[1]), lambda i: (i, 0)) for a in arrays],
        out_specs=whole(out),
        scratch_shapes=[pltpu.VMEM((3 * units, width), f32)],
        compiler_params=params(40),
        cost_estimate=cost(us),
        name=name,
    )(*[in_hbm(a) for a in arrays])


def resid_back_kernel(info, own, sib, got0, got1, resid, g, gain, resid_grad, low, gain_grad):
    i = pl.program_id(0)
    got = jnp.where(i == 0, got0[...], got1[...])
    back = own[...].astype(f32) + sib[...].astype(f32) + got.astype(f32)
    res = resid[...]
    scale = lax.rsqrt(jnp.mean(res * res, axis=-1, keepdims=True) + epsilon)
    unit = res * scale
    scaled = back * gain[...]
    grad = g[...].astype(f32) + scale * (
        scaled - unit * jnp.mean(scaled * unit, axis=-1, keepdims=True)
    )
    resid_grad[...] = grad
    low[...] = grad.astype(bf16)
    part = jnp.sum(back * unit, axis=0, keepdims=True)

    @pl.when(i == 0)
    def _():
        gain_grad[...] = part

    @pl.when(i > 0)
    def _():
        gain_grad[...] += part


def input_back_kernel(info, own, sib, x, resid_grad, gain, input_grad, gain_grad):
    i = pl.program_id(0)
    back = own[...].astype(f32) + sib[...].astype(f32)
    values = x[...].astype(f32)
    scale = lax.rsqrt(jnp.mean(values * values, axis=-1, keepdims=True) + epsilon)
    unit = values * scale
    scaled = back * gain[...]
    grad = resid_grad[...] + scale * (
        scaled - unit * jnp.mean(scaled * unit, axis=-1, keepdims=True)
    )
    input_grad[...] = grad.astype(bf16)
    part = jnp.sum(back * unit, axis=0, keepdims=True)

    @pl.when(i == 0)
    def _():
        gain_grad[...] = part

    @pl.when(i > 0)
    def _():
        gain_grad[...] += part


def params(mib):
    return pltpu.CompilerParams(
        dimension_semantics=("arbitrary",), vmem_limit_bytes=mib * 1024 * 1024
    )


def cost(us):
    return pl.CostEstimate(flops=us * 1_000_000_000, transcendentals=0, bytes_accessed=us * 1_000_000)


def in_hbm(a):
    return pltpu.with_memory_space_constraint(a, pltpu.HBM)


def out_hbm(a):
    return pltpu.HBM(a.shape, a.dtype)


def whole(a):
    zero = (0,) * a.ndim
    return pl.BlockSpec(a.shape, lambda *_: zero)


def resident():
    return pl.BlockSpec(memory_space=pltpu.VMEM)


def mixer_call(
    kernel, info, ins, outs, scratch, name, us, mib, reverse=False, block=PER * ROWS
):
    steps = HALVES

    def at(s):
        return steps - 1 - s if reverse else s

    def spec(a, kind):
        if isinstance(kind, tuple) and kind[0] == "col":
            return pl.BlockSpec((block, kind[2]), lambda s, info: (at(s), kind[1]))
        if isinstance(kind, tuple) and kind[0] == "phycol":
            return pl.BlockSpec((block, kind[2]), lambda s, info: ((at(s) + info[0]) % 2, kind[1]))
        if isinstance(kind, tuple) and kind[0] == "head":
            return pl.BlockSpec(
                (a.shape[0] // steps, 1, *a.shape[2:]), lambda s, info: (at(s), kind[1], 0, 0, 0)
            )
        if isinstance(kind, tuple) and kind[0] == "one":
            return pl.BlockSpec((1, *a.shape[1:]), lambda s, info: (kind[1], 0, 0))
        if kind == "seq":
            return pl.BlockSpec((block, a.shape[1]), lambda s, info: (at(s), 0))
        if kind == "phy":
            return pl.BlockSpec((block, a.shape[1]), lambda s, info: ((at(s) + info[0]) % 2, 0))
        if kind == "blk":
            zero = (0,) * (a.ndim - 1)
            return pl.BlockSpec((a.shape[0] // steps, *a.shape[1:]), lambda s, info: (at(s), *zero))
        return whole(a)

    return pl.pallas_call(
        kernel,
        out_shape=[out_hbm(a) for a, _ in outs],
        grid_spec=pltpu.PrefetchScalarGridSpec(
            num_scalar_prefetch=1,
            grid=(steps,),
            in_specs=[spec(a, kind) for a, kind in ins],
            out_specs=[spec(a, kind) for a, kind in outs],
            scratch_shapes=scratch,
        ),
        compiler_params=params(mib),
        cost_estimate=cost(us),
        name=name,
    )(info, *[in_hbm(a) for a, _ in ins])


def ffn_call(place, n_a, n_b, g_a, g_b, gate_w, up_w, down_w, name, flip, part=0, given=()):
    rows, width = n_a.shape
    units = gate_w.shape[0]
    steps = 2 * rows // ROWS
    half = steps // 2
    per = 2
    done = 2 * (flip + part)
    at = part + (flip // 2) * per

    def g_low(i, place):
        here = (place[0] ^ flip) * per + part if flip else 0
        return here + jnp.minimum(i, half - 1), 0

    def g_high(i, place):
        here = (place[0] ^ (flip + 1)) * per + part if flip else 0
        return here + jnp.maximum(i - half, 0), 0

    def low(first):
        return pl.BlockSpec((ROWS, width), lambda i, place: (first + jnp.minimum(i, half - 1), 0))

    def high(first):
        return pl.BlockSpec((ROWS, width), lambda i, place: (first + jnp.maximum(i - half, 0), 0))

    cat = pl.BlockSpec((ROWS, width), lambda i, place: (done + i, 0))
    mid = pl.BlockSpec((ROWS, units), lambda i, place: (done + i, 0))
    hbm = pl.BlockSpec(memory_space=pl.ANY)
    every = 4 * per * ROWS

    def out(count, cols):
        return pltpu.HBM((count, cols), bf16)

    return pl.pallas_call(
        ffn_kernel,
        out_shape=[out(every, units)] * 3
        + [out(every, width)] * 2
        + [out(2 * per * ROWS, width)] * 2
        + [out(rows, width)] * 2,
        grid_spec=pltpu.PrefetchScalarGridSpec(
            num_scalar_prefetch=1,
            grid=(steps,),
            in_specs=[low(0), high(0), pl.BlockSpec((ROWS, width), g_low), pl.BlockSpec((ROWS, width), g_high)]
            + [whole(w) for w in (gate_w, up_w, down_w)]
            + [hbm] * len(given),
            out_specs=[mid, mid, mid, cat, cat, low(at), high(at), low(0), high(0)],
        ),
        input_output_aliases={8 + k: k for k in range(len(given))},
        compiler_params=params(32),
        cost_estimate=cost(3 * steps + 2),
        name=name,
    )(place, *[in_hbm(a) for a in (n_a, n_b, g_a, g_b)], *[in_hbm(w) for w in (gate_w, up_w, down_w)], *[in_hbm(a) for a in given])


def across(v, bit):
    return lax.ppermute(v, "narrow", [(i, i ^ bit) for i in range(4)])


def forth(v):
    return lax.ppermute(v, "narrow", [(0, 2), (1, 3)])


def back_to(v):
    return lax.ppermute(v, "narrow", [(2, 0), (3, 1)])


def after(v, *others):
    return lax.optimization_barrier((v, *others))[0]


def pairs(count, bit):
    return [(i, i ^ bit) for i in range(count)]


def wide_send(v, bit, count):
    half = v.shape[0] // 2
    high = (lax.axis_index("wide") // bit) % 2
    keep = lax.dynamic_slice_in_dim(v, high * half, half, 0)
    send = lax.dynamic_slice_in_dim(v, (1 - high) * half, half, 0)
    return keep, lax.ppermute(send, "wide", pairs(count, bit))


def wide_add(keep, got, *earlier):
    got = after(got, *earlier) if earlier else got
    return (keep.astype(f32) + got.astype(f32)).astype(bf16)


class Exchange:
    def __init__(self, arrays, orders, count):
        self.arrays, self.orders, self.count, self.step = arrays, orders, count, 0

    def begin(self, keeps, sends):
        self.sent = [
            (keep, lax.ppermute(send, "wide", pairs(self.count, order[0])))
            for keep, send, order in zip(keeps, sends, self.orders)
        ]

    def send(self):
        n = len(self.orders[0])
        self.sent = []
        for v, order in zip(self.arrays, self.orders):
            if self.step < n:
                self.sent.append(wide_send(v, order[self.step], self.count))
            else:
                got = lax.ppermute(v, "wide", pairs(self.count, order[2 * n - 1 - self.step]))
                self.sent.append((v, got))

    def take(self, *earlier):
        n = len(self.orders[0])
        arrays = []
        for (keep, got), order in zip(self.sent, self.orders):
            if self.step < n:
                arrays.append(wide_add(keep, got, *earlier))
            else:
                got = after(got, *earlier) if earlier else got
                high = (lax.axis_index("wide") // order[2 * n - 1 - self.step]) % 2
                arrays.append(
                    jnp.where(
                        high == 0,
                        jnp.concatenate([keep, got], 0),
                        jnp.concatenate([got, keep], 0),
                    )
                )
        self.arrays = arrays
        self.step += 1

    def tie(self, v):
        v, *self.arrays = lax.optimization_barrier((v, *self.arrays))
        return v

    def finish(self, fresh=False):
        if not fresh:
            self.take()
        while self.step < 2 * len(self.orders[0]):
            self.send()
            self.take()
        return self.arrays


def wide_pieces(v, count):
    return lax.all_to_all(
        v.reshape(count, v.shape[0] // count, v.shape[1]), "wide", 0, 0, tiled=True
    )


def added(pieces):
    return jnp.sum(pieces.astype(f32), axis=0).astype(bf16)


def wide_copies(v, count):
    spread_out = jnp.broadcast_to(v[None], (count, *v.shape))
    got = lax.all_to_all(spread_out, "wide", 0, 0, tiled=True)
    return got.reshape(count * v.shape[0], v.shape[1])


def body(
    count, block_input, doc_lengths, mixer_gain, query_proj, key_proj, value_proj, outgate_proj,
    decay_down, decay_up, decay_bias, group_gain, output_proj, ffn_gain, gate_proj, up_proj,
    down_proj, cotangent,
):
    sds = jax.ShapeDtypeStruct
    rows, width = block_input.shape
    chip = 2 * rows
    place = lax.axis_index("narrow")
    lengths = doc_lengths[0]
    e1 = lengths[0]
    e2 = e1 + lengths[1]
    e3 = e2 + lengths[2]
    info = jnp.stack([place % 2, (place // 2) * chip, e1, e2, e3]).astype(jnp.int32)

    u_own = jnp.concatenate(
        [decay_up, decay_bias[None, :], jnp.zeros((15, decay_up.shape[1]), bf16)], axis=0
    )
    kvu_own = jnp.concatenate(
        [
            jnp.concatenate([key_proj, value_proj], axis=1),
            jnp.pad(u_own, ((0, 0), (0, HV))),
        ],
        axis=0,
    )
    kvu = across(kvu_own, 2)
    inputs = after(block_input, kvu_own).astype(f32)
    scale_one = lax.rsqrt(jnp.mean(inputs * inputs, axis=-1, keepdims=True) + epsilon)
    unit_one = inputs * scale_one
    gain_one = mixer_gain.astype(f32)
    n_own = (unit_one * gain_one).astype(bf16)
    n_sib = across(n_own, 1)
    out_flat = output_proj.reshape(width, HV)
    qo = across(
        after(jnp.concatenate([query_proj, outgate_proj, out_flat], axis=1), n_own), 2
    )
    out_par = qo[:, HK + HV :].reshape(HV, width)
    down_t = decay_down.T

    group = group_gain.astype(f32)[None, :]
    key, value, raw, csum, state = mixer_call(
        project_kernel, info,
        [(n_own, "own"), (n_sib, "sib"), (key_proj, "vmem"), (value_proj, "vmem"), (u_own, "vmem"),
         (kvu, "vmem"), (down_t, "vmem")],
        [(sds((chip, 2 * HK), bf16), "seq"), (sds((chip, 2 * HV), bf16), "seq"),
         (sds((chip, 2 * HK), f32), "seq"), (sds((chip, 2 * HK), f32), "seq"),
         (sds((2, HV, HK), bf16), "all")],
        [pltpu.VMEM((2, HV, HK), f32)], "project", 10, 24,
    )
    entering = forth(state)
    g_sib = across(after(cotangent, state), 1)
    g_all = lax.all_gather(after(cotangent, qo, state), "narrow", axis=0, tiled=True)
    query, gate_out, mixed, merged, states = mixer_call(
        forward_kernel, info,
        [(n_own, "own"), (n_sib, "sib"), (query_proj, "vmem"), (outgate_proj, "vmem"), (qo, "vmem"), (group, "vmem"), (key, "seq"), (value, "seq"), (csum, "seq"), (entering, "vmem")],
        [(sds((chip, 2 * HK), bf16), "seq"), (sds((chip, 2 * HV), bf16), "seq"),
         (sds((chip, 2 * HV), bf16), "seq"), (sds((chip, 2 * HV), bf16), "phy"),
         (sds((4, 2, NB, HV, HK), bf16), "blk")],
        [pltpu.VMEM((2, HV, HK), f32)], "mixer_forward", 11, 32,
    )
    out_w = jnp.concatenate([output_proj, out_par], axis=0)
    att_sib = across(nn(merged[rows:], out_w).astype(bf16), 1)
    resid = inputs + nn(merged[:rows], out_w) + att_sib.astype(f32)
    scale_two = lax.rsqrt(jnp.mean(resid * resid, axis=-1, keepdims=True) + epsilon)
    gain_two = ffn_gain.astype(f32)[None, :]
    m_own = (resid * scale_two * gain_two).astype(bf16)
    m_0, m_1 = m_own[: rows // 2], m_own[rows // 2 :]
    m_sib = across(m_own, 1)
    m_x0 = across(m_0, 2)
    m_x1 = across(m_1, 2)
    gate_t, up_t = gate_proj.T, up_proj.T
    spot = place.astype(jnp.int32)[None]
    near = ffn_call(spot, m_own, m_sib, cotangent, g_sib, gate_t, up_t, down_proj, "ffn_near", 0)
    m_s0 = across(after(m_x0, near[0]), 1)
    far0 = ffn_call(
        spot, m_x0, m_s0, g_all, g_all, gate_t, up_t, down_proj, "ffn_far", 2, 0, near[:7]
    )
    m_s1 = across(after(m_x1, far0[0]), 1)
    far1 = ffn_call(
        spot, after(m_x1, far0[0]), m_s1, g_all, g_all, gate_t, up_t, down_proj, "ffn_far", 2, 1, far0[:7]
    )
    near_got = across(near[8], 1)
    back_x = [far[7] + across(far[8], 1) for far in (far0, far1)]
    back_got = [across(v, 2) for v in back_x]
    parts = [after(v, *back_x) for v in far1[:5]]
    bits = [1 << b for b in range(count.bit_length() - 1)]
    turned = bits[1:2] + bits[:1] + bits[2:]
    ffn_grads = ffn_grad_call(parts, bf16, "ffn_grads", 18)
    ffn_part = lax.psum_scatter(ffn_grads, "wide", scatter_dimension=0, tiled=True)
    resid_grad, r_own, grad_ffn_gain = mixer_call(
        resid_back_kernel, info,
        [(near[7], "seq"), (near_got, "seq"), (after(back_got[0], ffn_grads), "all"),
         (back_got[1], "all"), (resid, "seq"), (cotangent, "seq"), (gain_two, "all")],
        [(sds((rows, width), f32), "seq"), (sds((rows, width), bf16), "seq"),
         (sds((1, width), f32), "all")],
        [], "resid_back", 3, 24, block=ROWS,
    )
    r_sib = across(r_own, 1)


    mixed_grad, gate_grad, gain_grad, enter_grad = mixer_call(
        gate_back_kernel, info,
        [(r_own, "own"), (r_sib, "sib"), (output_proj, "vmem"), (out_par, "vmem"), (group, "vmem"),
         (mixed, "seq"), (gate_out, "seq"), (query, "seq"), (csum, "seq")],
        [(sds((chip, 2 * HV), bf16), "seq"), (sds((chip, 2 * HV), bf16), "phy"),
         (sds((1, HV), f32), "all"), (sds((2, HV, HK), bf16), "all")],
        [pltpu.VMEM((2, HV, HK), f32), pltpu.VMEM((1, 2 * HK), f32)], "gate_backward", 6, 32,
    )
    leaving = back_to(enter_grad)
    n_cat = jnp.concatenate([n_own, n_sib], axis=0)
    r_cat = after(jnp.concatenate([r_own, r_sib], axis=0), enter_grad)
    out_grad = tn(merged, r_cat)
    early = jnp.concatenate([out_grad[HV:], tn(gate_grad[:, HV:], n_cat)], axis=0).astype(bf16)
    early_got = across(after(early, leaving), 2)
    def backward(h, weights, given, name):
        outs = [(sds((chip, 2 * HK + HV), bf16), "phy"), (sds((16, HK), f32), "all"),
                (sds((1, HK), f32), "all"), (sds((16, width), f32), "all")]
        if given:
            outs += [(sds((rows, width), bf16), "own"), (sds((rows, width), bf16), "sib")]
        else:
            outs += [(sds((chip, width), bf16), "seq")]
        return mixer_call(
            backward_kernel, info,
            [(n_own, "own"), (n_sib, "sib"), *[(w, "vmem") for w in weights],
             (down_t, "vmem"), (query, ("col", h, HK)),
             (key, ("col", h, HK)), (value, ("col", h, HV)), (csum, ("col", h, HK)),
             (raw, ("col", h, HK)), (mixed_grad, ("col", h, HV)), (gate_grad, ("phycol", h, HV)),
             (states, ("head", h)), (leaving, ("one", h))] + [(a, "seq") for a in given],
            outs, [pltpu.VMEM((HV, HK), f32)], name, 10, 32, reverse=True,
        )

    kvq_grad_par, up_par_grad, bias_par_grad, down_par_grad, back_part = backward(
        1, (kvu, qo), (), "mixer_backward_par"
    )
    kvq_par = tn(kvq_grad_par, n_cat).astype(bf16)
    kvq_got = across(kvq_par, 2)
    feed_a, feed_b = far1[5:7]
    feed_got = across(after(feed_b, back_part), 1)
    feed_far = across(feed_a[rows:] + feed_got[rows:], 2)
    feed = feed_a[:rows].astype(f32) + feed_got[:rows].astype(f32) + feed_far.astype(f32)
    block_output = (resid + feed).astype(bf16)
    early_got = after(early_got, back_part)
    early_sum = jnp.concatenate(
        [out_grad[:HV] + early_got[:HV].astype(f32),
         tn(gate_grad[:, :HV], n_cat) + early_got[HV:].astype(f32)], axis=0
    ).astype(bf16)
    second = Exchange([early_sum], [turned], count)
    back_part = second.tie(back_part)
    second.send()
    kvq_grad_own, up_own_grad, bias_own_grad, down_own_grad, back_own, back_s = backward(
        0, (query_proj, outgate_proj, key_proj, value_proj, u_own), (back_part,),
        "mixer_backward_own",
    )
    input_grad, grad_mixer_gain = mixer_call(
        input_back_kernel, info,
        [(after(back_own, kvq_got), "seq"), (across(back_s, 1), "seq"), (block_input, "seq"),
         (resid_grad, "seq"), (gain_one[None, :], "all")],
        [(sds((rows, width), bf16), "seq"), (sds((1, width), f32), "all")],
        [], "input_back", 5, 24, block=ROWS,
    )

    kvq_sum = (tn(kvq_grad_own, n_cat) + kvq_got.astype(f32)).astype(bf16)
    decay_own = jnp.concatenate([up_own_grad, bias_own_grad], axis=0)
    decay_par = jnp.concatenate([up_par_grad, bias_par_grad], axis=0)
    small = jnp.concatenate(
        [down_own_grad + down_par_grad, grad_mixer_gain, grad_ffn_gain,
         jnp.pad(gain_grad, ((0, 0), (0, width - HV)))], axis=0
    )
    small = small + across(small, 1)

    def wide_rows(v):
        return jnp.pad(v, ((0, 0), (0, width - HK)))

    got = across(jnp.concatenate([small, wide_rows(decay_par)], axis=0), 2)
    few = got + jnp.concatenate([small, wide_rows(decay_own)], axis=0)
    few = jnp.pad(few, ((0, 28), (0, 0))).astype(bf16)
    second.take(back_s)
    second.send()
    [second] = second.finish()
    second = second.astype(f32)
    packed = jnp.concatenate([kvq_sum, few], axis=0)
    ffn_sum = lax.all_gather(after(ffn_part, packed), "wide", axis=0, tiled=True).astype(f32)
    first = Exchange([packed], [bits], count)
    for step in range(2 * len(bits)):
        first.send()
        if step == 2 * len(bits) - 2:
            first.take(ffn_sum)
        else:
            first.take()
    first = first.arrays[0].astype(f32)
    kvq, few = first[: 2 * HK + HV], first[2 * HK + HV :]
    grad_gate, grad_up, grad_down = jnp.split(ffn_sum, 3, axis=0)
    grad_gate, grad_up = grad_gate.T, grad_up.T
    return (
        block_output,
        input_grad,
        few[16],
        kvq[HK + HV :].T,
        kvq[:HK].T,
        kvq[HK : HK + HV].T,
        second[HV:].T,
        few[:16].T,
        few[19:35, :HK],
        few[35, :HK],
        few[18, :HV],
        second[:HV],
        few[17],
        grad_gate,
        grad_up,
        grad_down,
    )


def solution(mesh):
    placed = (
        P(("wide", "narrow"), None),
        P("wide", None),
        P(),
        P(None, "narrow"),
        P(None, "narrow"),
        P(None, "narrow"),
        P(None, "narrow"),
        P(),
        P(None, "narrow"),
        P("narrow"),
        P(),
        P("narrow", None),
        P(),
        P(None, "narrow"),
        P(None, "narrow"),
        P("narrow", None),
        P(("wide", "narrow"), None),
    )
    return jax.shard_map(
        functools.partial(body, mesh.shape["wide"]),
        mesh=mesh,
        in_specs=placed,
        out_specs=(
            P(("wide", "narrow"), None),
            P(("wide", "narrow"), None),
            P(),
            P(None, "narrow"),
            P(None, "narrow"),
            P(None, "narrow"),
            P(None, "narrow"),
            P(),
            P(None, "narrow"),
            P("narrow"),
            P(),
            P("narrow", None),
            P(),
            P(None, "narrow"),
            P(None, "narrow"),
            P("narrow", None),
        ),
        check_vma=False,
    )
```

```python
import functools

import jax
import jax.numpy as jnp
from jax import lax
from jax.experimental import pallas as pl
from jax.experimental.pallas import tpu as pltpu
from jax.sharding import PartitionSpec as P

HK = 128
HV = 256
SPAN = 64
ROWS = 256
NB = ROWS // SPAN
PER = 2
HALVES = 2
GRAD_ROWS = 512

epsilon = 1e-06
group_floor = 0.25
highest = lax.Precision.HIGHEST
f32 = jnp.float32
bf16 = jnp.bfloat16
scale_q = HK ** (-0.5)


def nn(a, b, precision=None):
    return lax.dot_general(
        a, b, (((1,), (0,)), ((), ())), precision=precision, preferred_element_type=f32
    )


def nt(a, b, precision=None):
    return lax.dot_general(
        a, b, (((1,), (1,)), ((), ())), precision=precision, preferred_element_type=f32
    )


def tn(a, b, precision=None):
    return lax.dot_general(
        a, b, (((0,), (0,)), ((), ())), precision=precision, preferred_element_type=f32
    )


def sigmoid(v):
    return 1.0 / (1.0 + jnp.exp(-v))


def rows_cols():
    i = lax.broadcasted_iota(jnp.int32, (ROWS, ROWS), 0)
    j = lax.broadcasted_iota(jnp.int32, (ROWS, ROWS), 1)
    return i, j


def block_low():
    i, j = rows_cols()
    return (i >= j) & (i // SPAN == j // SPAN)


def doc_start(info, pos):
    e1, e2, e3 = info[2], info[3], info[4]
    start = jnp.where(pos >= e1, e1, 0)
    start = jnp.where(pos >= e2, e2, start)
    return jnp.where(pos >= e3, e3, start)


def scalar_start(info, pos):
    e1, e2, e3 = info[2], info[3], info[4]
    start = jnp.where(pos >= e1, e1, 0)
    start = jnp.where(pos >= e2, e2, start)
    return jnp.where(pos >= e3, e3, start)


def spread(v, row):
    return jnp.concatenate(
        [
            jnp.broadcast_to(v[b * SPAN + row : b * SPAN + row + 1], (SPAN, v.shape[1]))
            for b in range(NB)
        ],
        axis=0,
    )


def pick(info, half, own, sib, r):
    return jnp.where(half == info[0], own[r], sib[r])


def ones_times(mask, v):
    ones = jnp.where(mask, 1.0, 0.0).astype(bf16)
    high = v.astype(bf16)
    rest = v - high.astype(f32)
    middle = rest.astype(bf16)
    low = (rest - middle.astype(f32)).astype(bf16)
    return nn(ones, high) + (nn(ones, middle) + nn(ones, low))


def both(own, par):
    return jnp.concatenate([own[...], par[...]], axis=1)


def project_kernel(
    info, own, sib, k_own, v_own, u_own, kvu, down, key, value, raw, csum, state, acc
):
    half = pl.program_id(0)
    width = own.shape[1]
    k_par, v_par, u_par = kvu.at[:width, :HK], kvu.at[:width, HK:], kvu.at[width:, :HK]
    i, j = rows_cols()
    up = both(u_own, u_par).astype(f32)

    @pl.when(half == 0)
    def _():
        acc[...] = jnp.zeros_like(acc)

    for t in range(PER):
        r = slice(t * ROWS, (t + 1) * ROWS)
        x = pick(info, half, own, sib, r)
        low = nt(x, down[...])
        raws = nn(low, up[:16], highest) + up[16:17]
        raw[r] = raws
        decay = (jnp.minimum(raws, 0.0) - jnp.log1p(jnp.exp(-jnp.abs(raws)))) * (1.0 / 16.0)
        k = nn(x, both(k_own, k_par)).astype(bf16)
        key[r] = k
        v0 = nn(x, v_own[...]).astype(bf16)
        v1 = nn(x, v_par[...]).astype(bf16)
        value[r, :HV] = v0
        value[r, HV:] = v1
        csum[r] = ones_times(block_low(), decay)
        rest = ones_times(j > i, decay)
        total = rest[0:1] + decay[0:1]
        base = info[1] + (half * PER + t) * ROWS
        last = scalar_start(info, base + ROWS - 1)
        pos = base + lax.broadcasted_iota(jnp.int32, (ROWS, 1), 0)
        tail = jnp.where(pos >= last, 1.0, 0.0)
        alive = jnp.where((last < base) & (half + t > 0), 1.0, 0.0)
        ks = (k.astype(f32) * jnp.exp(rest) * tail).astype(bf16)
        keep = jnp.exp(total) * alive
        for h, v in enumerate((v0, v1)):
            hs = slice(h * HK, (h + 1) * HK)
            acc[h] = acc[h] * keep[:, hs] + tn(v, ks[:, hs])

    @pl.when(half == HALVES - 1)
    def _():
        state[0] = acc[1].astype(bf16)
        state[1] = acc[0].astype(bf16)


def factors(info, s, cs):
    base = info[1] + s * ROWS
    row = lax.broadcasted_iota(jnp.int32, (ROWS, 1), 0)
    pos = base + row
    start = doc_start(info, pos)
    living = jnp.where(start < base + (row // SPAN) * SPAN, 1.0, 0.0)
    final = doc_start(info, base + (row // SPAN) * SPAN + SPAN - 1)
    tail = jnp.where(pos >= final, 1.0, 0.0)
    alive = []
    for b in range(NB):
        first = base + b * SPAN
        alive.append(jnp.where(scalar_start(info, first + SPAN - 1) < first, 1.0, 0.0))
    i, j = rows_cols()
    mask = block_low() & (base + j >= start)
    return living, tail, alive, mask


def forward_kernel(
    info, own, sib, q_own, o_own, qo, gain, key, value, csum, entering,
    query, gate_out, mixed, merged, states, acc,
):
    half = pl.program_id(0)
    q_par, o_par = qo.at[:, :HK], qo.at[:, HK : HK + HV]

    @pl.when(half == 0)
    def _():
        acc[...] = entering[...].astype(f32)

    sts = [acc[0], acc[1]]
    for t in range(PER):
        r = slice(t * ROWS, (t + 1) * ROWS)
        x = pick(info, half, own, sib, r)
        living, tail, alive, mask = factors(info, half * PER + t, None)
        q = nn(x, both(q_own, q_par)).astype(bf16)
        query[r] = q
        for h in range(2):
            w = o_own if h == 0 else o_par
            hs, vs = slice(h * HK, (h + 1) * HK), slice(h * HV, (h + 1) * HV)
            go = nn(x, w[...])
            gate_out[r, vs] = go.astype(bf16)
            cs = csum[r, hs]
            centre, last = spread(cs, SPAN // 2), spread(cs, SPAN - 1)
            qt = q[:, hs].astype(f32) * scale_q
            k = key[r, hs].astype(f32)
            v = value[r, vs]
            qe = (qt * jnp.exp(cs - centre)).astype(bf16)
            ke = (k * jnp.exp(centre - cs)).astype(bf16)
            qc = (qt * jnp.exp(cs) * living).astype(bf16)
            kt = (k * jnp.exp(last - cs) * tail).astype(bf16)
            scores = jnp.where(mask, nt(qe, ke), 0.0).astype(bf16)
            inside = nn(scores, v)
            st = sts[h]
            carried = []
            for b in range(NB):
                rb = slice(b * SPAN, (b + 1) * SPAN)
                stb = st.astype(bf16)
                states[t, h, b] = stb
                carried.append(nt(qc[rb], stb))
                f = jnp.exp(cs[(b + 1) * SPAN - 1 : (b + 1) * SPAN]) * alive[b]
                st = st * f + tn(v[rb], kt[rb])
            sts[h] = st
            mix = inside + jnp.concatenate(carried, axis=0)
            mixed[r, vs] = mix.astype(bf16)
            inv = lax.rsqrt(jnp.mean(mix * mix, axis=-1, keepdims=True) + group_floor)
            merged[r, vs] = (mix * inv * gain[...] * (go * sigmoid(go))).astype(bf16)
    acc[0] = sts[0]
    acc[1] = sts[1]


def gate_back_kernel(
    info, own, sib, out_own, out_par, gain, mixed, gate_out, query, csum,
    mixed_grad, gate_grad, gain_grad, enter_grad, acc, carry,
):
    half = pl.program_id(0)

    @pl.when(half == 0)
    def _():
        acc[...] = jnp.zeros_like(acc)
        carry[...] = jnp.zeros_like(carry)
        gain_grad[...] = jnp.zeros_like(gain_grad)

    gn = gain[...]
    total = jnp.zeros_like(gn)
    for h in range(2):
        hs, vs = slice(h * HK, (h + 1) * HK), slice(h * HV, (h + 1) * HV)
        offset = carry[:, hs]
        for t in range(PER):
            r = slice(t * ROWS, (t + 1) * ROWS)
            g = pick(info, half, own, sib, r)
            base = info[1] + (half * PER + t) * ROWS
            pos = base + lax.broadcasted_iota(jnp.int32, (ROWS, 1), 0)
            living = jnp.where(doc_start(info, pos) < info[1], 1.0, 0.0)
            wo = out_own if h == 0 else out_par
            mg = nt(g, wo[...]).astype(bf16).astype(f32)
            mix = mixed[r, vs].astype(f32)
            go = gate_out[r, vs].astype(f32)
            inv = lax.rsqrt(jnp.mean(mix * mix, axis=-1, keepdims=True) + group_floor)
            n = mix * inv
            sg = sigmoid(go)
            silu = go * sg
            ng = mg * n
            dgo = (ng * gn * (sg + silu * (1.0 - sg))).astype(bf16)
            gate_grad[r, vs] = dgo
            total = total + jnp.sum(ng * silu, axis=0, keepdims=True)
            dn = mg * gn * silu
            do = (inv * (dn - n * jnp.mean(dn * n, axis=-1, keepdims=True))).astype(bf16)
            mixed_grad[r, vs] = do
            cs = csum[r, hs]
            parts = []
            for b in range(NB):
                parts.append(cs[b * SPAN : (b + 1) * SPAN] + offset)
                offset = offset + cs[(b + 1) * SPAN - 1 : (b + 1) * SPAN]
            qcc = (
                query[r, hs].astype(f32) * scale_q * jnp.exp(jnp.concatenate(parts, axis=0)) * living
            )
            acc[h] += tn(do, qcc.astype(bf16))
        carry[:, hs] = offset
    gain_grad[...] += total

    @pl.when(half == HALVES - 1)
    def _():
        enter_grad[0] = acc[1].astype(bf16)
        enter_grad[1] = acc[0].astype(bf16)


def backward_kernel(
    info, own, sib, *rest,
):
    width = own.shape[1]
    if len(rest) == 18:
        kvu, qo, *rest = rest
        q_w, o_w = qo.at[:, :HK], qo.at[:, HK : HK + HV]
        k_w, v_w, u_w = kvu.at[:width, :HK], kvu.at[:width, HK:], kvu.at[width:, :HK]
    else:
        q_w, o_w, k_w, v_w, u_w, *rest = rest
    down, query, key, value, csum, raw, mixed_grad, gate_grad, states, leaving, *rest = rest
    given, rest = (rest[:1], rest[1:]) if len(rest) == 8 else ((), rest)
    kvq_grad, up_grad, bias_grad, down_grad, *outs, acc = rest
    step = pl.program_id(0)
    half = HALVES - 1 - step

    @pl.when(step == 0)
    def _():
        acc[...] = leaving[0].astype(f32)
        up_grad[...] = jnp.zeros_like(up_grad)
        bias_grad[...] = jnp.zeros_like(bias_grad)
        down_grad[...] = jnp.zeros_like(down_grad)

    i, j = rows_cols()
    upper = (i <= j) & (i // SPAN == j // SPAN)
    up = u_w[:16].astype(f32)
    w_qk = jnp.concatenate([q_w[...], k_w[...]], axis=1)
    gt = acc[...]
    lows, ranks, grads, backs = [None] * PER, [None] * PER, [None] * PER, [None] * PER
    for t in reversed(range(PER)):
        r = slice(t * ROWS, (t + 1) * ROWS)
        x = pick(info, half, own, sib, r)
        living, tail, alive, mask = factors(info, half * PER + t, None)
        cs = csum[r]
        centre, last = spread(cs, SPAN // 2), spread(cs, SPAN - 1)
        qt = query[r].astype(f32) * scale_q
        k = key[r].astype(f32)
        v = value[r]
        do = mixed_grad[r]
        eq, ek = jnp.exp(cs - centre), jnp.exp(centre - cs)
        ec, et = jnp.exp(cs) * living, jnp.exp(last - cs) * tail
        qe, ke = (qt * eq).astype(bf16), (k * ek).astype(bf16)
        qcf, ktf = qt * ec, k * et
        qc, kt = qcf.astype(bf16), ktf.astype(bf16)
        scores = jnp.where(mask, nt(qe, ke), 0.0).astype(bf16)
        ds = jnp.where(mask, nt(do, v), 0.0).astype(bf16)
        dqe = nn(ds, ke)
        dke = tn(ds, qe)
        dv = tn(scores, do)
        dqc, dkt, dvt, dlast = [None] * NB, [None] * NB, [None] * NB, [None] * NB
        for b in reversed(range(NB)):
            rb = slice(b * SPAN, (b + 1) * SPAN)
            gtb = gt.astype(bf16)
            st = states[t, 0, b]
            dvt[b] = nt(kt[rb], gtb)
            dkt[b] = nn(v[rb], gtb)
            dqc[b] = nn(do[rb], st)
            f = jnp.exp(cs[(b + 1) * SPAN - 1 : (b + 1) * SPAN]) * alive[b]
            moved = f * jnp.sum(st.astype(f32) * gt, axis=0, keepdims=True)
            tails = jnp.sum(ktf[rb] * dkt[b], axis=0, keepdims=True)
            dlast[b] = jnp.broadcast_to(moved + tails, (SPAN, HK))
            gt = gt * f + tn(do[rb], qc[rb])
        dqc = jnp.concatenate(dqc, axis=0)
        dkt = jnp.concatenate(dkt, axis=0)
        dv = (dv + jnp.concatenate(dvt, axis=0)).astype(bf16)
        dq = ((dqe * eq + dqc * ec) * scale_q).astype(bf16)
        dk = (dke * ek + dkt * et).astype(bf16)
        dc = qe.astype(f32) * dqe - ke.astype(f32) * dke + qcf * dqc - ktf * dkt
        ddecay = ones_times(upper, dc) + jnp.concatenate(dlast, axis=0)
        raw_grad = ddecay * sigmoid(-raw[r]) * (1.0 / 16.0)
        kvq_grad[r, :HK] = dk
        kvq_grad[r, HK : HK + HV] = dv
        kvq_grad[r, HK + HV :] = dq
        rank_low = nt(raw_grad, up, highest).astype(bf16)
        lows[t] = nt(x, down[...])
        ranks[t], grads[t] = rank_low, raw_grad
        back = nt(dv, v_w[...]) + nt(gate_grad[r], o_w[...]) + nn(rank_low, down[...])
        back = back + nt(jnp.concatenate([dq, dk], axis=1), w_qk)
        if given:
            backs[t] = (back + given[0][r].astype(f32)).astype(bf16)
        else:
            outs[0][r] = back.astype(bf16)
    acc[...] = gt
    raw_grad = jnp.concatenate(grads, axis=0)
    up_grad[...] += tn(jnp.concatenate(lows, axis=0), raw_grad, highest)
    bias_grad[...] += jnp.sum(raw_grad, axis=0, keepdims=True)
    down_grad[...] += tn(
        jnp.concatenate(ranks, axis=0), jnp.where(half == info[0], own[...], sib[...])
    )
    if not given:
        return
    use_own = half == info[0]
    back = jnp.concatenate(backs, axis=0)

    @pl.when(use_own)
    def _():
        outs[0][...] = back

    @pl.when(jnp.logical_not(use_own))
    def _():
        outs[1][...] = back


def ffn_kernel(
    place, n_a, n_b, g_a, g_b, gate_w, up_w, down_w, *rest,
):
    hidden, gate_grad, up_grad, n_cat, g_cat, feed_a, feed_b, back_a, back_b = rest[-9:]
    i = pl.program_id(0)
    first = i < pl.num_programs(0) // 2
    n = jnp.where(first, n_a[...], n_b[...])
    g = jnp.where(first, g_a[...], g_b[...])
    n_cat[...] = n
    g_cat[...] = g
    gate = nt(n, gate_w[...])
    up = nt(n, up_w[...])
    gh = nt(g, down_w[...]).astype(bf16).astype(f32)
    sg = sigmoid(gate)
    silu = gate * sg
    hid = (silu * up).astype(bf16)
    gg = (gh * up * (sg + silu * (1.0 - sg))).astype(bf16)
    ug = (gh * silu).astype(bf16)
    hidden[...] = hid
    gate_grad[...] = gg
    up_grad[...] = ug
    feed = nn(hid, down_w[...]).astype(bf16)
    back = (nn(gg, gate_w[...]) + nn(ug, up_w[...])).astype(bf16)

    @pl.when(first)
    def _():
        feed_a[...] = feed
        back_a[...] = back

    @pl.when(jnp.logical_not(first))
    def _():
        feed_b[...] = feed
        back_b[...] = back


def ffn_grad_kernel(h, gg, ug, n, g, out, acc):
    units = h.shape[1]
    i = pl.program_id(0)

    @pl.when(i == 0)
    def _():
        acc[...] = jnp.zeros_like(acc)

    for k, (left, right) in enumerate(((gg, n), (ug, n), (h, g))):
        rows = slice(k * units, (k + 1) * units)
        acc[rows] += tn(left[...], right[...])

    @pl.when(i == pl.num_programs(0) - 1)
    def _():
        out[...] = acc[...].astype(out.dtype)


def ffn_grad_call(arrays, dtype, name, us):
    rows, units = arrays[0].shape
    width = arrays[3].shape[1]
    step = GRAD_ROWS
    out = jax.ShapeDtypeStruct((3 * units, width), dtype)
    return pl.pallas_call(
        ffn_grad_kernel,
        out_shape=out_hbm(out),
        grid=(rows // step,),
        in_specs=[pl.BlockSpec((step, a.shape[1]), lambda i: (i, 0)) for a in arrays],
        out_specs=whole(out),
        scratch_shapes=[pltpu.VMEM((3 * units, width), f32)],
        compiler_params=params(40),
        cost_estimate=cost(us),
        name=name,
    )(*[in_hbm(a) for a in arrays])


def resid_back_kernel(info, own, sib, got0, got1, resid, g, gain, resid_grad, low, gain_grad):
    i = pl.program_id(0)
    got = jnp.where(i == 0, got0[...], got1[...])
    back = own[...].astype(f32) + sib[...].astype(f32) + got.astype(f32)
    res = resid[...]
    scale = lax.rsqrt(jnp.mean(res * res, axis=-1, keepdims=True) + epsilon)
    unit = res * scale
    scaled = back * gain[...]
    grad = g[...].astype(f32) + scale * (
        scaled - unit * jnp.mean(scaled * unit, axis=-1, keepdims=True)
    )
    resid_grad[...] = grad
    low[...] = grad.astype(bf16)
    part = jnp.sum(back * unit, axis=0, keepdims=True)

    @pl.when(i == 0)
    def _():
        gain_grad[...] = part

    @pl.when(i > 0)
    def _():
        gain_grad[...] += part


def input_back_kernel(info, own, sib, x, resid_grad, gain, input_grad, gain_grad):
    i = pl.program_id(0)
    back = own[...].astype(f32) + sib[...].astype(f32)
    values = x[...].astype(f32)
    scale = lax.rsqrt(jnp.mean(values * values, axis=-1, keepdims=True) + epsilon)
    unit = values * scale
    scaled = back * gain[...]
    grad = resid_grad[...] + scale * (
        scaled - unit * jnp.mean(scaled * unit, axis=-1, keepdims=True)
    )
    input_grad[...] = grad.astype(bf16)
    part = jnp.sum(back * unit, axis=0, keepdims=True)

    @pl.when(i == 0)
    def _():
        gain_grad[...] = part

    @pl.when(i > 0)
    def _():
        gain_grad[...] += part


def turn_kernel(high, own, got, key, value, query, down, gain_one, gain_two, gain, decay, bias):
    swap = high[0] == 1
    low = jnp.where(swap, got[...], own[...]).astype(f32)
    up = jnp.where(swap, own[...], got[...]).astype(f32)
    half = own.shape[0]
    key[...] = low[:HK].T
    rest = HK + HV - half
    value[:, : half - HK] = low[HK:].T
    value[:, half - HK :] = up[:rest].T
    query[...] = up[rest : rest + HK].T
    few = up[rest + HK :]
    down[...] = few[:16]
    gain_one[...] = few[16:17]
    gain_two[...] = few[17:18]
    gain[...] = few[18:19, :HV]
    decay[...] = few[19:35, :HK]
    bias[...] = few[35:36, :HK]


def params(mib):
    return pltpu.CompilerParams(
        dimension_semantics=("arbitrary",), vmem_limit_bytes=mib * 1024 * 1024
    )


def cost(us):
    return pl.CostEstimate(flops=us * 1_000_000_000, transcendentals=0, bytes_accessed=us * 1_000_000)


def in_hbm(a):
    return pltpu.with_memory_space_constraint(a, pltpu.HBM)


def out_hbm(a):
    return pltpu.HBM(a.shape, a.dtype)


def whole(a):
    zero = (0,) * a.ndim
    return pl.BlockSpec(a.shape, lambda *_: zero)


def resident():
    return pl.BlockSpec(memory_space=pltpu.VMEM)


def mixer_call(
    kernel, info, ins, outs, scratch, name, us, mib, reverse=False, block=PER * ROWS
):
    steps = HALVES

    def at(s):
        return steps - 1 - s if reverse else s

    def spec(a, kind):
        if isinstance(kind, tuple) and kind[0] == "col":
            return pl.BlockSpec((block, kind[2]), lambda s, info: (at(s), kind[1]))
        if isinstance(kind, tuple) and kind[0] == "phycol":
            return pl.BlockSpec((block, kind[2]), lambda s, info: ((at(s) + info[0]) % 2, kind[1]))
        if isinstance(kind, tuple) and kind[0] == "head":
            return pl.BlockSpec(
                (a.shape[0] // steps, 1, *a.shape[2:]), lambda s, info: (at(s), kind[1], 0, 0, 0)
            )
        if isinstance(kind, tuple) and kind[0] == "one":
            return pl.BlockSpec((1, *a.shape[1:]), lambda s, info: (kind[1], 0, 0))
        if kind == "seq":
            return pl.BlockSpec((block, a.shape[1]), lambda s, info: (at(s), 0))
        if kind == "phy":
            return pl.BlockSpec((block, a.shape[1]), lambda s, info: ((at(s) + info[0]) % 2, 0))
        if kind == "blk":
            zero = (0,) * (a.ndim - 1)
            return pl.BlockSpec((a.shape[0] // steps, *a.shape[1:]), lambda s, info: (at(s), *zero))
        return whole(a)

    return pl.pallas_call(
        kernel,
        out_shape=[out_hbm(a) for a, _ in outs],
        grid_spec=pltpu.PrefetchScalarGridSpec(
            num_scalar_prefetch=1,
            grid=(steps,),
            in_specs=[spec(a, kind) for a, kind in ins],
            out_specs=[spec(a, kind) for a, kind in outs],
            scratch_shapes=scratch,
        ),
        compiler_params=params(mib),
        cost_estimate=cost(us),
        name=name,
    )(info, *[in_hbm(a) for a, _ in ins])


def ffn_call(place, n_a, n_b, g_a, g_b, gate_w, up_w, down_w, name, flip, part=0, given=()):
    rows, width = n_a.shape
    units = gate_w.shape[0]
    steps = 2 * rows // ROWS
    half = steps // 2
    per = 2
    done = 2 * (flip + part)
    at = part + (flip // 2) * per

    def g_low(i, place):
        here = (place[0] ^ flip) * per + part if flip else 0
        return here + jnp.minimum(i, half - 1), 0

    def g_high(i, place):
        here = (place[0] ^ (flip + 1)) * per + part if flip else 0
        return here + jnp.maximum(i - half, 0), 0

    def low(first):
        return pl.BlockSpec((ROWS, width), lambda i, place: (first + jnp.minimum(i, half - 1), 0))

    def high(first):
        return pl.BlockSpec((ROWS, width), lambda i, place: (first + jnp.maximum(i - half, 0), 0))

    cat = pl.BlockSpec((ROWS, width), lambda i, place: (done + i, 0))
    mid = pl.BlockSpec((ROWS, units), lambda i, place: (done + i, 0))
    hbm = pl.BlockSpec(memory_space=pl.ANY)
    every = 4 * per * ROWS

    def out(count, cols):
        return pltpu.HBM((count, cols), bf16)

    return pl.pallas_call(
        ffn_kernel,
        out_shape=[out(every, units)] * 3
        + [out(every, width)] * 2
        + [out(2 * per * ROWS, width)] * 2
        + [out(rows, width)] * 2,
        grid_spec=pltpu.PrefetchScalarGridSpec(
            num_scalar_prefetch=1,
            grid=(steps,),
            in_specs=[low(0), high(0), pl.BlockSpec((ROWS, width), g_low), pl.BlockSpec((ROWS, width), g_high)]
            + [whole(w) for w in (gate_w, up_w, down_w)]
            + [hbm] * len(given),
            out_specs=[mid, mid, mid, cat, cat, low(at), high(at), low(0), high(0)],
        ),
        input_output_aliases={8 + k: k for k in range(len(given))},
        compiler_params=params(32),
        cost_estimate=cost(3 * steps + 2),
        name=name,
    )(place, *[in_hbm(a) for a in (n_a, n_b, g_a, g_b)], *[in_hbm(w) for w in (gate_w, up_w, down_w)], *[in_hbm(a) for a in given])


def across(v, bit):
    return lax.ppermute(v, "narrow", [(i, i ^ bit) for i in range(4)])


def forth(v):
    return lax.ppermute(v, "narrow", [(0, 2), (1, 3)])


def back_to(v):
    return lax.ppermute(v, "narrow", [(2, 0), (3, 1)])


def after(v, *others):
    return lax.optimization_barrier((v, *others))[0]


def pairs(count, bit):
    return [(i, i ^ bit) for i in range(count)]


def wide_send(v, bit, count):
    half = v.shape[0] // 2
    high = (lax.axis_index("wide") // bit) % 2
    keep = lax.dynamic_slice_in_dim(v, high * half, half, 0)
    send = lax.dynamic_slice_in_dim(v, (1 - high) * half, half, 0)
    return keep, lax.ppermute(send, "wide", pairs(count, bit))


def wide_add(keep, got, *earlier):
    got = after(got, *earlier) if earlier else got
    return (keep.astype(f32) + got.astype(f32)).astype(bf16)


class Exchange:
    def __init__(self, arrays, orders, count):
        self.arrays, self.orders, self.count, self.step = arrays, orders, count, 0

    def begin(self, keeps, sends):
        self.sent = [
            (keep, lax.ppermute(send, "wide", pairs(self.count, order[0])))
            for keep, send, order in zip(keeps, sends, self.orders)
        ]

    def send(self):
        n = len(self.orders[0])
        self.sent = []
        for v, order in zip(self.arrays, self.orders):
            if self.step < n:
                self.sent.append(wide_send(v, order[self.step], self.count))
            else:
                got = lax.ppermute(v, "wide", pairs(self.count, order[2 * n - 1 - self.step]))
                self.sent.append((v, got))

    def take(self, *earlier):
        n = len(self.orders[0])
        arrays = []
        for (keep, got), order in zip(self.sent, self.orders):
            if self.step < n:
                arrays.append(wide_add(keep, got, *earlier))
            else:
                got = after(got, *earlier) if earlier else got
                high = (lax.axis_index("wide") // order[2 * n - 1 - self.step]) % 2
                arrays.append(
                    jnp.where(
                        high == 0,
                        jnp.concatenate([keep, got], 0),
                        jnp.concatenate([got, keep], 0),
                    )
                )
        self.arrays = arrays
        self.step += 1

    def tie(self, v):
        v, *self.arrays = lax.optimization_barrier((v, *self.arrays))
        return v

    def finish(self, fresh=False):
        if not fresh:
            self.take()
        while self.step < 2 * len(self.orders[0]):
            self.send()
            self.take()
        return self.arrays


def wide_pieces(v, count):
    return lax.all_to_all(
        v.reshape(count, v.shape[0] // count, v.shape[1]), "wide", 0, 0, tiled=True
    )


def added(pieces):
    return jnp.sum(pieces.astype(f32), axis=0).astype(bf16)


def wide_copies(v, count):
    spread_out = jnp.broadcast_to(v[None], (count, *v.shape))
    got = lax.all_to_all(spread_out, "wide", 0, 0, tiled=True)
    return got.reshape(count * v.shape[0], v.shape[1])


def body(
    count, block_input, doc_lengths, mixer_gain, query_proj, key_proj, value_proj, outgate_proj,
    decay_down, decay_up, decay_bias, group_gain, output_proj, ffn_gain, gate_proj, up_proj,
    down_proj, cotangent,
):
    sds = jax.ShapeDtypeStruct
    rows, width = block_input.shape
    chip = 2 * rows
    place = lax.axis_index("narrow")
    lengths = doc_lengths[0]
    e1 = lengths[0]
    e2 = e1 + lengths[1]
    e3 = e2 + lengths[2]
    info = jnp.stack([place % 2, (place // 2) * chip, e1, e2, e3]).astype(jnp.int32)

    u_own = jnp.concatenate(
        [decay_up, decay_bias[None, :], jnp.zeros((15, decay_up.shape[1]), bf16)], axis=0
    )
    kvu_own = jnp.concatenate(
        [
            jnp.concatenate([key_proj, value_proj], axis=1),
            jnp.pad(u_own, ((0, 0), (0, HV))),
        ],
        axis=0,
    )
    kvu = across(kvu_own, 2)
    inputs = after(block_input, kvu_own).astype(f32)
    scale_one = lax.rsqrt(jnp.mean(inputs * inputs, axis=-1, keepdims=True) + epsilon)
    unit_one = inputs * scale_one
    gain_one = mixer_gain.astype(f32)
    n_own = (unit_one * gain_one).astype(bf16)
    n_sib = across(n_own, 1)
    out_flat = output_proj.reshape(width, HV)
    qo = across(
        after(jnp.concatenate([query_proj, outgate_proj, out_flat], axis=1), n_own), 2
    )
    out_par = qo[:, HK + HV :].reshape(HV, width)
    down_t = decay_down.T

    group = group_gain.astype(f32)[None, :]
    key, value, raw, csum, state = mixer_call(
        project_kernel, info,
        [(n_own, "own"), (n_sib, "sib"), (key_proj, "vmem"), (value_proj, "vmem"), (u_own, "vmem"),
         (kvu, "vmem"), (down_t, "vmem")],
        [(sds((chip, 2 * HK), bf16), "seq"), (sds((chip, 2 * HV), bf16), "seq"),
         (sds((chip, 2 * HK), f32), "seq"), (sds((chip, 2 * HK), f32), "seq"),
         (sds((2, HV, HK), bf16), "all")],
        [pltpu.VMEM((2, HV, HK), f32)], "project", 10, 24,
    )
    entering = forth(state)
    g_sib = across(after(cotangent, state), 1)
    g_all = lax.all_gather(after(cotangent, qo, state), "narrow", axis=0, tiled=True)
    query, gate_out, mixed, merged, states = mixer_call(
        forward_kernel, info,
        [(n_own, "own"), (n_sib, "sib"), (query_proj, "vmem"), (outgate_proj, "vmem"), (qo, "vmem"), (group, "vmem"), (key, "seq"), (value, "seq"), (csum, "seq"), (entering, "vmem")],
        [(sds((chip, 2 * HK), bf16), "seq"), (sds((chip, 2 * HV), bf16), "seq"),
         (sds((chip, 2 * HV), bf16), "seq"), (sds((chip, 2 * HV), bf16), "phy"),
         (sds((4, 2, NB, HV, HK), bf16), "blk")],
        [pltpu.VMEM((2, HV, HK), f32)], "mixer_forward", 11, 32,
    )
    out_w = jnp.concatenate([output_proj, out_par], axis=0)
    att_sib = across(nn(merged[rows:], out_w).astype(bf16), 1)
    resid = inputs + nn(merged[:rows], out_w) + att_sib.astype(f32)
    scale_two = lax.rsqrt(jnp.mean(resid * resid, axis=-1, keepdims=True) + epsilon)
    gain_two = ffn_gain.astype(f32)[None, :]
    m_own = (resid * scale_two * gain_two).astype(bf16)
    m_0, m_1 = m_own[: rows // 2], m_own[rows // 2 :]
    m_sib = across(m_own, 1)
    m_x0 = across(m_0, 2)
    m_x1 = across(m_1, 2)
    gate_t, up_t = gate_proj.T, up_proj.T
    spot = place.astype(jnp.int32)[None]
    near = ffn_call(spot, m_own, m_sib, cotangent, g_sib, gate_t, up_t, down_proj, "ffn_near", 0)
    m_s0 = across(after(m_x0, near[0]), 1)
    far0 = ffn_call(
        spot, m_x0, m_s0, g_all, g_all, gate_t, up_t, down_proj, "ffn_far", 2, 0, near[:7]
    )
    m_s1 = across(after(m_x1, far0[0]), 1)
    far1 = ffn_call(
        spot, after(m_x1, far0[0]), m_s1, g_all, g_all, gate_t, up_t, down_proj, "ffn_far", 2, 1, far0[:7]
    )
    near_got = across(near[8], 1)
    back_x = [far[7] + across(far[8], 1) for far in (far0, far1)]
    back_got = [across(v, 2) for v in back_x]
    parts = [after(v, *back_x) for v in far1[:5]]
    bits = [1 << b for b in range(count.bit_length() - 1)]
    turned = bits[1:2] + bits[:1] + bits[2:]
    ffn_grads = ffn_grad_call(parts, bf16, "ffn_grads", 18)
    ffn_part = lax.psum_scatter(ffn_grads, "wide", scatter_dimension=0, tiled=True)
    resid_grad, r_own, grad_ffn_gain = mixer_call(
        resid_back_kernel, info,
        [(near[7], "seq"), (near_got, "seq"), (after(back_got[0], ffn_grads), "all"),
         (back_got[1], "all"), (resid, "seq"), (cotangent, "seq"), (gain_two, "all")],
        [(sds((rows, width), f32), "seq"), (sds((rows, width), bf16), "seq"),
         (sds((1, width), f32), "all")],
        [], "resid_back", 3, 24, block=ROWS,
    )
    r_sib = across(r_own, 1)


    mixed_grad, gate_grad, gain_grad, enter_grad = mixer_call(
        gate_back_kernel, info,
        [(r_own, "own"), (r_sib, "sib"), (output_proj, "vmem"), (out_par, "vmem"), (group, "vmem"),
         (mixed, "seq"), (gate_out, "seq"), (query, "seq"), (csum, "seq")],
        [(sds((chip, 2 * HV), bf16), "seq"), (sds((chip, 2 * HV), bf16), "phy"),
         (sds((1, HV), f32), "all"), (sds((2, HV, HK), bf16), "all")],
        [pltpu.VMEM((2, HV, HK), f32), pltpu.VMEM((1, 2 * HK), f32)], "gate_backward", 6, 32,
    )
    leaving = back_to(enter_grad)
    n_cat = jnp.concatenate([n_own, n_sib], axis=0)
    r_cat = after(jnp.concatenate([r_own, r_sib], axis=0), enter_grad)
    out_grad = tn(merged, r_cat)
    early = jnp.concatenate([out_grad[HV:], tn(gate_grad[:, HV:], n_cat)], axis=0).astype(bf16)
    early_got = across(after(early, leaving), 2)
    def backward(h, weights, given, name):
        outs = [(sds((chip, 2 * HK + HV), bf16), "phy"), (sds((16, HK), f32), "all"),
                (sds((1, HK), f32), "all"), (sds((16, width), f32), "all")]
        if given:
            outs += [(sds((rows, width), bf16), "own"), (sds((rows, width), bf16), "sib")]
        else:
            outs += [(sds((chip, width), bf16), "seq")]
        return mixer_call(
            backward_kernel, info,
            [(n_own, "own"), (n_sib, "sib"), *[(w, "vmem") for w in weights],
             (down_t, "vmem"), (query, ("col", h, HK)),
             (key, ("col", h, HK)), (value, ("col", h, HV)), (csum, ("col", h, HK)),
             (raw, ("col", h, HK)), (mixed_grad, ("col", h, HV)), (gate_grad, ("phycol", h, HV)),
             (states, ("head", h)), (leaving, ("one", h))] + [(a, "seq") for a in given],
            outs, [pltpu.VMEM((HV, HK), f32)], name, 10, 32, reverse=True,
        )

    kvq_grad_par, up_par_grad, bias_par_grad, down_par_grad, back_part = backward(
        1, (kvu, qo), (), "mixer_backward_par"
    )
    kvq_par = tn(kvq_grad_par, n_cat).astype(bf16)
    kvq_got = across(kvq_par, 2)
    feed_a, feed_b = far1[5:7]
    feed_got = across(after(feed_b, back_part), 1)
    feed_far = across(feed_a[rows:] + feed_got[rows:], 2)
    feed = feed_a[:rows].astype(f32) + feed_got[:rows].astype(f32) + feed_far.astype(f32)
    block_output = (resid + feed).astype(bf16)
    early_got = after(early_got, back_part)
    early_sum = jnp.concatenate(
        [out_grad[:HV] + early_got[:HV].astype(f32),
         tn(gate_grad[:, :HV], n_cat) + early_got[HV:].astype(f32)], axis=0
    ).astype(bf16)
    second = Exchange([early_sum], [turned], count)
    back_part = second.tie(back_part)
    second.send()
    kvq_grad_own, up_own_grad, bias_own_grad, down_own_grad, back_own, back_s = backward(
        0, (query_proj, outgate_proj, key_proj, value_proj, u_own), (back_part,),
        "mixer_backward_own",
    )
    input_grad, grad_mixer_gain = mixer_call(
        input_back_kernel, info,
        [(after(back_own, kvq_got), "seq"), (across(back_s, 1), "seq"), (block_input, "seq"),
         (resid_grad, "seq"), (gain_one[None, :], "all")],
        [(sds((rows, width), bf16), "seq"), (sds((1, width), f32), "all")],
        [], "input_back", 5, 24, block=ROWS,
    )

    kvq_sum = (tn(kvq_grad_own, n_cat) + kvq_got.astype(f32)).astype(bf16)
    decay_own = jnp.concatenate([up_own_grad, bias_own_grad], axis=0)
    decay_par = jnp.concatenate([up_par_grad, bias_par_grad], axis=0)
    small = jnp.concatenate(
        [down_own_grad + down_par_grad, grad_mixer_gain, grad_ffn_gain,
         jnp.pad(gain_grad, ((0, 0), (0, width - HV)))], axis=0
    )
    small = small + across(small, 1)

    def wide_rows(v):
        return jnp.pad(v, ((0, 0), (0, width - HK)))

    got = across(jnp.concatenate([small, wide_rows(decay_par)], axis=0), 2)
    few = got + jnp.concatenate([small, wide_rows(decay_own)], axis=0)
    few = jnp.pad(few, ((0, 28), (0, 0))).astype(bf16)
    second.take(back_s)
    second.send()
    [second] = second.finish()
    second = second.astype(f32)
    packed = jnp.concatenate([kvq_sum, few], axis=0)
    ffn_sum = lax.all_gather(after(ffn_part, packed), "wide", axis=0, tiled=True).astype(f32)
    first = Exchange([packed], [bits], count)
    for step in range(2 * len(bits) - 1):
        first.send()
        if step == 2 * len(bits) - 2:
            first.take(ffn_sum)
        else:
            first.take()
    first.send()
    [(own_half, got_half)] = first.sent
    high = (lax.axis_index("wide") % 2).astype(jnp.int32)[None]
    turned_shapes = [
        sds(shape, f32)
        for shape in (
            (width, HK), (width, HV), (width, HK), (16, width), (1, width), (1, width),
            (1, HV), (16, HK), (1, HK),
        )
    ]
    (key_sum, value_sum, query_sum, down_sum, one_sum, two_sum, group_sum, decay_sum,
     bias_sum) = pl.pallas_call(
        turn_kernel,
        out_shape=[out_hbm(a) for a in turned_shapes],
        grid_spec=pltpu.PrefetchScalarGridSpec(
            num_scalar_prefetch=1,
            grid=(1,),
            in_specs=[whole(own_half), whole(got_half)],
            out_specs=[whole(a) for a in turned_shapes],
        ),
        compiler_params=params(24),
        cost_estimate=cost(3),
        name="turn",
    )(high, in_hbm(own_half), in_hbm(got_half))
    grad_gate, grad_up, grad_down = jnp.split(ffn_sum, 3, axis=0)
    grad_gate, grad_up = grad_gate.T, grad_up.T
    return (
        block_output,
        input_grad,
        one_sum[0],
        query_sum,
        key_sum,
        value_sum,
        second[HV:].T,
        down_sum.T,
        decay_sum,
        bias_sum[0],
        group_sum[0],
        second[:HV],
        two_sum[0],
        grad_gate,
        grad_up,
        grad_down,
    )


def solution(mesh):
    placed = (
        P(("wide", "narrow"), None),
        P("wide", None),
        P(),
        P(None, "narrow"),
        P(None, "narrow"),
        P(None, "narrow"),
        P(None, "narrow"),
        P(),
        P(None, "narrow"),
        P("narrow"),
        P(),
        P("narrow", None),
        P(),
        P(None, "narrow"),
        P(None, "narrow"),
        P("narrow", None),
        P(("wide", "narrow"), None),
    )
    return jax.shard_map(
        functools.partial(body, mesh.shape["wide"]),
        mesh=mesh,
        in_specs=placed,
        out_specs=(
            P(("wide", "narrow"), None),
            P(("wide", "narrow"), None),
            P(),
            P(None, "narrow"),
            P(None, "narrow"),
            P(None, "narrow"),
            P(None, "narrow"),
            P(),
            P(None, "narrow"),
            P("narrow"),
            P(),
            P("narrow", None),
            P(),
            P(None, "narrow"),
            P(None, "narrow"),
            P("narrow", None),
        ),
        check_vma=False,
    )
```

```python
import functools

import jax
import jax.numpy as jnp
from jax import lax
from jax.experimental import pallas as pl
from jax.experimental.pallas import tpu as pltpu
from jax.sharding import PartitionSpec as P

HK = 128
HV = 256
SPAN = 64
ROWS = 256
NB = ROWS // SPAN
PER = 2
HALVES = 2
GRAD_ROWS = 512

epsilon = 1e-06
group_floor = 0.25
highest = lax.Precision.HIGHEST
f32 = jnp.float32
bf16 = jnp.bfloat16
scale_q = HK ** (-0.5)


def nn(a, b, precision=None):
    return lax.dot_general(
        a, b, (((1,), (0,)), ((), ())), precision=precision, preferred_element_type=f32
    )


def nt(a, b, precision=None):
    return lax.dot_general(
        a, b, (((1,), (1,)), ((), ())), precision=precision, preferred_element_type=f32
    )


def tn(a, b, precision=None):
    return lax.dot_general(
        a, b, (((0,), (0,)), ((), ())), precision=precision, preferred_element_type=f32
    )


def sigmoid(v):
    return 1.0 / (1.0 + jnp.exp(-v))


def rows_cols():
    i = lax.broadcasted_iota(jnp.int32, (ROWS, ROWS), 0)
    j = lax.broadcasted_iota(jnp.int32, (ROWS, ROWS), 1)
    return i, j


def block_low():
    i, j = rows_cols()
    return (i >= j) & (i // SPAN == j // SPAN)


def doc_start(info, pos):
    e1, e2, e3 = info[2], info[3], info[4]
    start = jnp.where(pos >= e1, e1, 0)
    start = jnp.where(pos >= e2, e2, start)
    return jnp.where(pos >= e3, e3, start)


def scalar_start(info, pos):
    e1, e2, e3 = info[2], info[3], info[4]
    start = jnp.where(pos >= e1, e1, 0)
    start = jnp.where(pos >= e2, e2, start)
    return jnp.where(pos >= e3, e3, start)


def spread(v, row):
    return jnp.concatenate(
        [
            jnp.broadcast_to(v[b * SPAN + row : b * SPAN + row + 1], (SPAN, v.shape[1]))
            for b in range(NB)
        ],
        axis=0,
    )


def pick(info, half, own, sib, r):
    return jnp.where(half == info[0], own[r], sib[r])


def ones_times(mask, v):
    ones = jnp.where(mask, 1.0, 0.0).astype(bf16)
    high = v.astype(bf16)
    rest = v - high.astype(f32)
    middle = rest.astype(bf16)
    low = (rest - middle.astype(f32)).astype(bf16)
    return nn(ones, high) + (nn(ones, middle) + nn(ones, low))


def both(own, par):
    return jnp.concatenate([own[...], par[...]], axis=1)


def project_kernel(
    info, own, sib, k_own, v_own, u_own, kvu, down, key, value, raw, csum, state, acc
):
    half = pl.program_id(0)
    width = own.shape[1]
    k_par, v_par, u_par = kvu.at[:width, :HK], kvu.at[:width, HK:], kvu.at[width:, :HK]
    i, j = rows_cols()
    up = both(u_own, u_par).astype(f32)

    @pl.when(half == 0)
    def _():
        acc[...] = jnp.zeros_like(acc)

    for t in range(PER):
        r = slice(t * ROWS, (t + 1) * ROWS)
        x = pick(info, half, own, sib, r)
        low = nt(x, down[...])
        raws = nn(low, up[:16], highest) + up[16:17]
        raw[r] = raws
        decay = (jnp.minimum(raws, 0.0) - jnp.log1p(jnp.exp(-jnp.abs(raws)))) * (1.0 / 16.0)
        k = nn(x, both(k_own, k_par)).astype(bf16)
        key[r] = k
        v0 = nn(x, v_own[...]).astype(bf16)
        v1 = nn(x, v_par[...]).astype(bf16)
        value[r, :HV] = v0
        value[r, HV:] = v1
        csum[r] = ones_times(block_low(), decay)
        rest = ones_times(j > i, decay)
        total = rest[0:1] + decay[0:1]
        base = info[1] + (half * PER + t) * ROWS
        last = scalar_start(info, base + ROWS - 1)
        pos = base + lax.broadcasted_iota(jnp.int32, (ROWS, 1), 0)
        tail = jnp.where(pos >= last, 1.0, 0.0)
        alive = jnp.where((last < base) & (half + t > 0), 1.0, 0.0)
        ks = (k.astype(f32) * jnp.exp(rest) * tail).astype(bf16)
        keep = jnp.exp(total) * alive
        for h, v in enumerate((v0, v1)):
            hs = slice(h * HK, (h + 1) * HK)
            acc[h] = acc[h] * keep[:, hs] + tn(v, ks[:, hs])

    @pl.when(half == HALVES - 1)
    def _():
        state[0] = acc[1].astype(bf16)
        state[1] = acc[0].astype(bf16)


def factors(info, s, cs):
    base = info[1] + s * ROWS
    row = lax.broadcasted_iota(jnp.int32, (ROWS, 1), 0)
    pos = base + row
    start = doc_start(info, pos)
    living = jnp.where(start < base + (row // SPAN) * SPAN, 1.0, 0.0)
    final = doc_start(info, base + (row // SPAN) * SPAN + SPAN - 1)
    tail = jnp.where(pos >= final, 1.0, 0.0)
    alive = []
    for b in range(NB):
        first = base + b * SPAN
        alive.append(jnp.where(scalar_start(info, first + SPAN - 1) < first, 1.0, 0.0))
    i, j = rows_cols()
    mask = block_low() & (base + j >= start)
    return living, tail, alive, mask


def forward_kernel(
    info, own, sib, q_own, o_own, qo, gain, key, value, csum, entering,
    query, gate_out, mixed, merged, states, acc,
):
    half = pl.program_id(0)
    q_par, o_par = qo.at[:, :HK], qo.at[:, HK : HK + HV]

    @pl.when(half == 0)
    def _():
        acc[...] = entering[...].astype(f32)

    sts = [acc[0], acc[1]]
    for t in range(PER):
        r = slice(t * ROWS, (t + 1) * ROWS)
        x = pick(info, half, own, sib, r)
        living, tail, alive, mask = factors(info, half * PER + t, None)
        q = nn(x, both(q_own, q_par)).astype(bf16)
        query[r] = q
        for h in range(2):
            w = o_own if h == 0 else o_par
            hs, vs = slice(h * HK, (h + 1) * HK), slice(h * HV, (h + 1) * HV)
            go = nn(x, w[...])
            gate_out[r, vs] = go.astype(bf16)
            cs = csum[r, hs]
            centre, last = spread(cs, SPAN // 2), spread(cs, SPAN - 1)
            qt = q[:, hs].astype(f32) * scale_q
            k = key[r, hs].astype(f32)
            v = value[r, vs]
            qe = (qt * jnp.exp(cs - centre)).astype(bf16)
            ke = (k * jnp.exp(centre - cs)).astype(bf16)
            qc = (qt * jnp.exp(cs) * living).astype(bf16)
            kt = (k * jnp.exp(last - cs) * tail).astype(bf16)
            scores = jnp.where(mask, nt(qe, ke), 0.0).astype(bf16)
            inside = nn(scores, v)
            st = sts[h]
            carried = []
            for b in range(NB):
                rb = slice(b * SPAN, (b + 1) * SPAN)
                stb = st.astype(bf16)
                states[t, h, b] = stb
                carried.append(nt(qc[rb], stb))
                f = jnp.exp(cs[(b + 1) * SPAN - 1 : (b + 1) * SPAN]) * alive[b]
                st = st * f + tn(v[rb], kt[rb])
            sts[h] = st
            mix = inside + jnp.concatenate(carried, axis=0)
            mixed[r, vs] = mix.astype(bf16)
            inv = lax.rsqrt(jnp.mean(mix * mix, axis=-1, keepdims=True) + group_floor)
            merged[r, vs] = (mix * inv * gain[...] * (go * sigmoid(go))).astype(bf16)
    acc[0] = sts[0]
    acc[1] = sts[1]


def gate_back_kernel(
    info, own, sib, out_own, out_par, gain, mixed, gate_out, query, csum,
    mixed_grad, gate_grad, gain_grad, enter_grad, acc, carry,
):
    half = pl.program_id(0)

    @pl.when(half == 0)
    def _():
        acc[...] = jnp.zeros_like(acc)
        carry[...] = jnp.zeros_like(carry)
        gain_grad[...] = jnp.zeros_like(gain_grad)

    gn = gain[...]
    total = jnp.zeros_like(gn)
    for h in range(2):
        hs, vs = slice(h * HK, (h + 1) * HK), slice(h * HV, (h + 1) * HV)
        offset = carry[:, hs]
        for t in range(PER):
            r = slice(t * ROWS, (t + 1) * ROWS)
            g = pick(info, half, own, sib, r)
            base = info[1] + (half * PER + t) * ROWS
            pos = base + lax.broadcasted_iota(jnp.int32, (ROWS, 1), 0)
            living = jnp.where(doc_start(info, pos) < info[1], 1.0, 0.0)
            wo = out_own if h == 0 else out_par
            mg = nt(g, wo[...]).astype(bf16).astype(f32)
            mix = mixed[r, vs].astype(f32)
            go = gate_out[r, vs].astype(f32)
            inv = lax.rsqrt(jnp.mean(mix * mix, axis=-1, keepdims=True) + group_floor)
            n = mix * inv
            sg = sigmoid(go)
            silu = go * sg
            ng = mg * n
            dgo = (ng * gn * (sg + silu * (1.0 - sg))).astype(bf16)
            gate_grad[r, vs] = dgo
            total = total + jnp.sum(ng * silu, axis=0, keepdims=True)
            dn = mg * gn * silu
            do = (inv * (dn - n * jnp.mean(dn * n, axis=-1, keepdims=True))).astype(bf16)
            mixed_grad[r, vs] = do
            cs = csum[r, hs]
            parts = []
            for b in range(NB):
                parts.append(cs[b * SPAN : (b + 1) * SPAN] + offset)
                offset = offset + cs[(b + 1) * SPAN - 1 : (b + 1) * SPAN]
            qcc = (
                query[r, hs].astype(f32) * scale_q * jnp.exp(jnp.concatenate(parts, axis=0)) * living
            )
            acc[h] += tn(do, qcc.astype(bf16))
        carry[:, hs] = offset
    gain_grad[...] += total

    @pl.when(half == HALVES - 1)
    def _():
        enter_grad[0] = acc[1].astype(bf16)
        enter_grad[1] = acc[0].astype(bf16)


def backward_kernel(
    info, own, sib, *rest,
):
    width = own.shape[1]
    if len(rest) == 18:
        kvu, qo, *rest = rest
        q_w, o_w = qo.at[:, :HK], qo.at[:, HK : HK + HV]
        k_w, v_w, u_w = kvu.at[:width, :HK], kvu.at[:width, HK:], kvu.at[width:, :HK]
    else:
        q_w, o_w, k_w, v_w, u_w, *rest = rest
    down, query, key, value, csum, raw, mixed_grad, gate_grad, states, leaving, *rest = rest
    given, rest = (rest[:1], rest[1:]) if len(rest) == 8 else ((), rest)
    kvq_grad, up_grad, bias_grad, down_grad, *outs, acc = rest
    step = pl.program_id(0)
    half = HALVES - 1 - step

    @pl.when(step == 0)
    def _():
        acc[...] = leaving[0].astype(f32)
        up_grad[...] = jnp.zeros_like(up_grad)
        bias_grad[...] = jnp.zeros_like(bias_grad)
        down_grad[...] = jnp.zeros_like(down_grad)

    i, j = rows_cols()
    upper = (i <= j) & (i // SPAN == j // SPAN)
    up = u_w[:16].astype(f32)
    w_qk = jnp.concatenate([q_w[...], k_w[...]], axis=1)
    gt = acc[...]
    lows, ranks, grads, backs = [None] * PER, [None] * PER, [None] * PER, [None] * PER
    for t in reversed(range(PER)):
        r = slice(t * ROWS, (t + 1) * ROWS)
        x = pick(info, half, own, sib, r)
        living, tail, alive, mask = factors(info, half * PER + t, None)
        cs = csum[r]
        centre, last = spread(cs, SPAN // 2), spread(cs, SPAN - 1)
        qt = query[r].astype(f32) * scale_q
        k = key[r].astype(f32)
        v = value[r]
        do = mixed_grad[r]
        eq, ek = jnp.exp(cs - centre), jnp.exp(centre - cs)
        ec, et = jnp.exp(cs) * living, jnp.exp(last - cs) * tail
        qe, ke = (qt * eq).astype(bf16), (k * ek).astype(bf16)
        qcf, ktf = qt * ec, k * et
        qc, kt = qcf.astype(bf16), ktf.astype(bf16)
        scores = jnp.where(mask, nt(qe, ke), 0.0).astype(bf16)
        ds = jnp.where(mask, nt(do, v), 0.0).astype(bf16)
        dqe = nn(ds, ke)
        dke = tn(ds, qe)
        dv = tn(scores, do)
        dqc, dkt, dvt, dlast = [None] * NB, [None] * NB, [None] * NB, [None] * NB
        for b in reversed(range(NB)):
            rb = slice(b * SPAN, (b + 1) * SPAN)
            gtb = gt.astype(bf16)
            st = states[t, 0, b]
            dvt[b] = nt(kt[rb], gtb)
            dkt[b] = nn(v[rb], gtb)
            dqc[b] = nn(do[rb], st)
            f = jnp.exp(cs[(b + 1) * SPAN - 1 : (b + 1) * SPAN]) * alive[b]
            moved = f * jnp.sum(st.astype(f32) * gt, axis=0, keepdims=True)
            tails = jnp.sum(ktf[rb] * dkt[b], axis=0, keepdims=True)
            dlast[b] = jnp.broadcast_to(moved + tails, (SPAN, HK))
            gt = gt * f + tn(do[rb], qc[rb])
        dqc = jnp.concatenate(dqc, axis=0)
        dkt = jnp.concatenate(dkt, axis=0)
        dv = (dv + jnp.concatenate(dvt, axis=0)).astype(bf16)
        dq = ((dqe * eq + dqc * ec) * scale_q).astype(bf16)
        dk = (dke * ek + dkt * et).astype(bf16)
        dc = qe.astype(f32) * dqe - ke.astype(f32) * dke + qcf * dqc - ktf * dkt
        ddecay = ones_times(upper, dc) + jnp.concatenate(dlast, axis=0)
        raw_grad = ddecay * sigmoid(-raw[r]) * (1.0 / 16.0)
        kvq_grad[r, :HK] = dk
        kvq_grad[r, HK : HK + HV] = dv
        kvq_grad[r, HK + HV :] = dq
        rank_low = nt(raw_grad, up, highest).astype(bf16)
        lows[t] = nt(x, down[...])
        ranks[t], grads[t] = rank_low, raw_grad
        back = nt(dv, v_w[...]) + nt(gate_grad[r], o_w[...]) + nn(rank_low, down[...])
        back = back + nt(jnp.concatenate([dq, dk], axis=1), w_qk)
        if given:
            backs[t] = (back + given[0][r].astype(f32)).astype(bf16)
        else:
            outs[0][r] = back.astype(bf16)
    acc[...] = gt
    raw_grad = jnp.concatenate(grads, axis=0)
    up_grad[...] += tn(jnp.concatenate(lows, axis=0), raw_grad, highest)
    bias_grad[...] += jnp.sum(raw_grad, axis=0, keepdims=True)
    down_grad[...] += tn(
        jnp.concatenate(ranks, axis=0), jnp.where(half == info[0], own[...], sib[...])
    )
    if not given:
        return
    use_own = half == info[0]
    back = jnp.concatenate(backs, axis=0)

    @pl.when(use_own)
    def _():
        outs[0][...] = back

    @pl.when(jnp.logical_not(use_own))
    def _():
        outs[1][...] = back


def ffn_kernel(
    place, n_a, n_b, g_a, g_b, gate_w, up_w, down_w, *rest,
):
    hidden, gate_grad, up_grad, n_cat, g_cat, feed_a, feed_b, back_a, back_b = rest[-9:]
    i = pl.program_id(0)
    first = i < pl.num_programs(0) // 2
    n = jnp.where(first, n_a[...], n_b[...])
    g = jnp.where(first, g_a[...], g_b[...])
    n_cat[...] = n
    g_cat[...] = g
    gate = nt(n, gate_w[...])
    up = nt(n, up_w[...])
    gh = nt(g, down_w[...]).astype(bf16).astype(f32)
    sg = sigmoid(gate)
    silu = gate * sg
    hid = (silu * up).astype(bf16)
    gg = (gh * up * (sg + silu * (1.0 - sg))).astype(bf16)
    ug = (gh * silu).astype(bf16)
    hidden[...] = hid
    gate_grad[...] = gg
    up_grad[...] = ug
    feed = nn(hid, down_w[...]).astype(bf16)
    back = (nn(gg, gate_w[...]) + nn(ug, up_w[...])).astype(bf16)

    @pl.when(first)
    def _():
        feed_a[...] = feed
        back_a[...] = back

    @pl.when(jnp.logical_not(first))
    def _():
        feed_b[...] = feed
        back_b[...] = back


def ffn_grad_kernel(h, gg, ug, n, g, out, acc):
    units = h.shape[1]
    i = pl.program_id(0)

    @pl.when(i == 0)
    def _():
        acc[...] = jnp.zeros_like(acc)

    for k, (left, right) in enumerate(((gg, n), (ug, n), (h, g))):
        rows = slice(k * units, (k + 1) * units)
        acc[rows] += tn(left[...], right[...])

    @pl.when(i == pl.num_programs(0) - 1)
    def _():
        out[...] = acc[...].astype(out.dtype)


def ffn_grad_call(arrays, dtype, name, us):
    rows, units = arrays[0].shape
    width = arrays[3].shape[1]
    step = GRAD_ROWS
    out = jax.ShapeDtypeStruct((3 * units, width), dtype)
    return pl.pallas_call(
        ffn_grad_kernel,
        out_shape=out_hbm(out),
        grid=(rows // step,),
        in_specs=[pl.BlockSpec((step, a.shape[1]), lambda i: (i, 0)) for a in arrays],
        out_specs=whole(out),
        scratch_shapes=[pltpu.VMEM((3 * units, width), f32)],
        compiler_params=params(40),
        cost_estimate=cost(us),
        name=name,
    )(*[in_hbm(a) for a in arrays])


def resid_back_kernel(info, own, sib, got0, got1, resid, g, gain, resid_grad, low, gain_grad):
    i = pl.program_id(0)
    got = jnp.where(i == 0, got0[...], got1[...])
    back = own[...].astype(f32) + sib[...].astype(f32) + got.astype(f32)
    res = resid[...]
    scale = lax.rsqrt(jnp.mean(res * res, axis=-1, keepdims=True) + epsilon)
    unit = res * scale
    scaled = back * gain[...]
    grad = g[...].astype(f32) + scale * (
        scaled - unit * jnp.mean(scaled * unit, axis=-1, keepdims=True)
    )
    resid_grad[...] = grad
    low[...] = grad.astype(bf16)
    part = jnp.sum(back * unit, axis=0, keepdims=True)

    @pl.when(i == 0)
    def _():
        gain_grad[...] = part

    @pl.when(i > 0)
    def _():
        gain_grad[...] += part


def input_back_kernel(info, own, sib, x, resid_grad, gain, input_grad, gain_grad):
    i = pl.program_id(0)
    back = own[...].astype(f32) + sib[...].astype(f32)
    values = x[...].astype(f32)
    scale = lax.rsqrt(jnp.mean(values * values, axis=-1, keepdims=True) + epsilon)
    unit = values * scale
    scaled = back * gain[...]
    grad = resid_grad[...] + scale * (
        scaled - unit * jnp.mean(scaled * unit, axis=-1, keepdims=True)
    )
    input_grad[...] = grad.astype(bf16)
    part = jnp.sum(back * unit, axis=0, keepdims=True)

    @pl.when(i == 0)
    def _():
        gain_grad[...] = part

    @pl.when(i > 0)
    def _():
        gain_grad[...] += part


def turn_kernel(high, own, got, key, value, query, down, gain_one, gain_two, gain, decay, bias):
    swap = high[0] == 1
    low = jnp.where(swap, got[...], own[...]).astype(f32)
    up = jnp.where(swap, own[...], got[...]).astype(f32)
    half = own.shape[0]
    key[...] = low[:HK].T
    rest = HK + HV - half
    value[:, : half - HK] = low[HK:].T
    value[:, half - HK :] = up[:rest].T
    query[...] = up[rest : rest + HK].T
    few = up[rest + HK :]
    down[...] = few[:16]
    gain_one[...] = few[16:17]
    gain_two[...] = few[17:18]
    gain[...] = few[18:19, :HV]
    decay[...] = few[19:35, :HK]
    bias[...] = few[35:36, :HK]


def params(mib):
    return pltpu.CompilerParams(
        dimension_semantics=("arbitrary",), vmem_limit_bytes=mib * 1024 * 1024
    )


def cost(us):
    return pl.CostEstimate(flops=us * 1_000_000_000, transcendentals=0, bytes_accessed=us * 1_000_000)


def in_hbm(a):
    return pltpu.with_memory_space_constraint(a, pltpu.HBM)


def out_hbm(a):
    return pltpu.HBM(a.shape, a.dtype)


def whole(a):
    zero = (0,) * a.ndim
    return pl.BlockSpec(a.shape, lambda *_: zero)


def resident():
    return pl.BlockSpec(memory_space=pltpu.VMEM)


def mixer_call(
    kernel, info, ins, outs, scratch, name, us, mib, reverse=False, block=PER * ROWS
):
    steps = HALVES

    def at(s):
        return steps - 1 - s if reverse else s

    def spec(a, kind):
        if isinstance(kind, tuple) and kind[0] == "col":
            return pl.BlockSpec((block, kind[2]), lambda s, info: (at(s), kind[1]))
        if isinstance(kind, tuple) and kind[0] == "phycol":
            return pl.BlockSpec((block, kind[2]), lambda s, info: ((at(s) + info[0]) % 2, kind[1]))
        if isinstance(kind, tuple) and kind[0] == "head":
            return pl.BlockSpec(
                (a.shape[0] // steps, 1, *a.shape[2:]), lambda s, info: (at(s), kind[1], 0, 0, 0)
            )
        if isinstance(kind, tuple) and kind[0] == "one":
            return pl.BlockSpec((1, *a.shape[1:]), lambda s, info: (kind[1], 0, 0))
        if kind == "seq":
            return pl.BlockSpec((block, a.shape[1]), lambda s, info: (at(s), 0))
        if kind == "phy":
            return pl.BlockSpec((block, a.shape[1]), lambda s, info: ((at(s) + info[0]) % 2, 0))
        if kind == "blk":
            zero = (0,) * (a.ndim - 1)
            return pl.BlockSpec((a.shape[0] // steps, *a.shape[1:]), lambda s, info: (at(s), *zero))
        return whole(a)

    return pl.pallas_call(
        kernel,
        out_shape=[out_hbm(a) for a, _ in outs],
        grid_spec=pltpu.PrefetchScalarGridSpec(
            num_scalar_prefetch=1,
            grid=(steps,),
            in_specs=[spec(a, kind) for a, kind in ins],
            out_specs=[spec(a, kind) for a, kind in outs],
            scratch_shapes=scratch,
        ),
        compiler_params=params(mib),
        cost_estimate=cost(us),
        name=name,
    )(info, *[in_hbm(a) for a, _ in ins])


def ffn_call(place, n_a, n_b, g_a, g_b, gate_w, up_w, down_w, name, flip, part=0, given=()):
    rows, width = n_a.shape
    units = gate_w.shape[0]
    steps = 2 * rows // ROWS
    half = steps // 2
    per = 2
    done = 2 * (flip + part)
    at = part + (flip // 2) * per

    def g_low(i, place):
        here = (place[0] ^ flip) * per + part if flip else 0
        return here + jnp.minimum(i, half - 1), 0

    def g_high(i, place):
        here = (place[0] ^ (flip + 1)) * per + part if flip else 0
        return here + jnp.maximum(i - half, 0), 0

    def low(first):
        return pl.BlockSpec((ROWS, width), lambda i, place: (first + jnp.minimum(i, half - 1), 0))

    def high(first):
        return pl.BlockSpec((ROWS, width), lambda i, place: (first + jnp.maximum(i - half, 0), 0))

    cat = pl.BlockSpec((ROWS, width), lambda i, place: (done + i, 0))
    mid = pl.BlockSpec((ROWS, units), lambda i, place: (done + i, 0))
    hbm = pl.BlockSpec(memory_space=pl.ANY)
    every = 4 * per * ROWS

    def out(count, cols):
        return pltpu.HBM((count, cols), bf16)

    return pl.pallas_call(
        ffn_kernel,
        out_shape=[out(every, units)] * 3
        + [out(every, width)] * 2
        + [out(2 * per * ROWS, width)] * 2
        + [out(rows, width)] * 2,
        grid_spec=pltpu.PrefetchScalarGridSpec(
            num_scalar_prefetch=1,
            grid=(steps,),
            in_specs=[low(0), high(0), pl.BlockSpec((ROWS, width), g_low), pl.BlockSpec((ROWS, width), g_high)]
            + [resident() for w in (gate_w, up_w, down_w)]
            + [hbm] * len(given),
            out_specs=[mid, mid, mid, cat, cat, low(at), high(at), low(0), high(0)],
        ),
        input_output_aliases={8 + k: k for k in range(len(given))},
        compiler_params=params(32),
        cost_estimate=cost(3 * steps + 2),
        name=name,
    )(place, *[in_hbm(a) for a in (n_a, n_b, g_a, g_b)], *(gate_w, up_w, down_w), *[in_hbm(a) for a in given])


def across(v, bit):
    return lax.ppermute(v, "narrow", [(i, i ^ bit) for i in range(4)])


def forth(v):
    return lax.ppermute(v, "narrow", [(0, 2), (1, 3)])


def back_to(v):
    return lax.ppermute(v, "narrow", [(2, 0), (3, 1)])


def after(v, *others):
    return lax.optimization_barrier((v, *others))[0]


def pairs(count, bit):
    return [(i, i ^ bit) for i in range(count)]


def wide_send(v, bit, count):
    half = v.shape[0] // 2
    high = (lax.axis_index("wide") // bit) % 2
    keep = lax.dynamic_slice_in_dim(v, high * half, half, 0)
    send = lax.dynamic_slice_in_dim(v, (1 - high) * half, half, 0)
    return keep, lax.ppermute(send, "wide", pairs(count, bit))


def wide_add(keep, got, *earlier):
    got = after(got, *earlier) if earlier else got
    return (keep.astype(f32) + got.astype(f32)).astype(bf16)


class Exchange:
    def __init__(self, arrays, orders, count):
        self.arrays, self.orders, self.count, self.step = arrays, orders, count, 0

    def begin(self, keeps, sends):
        self.sent = [
            (keep, lax.ppermute(send, "wide", pairs(self.count, order[0])))
            for keep, send, order in zip(keeps, sends, self.orders)
        ]

    def send(self):
        n = len(self.orders[0])
        self.sent = []
        for v, order in zip(self.arrays, self.orders):
            if self.step < n:
                self.sent.append(wide_send(v, order[self.step], self.count))
            else:
                got = lax.ppermute(v, "wide", pairs(self.count, order[2 * n - 1 - self.step]))
                self.sent.append((v, got))

    def take(self, *earlier):
        n = len(self.orders[0])
        arrays = []
        for (keep, got), order in zip(self.sent, self.orders):
            if self.step < n:
                arrays.append(wide_add(keep, got, *earlier))
            else:
                got = after(got, *earlier) if earlier else got
                high = (lax.axis_index("wide") // order[2 * n - 1 - self.step]) % 2
                arrays.append(
                    jnp.where(
                        high == 0,
                        jnp.concatenate([keep, got], 0),
                        jnp.concatenate([got, keep], 0),
                    )
                )
        self.arrays = arrays
        self.step += 1

    def tie(self, v):
        v, *self.arrays = lax.optimization_barrier((v, *self.arrays))
        return v

    def finish(self, fresh=False):
        if not fresh:
            self.take()
        while self.step < 2 * len(self.orders[0]):
            self.send()
            self.take()
        return self.arrays


def wide_pieces(v, count):
    return lax.all_to_all(
        v.reshape(count, v.shape[0] // count, v.shape[1]), "wide", 0, 0, tiled=True
    )


def added(pieces):
    return jnp.sum(pieces.astype(f32), axis=0).astype(bf16)


def wide_copies(v, count):
    spread_out = jnp.broadcast_to(v[None], (count, *v.shape))
    got = lax.all_to_all(spread_out, "wide", 0, 0, tiled=True)
    return got.reshape(count * v.shape[0], v.shape[1])


def body(
    count, block_input, doc_lengths, mixer_gain, query_proj, key_proj, value_proj, outgate_proj,
    decay_down, decay_up, decay_bias, group_gain, output_proj, ffn_gain, gate_proj, up_proj,
    down_proj, cotangent,
):
    sds = jax.ShapeDtypeStruct
    rows, width = block_input.shape
    chip = 2 * rows
    place = lax.axis_index("narrow")
    lengths = doc_lengths[0]
    e1 = lengths[0]
    e2 = e1 + lengths[1]
    e3 = e2 + lengths[2]
    info = jnp.stack([place % 2, (place // 2) * chip, e1, e2, e3]).astype(jnp.int32)

    u_own = jnp.concatenate(
        [decay_up, decay_bias[None, :], jnp.zeros((15, decay_up.shape[1]), bf16)], axis=0
    )
    kvu_own = jnp.concatenate(
        [
            jnp.concatenate([key_proj, value_proj], axis=1),
            jnp.pad(u_own, ((0, 0), (0, HV))),
        ],
        axis=0,
    )
    kvu = across(kvu_own, 2)
    inputs = after(block_input, kvu_own).astype(f32)
    scale_one = lax.rsqrt(jnp.mean(inputs * inputs, axis=-1, keepdims=True) + epsilon)
    unit_one = inputs * scale_one
    gain_one = mixer_gain.astype(f32)
    n_own = (unit_one * gain_one).astype(bf16)
    n_sib = across(n_own, 1)
    out_flat = output_proj.reshape(width, HV)
    qo = across(
        after(jnp.concatenate([query_proj, outgate_proj, out_flat], axis=1), n_own), 2
    )
    out_par = qo[:, HK + HV :].reshape(HV, width)
    down_t = decay_down.T

    group = group_gain.astype(f32)[None, :]
    key, value, raw, csum, state = mixer_call(
        project_kernel, info,
        [(n_own, "own"), (n_sib, "sib"), (key_proj, "vmem"), (value_proj, "vmem"), (u_own, "vmem"),
         (kvu, "vmem"), (down_t, "vmem")],
        [(sds((chip, 2 * HK), bf16), "seq"), (sds((chip, 2 * HV), bf16), "seq"),
         (sds((chip, 2 * HK), f32), "seq"), (sds((chip, 2 * HK), f32), "seq"),
         (sds((2, HV, HK), bf16), "all")],
        [pltpu.VMEM((2, HV, HK), f32)], "project", 10, 24,
    )
    entering = forth(state)
    g_sib = across(after(cotangent, state), 1)
    g_all = lax.all_gather(after(cotangent, qo, state), "narrow", axis=0, tiled=True)
    query, gate_out, mixed, merged, states = mixer_call(
        forward_kernel, info,
        [(n_own, "own"), (n_sib, "sib"), (query_proj, "vmem"), (outgate_proj, "vmem"), (qo, "vmem"), (group, "vmem"), (key, "seq"), (value, "seq"), (csum, "seq"), (entering, "vmem")],
        [(sds((chip, 2 * HK), bf16), "seq"), (sds((chip, 2 * HV), bf16), "seq"),
         (sds((chip, 2 * HV), bf16), "seq"), (sds((chip, 2 * HV), bf16), "phy"),
         (sds((4, 2, NB, HV, HK), bf16), "blk")],
        [pltpu.VMEM((2, HV, HK), f32)], "mixer_forward", 11, 32,
    )
    out_w = jnp.concatenate([output_proj, out_par], axis=0)
    att_sib = across(nn(merged[rows:], out_w).astype(bf16), 1)
    resid = inputs + nn(merged[:rows], out_w) + att_sib.astype(f32)
    scale_two = lax.rsqrt(jnp.mean(resid * resid, axis=-1, keepdims=True) + epsilon)
    gain_two = ffn_gain.astype(f32)[None, :]
    m_own = (resid * scale_two * gain_two).astype(bf16)
    m_0, m_1 = m_own[: rows // 2], m_own[rows // 2 :]
    m_sib = across(m_own, 1)
    m_x0 = across(m_0, 2)
    m_x1 = across(m_1, 2)
    gate_t, up_t = gate_proj.T, up_proj.T
    spot = place.astype(jnp.int32)[None]
    near = ffn_call(spot, m_own, m_sib, cotangent, g_sib, gate_t, up_t, down_proj, "ffn_near", 0)
    m_s0 = across(after(m_x0, near[0]), 1)
    far0 = ffn_call(
        spot, m_x0, m_s0, g_all, g_all, gate_t, up_t, down_proj, "ffn_far", 2, 0, near[:7]
    )
    m_s1 = across(after(m_x1, far0[0]), 1)
    far1 = ffn_call(
        spot, after(m_x1, far0[0]), m_s1, g_all, g_all, gate_t, up_t, down_proj, "ffn_far", 2, 1, far0[:7]
    )
    near_got = across(near[8], 1)
    back_x = [far[7] + across(far[8], 1) for far in (far0, far1)]
    back_got = [across(v, 2) for v in back_x]
    parts = [after(v, *back_x) for v in far1[:5]]
    bits = [1 << b for b in range(count.bit_length() - 1)]
    turned = bits[1:2] + bits[:1] + bits[2:]
    ffn_grads = ffn_grad_call(parts, bf16, "ffn_grads", 18)
    ffn_part = lax.psum_scatter(ffn_grads, "wide", scatter_dimension=0, tiled=True)
    resid_grad, r_own, grad_ffn_gain = mixer_call(
        resid_back_kernel, info,
        [(near[7], "seq"), (near_got, "seq"), (after(back_got[0], ffn_grads), "all"),
         (back_got[1], "all"), (resid, "seq"), (cotangent, "seq"), (gain_two, "all")],
        [(sds((rows, width), f32), "seq"), (sds((rows, width), bf16), "seq"),
         (sds((1, width), f32), "all")],
        [], "resid_back", 3, 24, block=ROWS,
    )
    r_sib = across(r_own, 1)


    mixed_grad, gate_grad, gain_grad, enter_grad = mixer_call(
        gate_back_kernel, info,
        [(r_own, "own"), (r_sib, "sib"), (output_proj, "vmem"), (out_par, "vmem"), (group, "vmem"),
         (mixed, "seq"), (gate_out, "seq"), (query, "seq"), (csum, "seq")],
        [(sds((chip, 2 * HV), bf16), "seq"), (sds((chip, 2 * HV), bf16), "phy"),
         (sds((1, HV), f32), "all"), (sds((2, HV, HK), bf16), "all")],
        [pltpu.VMEM((2, HV, HK), f32), pltpu.VMEM((1, 2 * HK), f32)], "gate_backward", 6, 32,
    )
    leaving = back_to(enter_grad)
    n_cat = jnp.concatenate([n_own, n_sib], axis=0)
    r_cat = after(jnp.concatenate([r_own, r_sib], axis=0), enter_grad)
    out_grad = tn(merged, r_cat)
    early = jnp.concatenate([out_grad[HV:], tn(gate_grad[:, HV:], n_cat)], axis=0).astype(bf16)
    early_got = across(after(early, leaving), 2)
    def backward(h, weights, given, name):
        outs = [(sds((chip, 2 * HK + HV), bf16), "phy"), (sds((16, HK), f32), "all"),
                (sds((1, HK), f32), "all"), (sds((16, width), f32), "all")]
        if given:
            outs += [(sds((rows, width), bf16), "own"), (sds((rows, width), bf16), "sib")]
        else:
            outs += [(sds((chip, width), bf16), "seq")]
        return mixer_call(
            backward_kernel, info,
            [(n_own, "own"), (n_sib, "sib"), *[(w, "vmem") for w in weights],
             (down_t, "vmem"), (query, ("col", h, HK)),
             (key, ("col", h, HK)), (value, ("col", h, HV)), (csum, ("col", h, HK)),
             (raw, ("col", h, HK)), (mixed_grad, ("col", h, HV)), (gate_grad, ("phycol", h, HV)),
             (states, ("head", h)), (leaving, ("one", h))] + [(a, "seq") for a in given],
            outs, [pltpu.VMEM((HV, HK), f32)], name, 10, 32, reverse=True,
        )

    kvq_grad_par, up_par_grad, bias_par_grad, down_par_grad, back_part = backward(
        1, (kvu, qo), (), "mixer_backward_par"
    )
    kvq_par = tn(kvq_grad_par, n_cat).astype(bf16)
    kvq_got = across(kvq_par, 2)
    feed_a, feed_b = far1[5:7]
    feed_got = across(after(feed_b, back_part), 1)
    feed_far = across(feed_a[rows:] + feed_got[rows:], 2)
    feed = feed_a[:rows].astype(f32) + feed_got[:rows].astype(f32) + feed_far.astype(f32)
    block_output = (resid + feed).astype(bf16)
    early_got = after(early_got, back_part)
    early_sum = jnp.concatenate(
        [out_grad[:HV] + early_got[:HV].astype(f32),
         tn(gate_grad[:, :HV], n_cat) + early_got[HV:].astype(f32)], axis=0
    ).astype(bf16)
    second = Exchange([early_sum], [turned], count)
    back_part = second.tie(back_part)
    second.send()
    kvq_grad_own, up_own_grad, bias_own_grad, down_own_grad, back_own, back_s = backward(
        0, (query_proj, outgate_proj, key_proj, value_proj, u_own), (back_part,),
        "mixer_backward_own",
    )
    input_grad, grad_mixer_gain = mixer_call(
        input_back_kernel, info,
        [(after(back_own, kvq_got), "seq"), (across(back_s, 1), "seq"), (block_input, "seq"),
         (resid_grad, "seq"), (gain_one[None, :], "all")],
        [(sds((rows, width), bf16), "seq"), (sds((1, width), f32), "all")],
        [], "input_back", 5, 24, block=ROWS,
    )

    kvq_sum = (tn(kvq_grad_own, n_cat) + kvq_got.astype(f32)).astype(bf16)
    decay_own = jnp.concatenate([up_own_grad, bias_own_grad], axis=0)
    decay_par = jnp.concatenate([up_par_grad, bias_par_grad], axis=0)
    small = jnp.concatenate(
        [down_own_grad + down_par_grad, grad_mixer_gain, grad_ffn_gain,
         jnp.pad(gain_grad, ((0, 0), (0, width - HV)))], axis=0
    )
    small = small + across(small, 1)

    def wide_rows(v):
        return jnp.pad(v, ((0, 0), (0, width - HK)))

    got = across(jnp.concatenate([small, wide_rows(decay_par)], axis=0), 2)
    few = got + jnp.concatenate([small, wide_rows(decay_own)], axis=0)
    few = jnp.pad(few, ((0, 28), (0, 0))).astype(bf16)
    second.take(back_s)
    second.send()
    [second] = second.finish()
    second = second.astype(f32)
    packed = jnp.concatenate([kvq_sum, few], axis=0)
    ffn_sum = lax.all_gather(after(ffn_part, packed), "wide", axis=0, tiled=True).astype(f32)
    first = Exchange([packed], [bits], count)
    for step in range(2 * len(bits) - 1):
        first.send()
        if step == 2 * len(bits) - 2:
            first.take(ffn_sum)
        else:
            first.take()
    first.send()
    [(own_half, got_half)] = first.sent
    high = (lax.axis_index("wide") % 2).astype(jnp.int32)[None]
    turned_shapes = [
        sds(shape, f32)
        for shape in (
            (width, HK), (width, HV), (width, HK), (16, width), (1, width), (1, width),
            (1, HV), (16, HK), (1, HK),
        )
    ]
    (key_sum, value_sum, query_sum, down_sum, one_sum, two_sum, group_sum, decay_sum,
     bias_sum) = pl.pallas_call(
        turn_kernel,
        out_shape=[out_hbm(a) for a in turned_shapes],
        grid_spec=pltpu.PrefetchScalarGridSpec(
            num_scalar_prefetch=1,
            grid=(1,),
            in_specs=[whole(own_half), whole(got_half)],
            out_specs=[whole(a) for a in turned_shapes],
        ),
        compiler_params=params(24),
        cost_estimate=cost(3),
        name="turn",
    )(high, in_hbm(own_half), in_hbm(got_half))
    grad_gate, grad_up, grad_down = jnp.split(ffn_sum, 3, axis=0)
    grad_gate, grad_up = grad_gate.T, grad_up.T
    return (
        block_output,
        input_grad,
        one_sum[0],
        query_sum,
        key_sum,
        value_sum,
        second[HV:].T,
        down_sum.T,
        decay_sum,
        bias_sum[0],
        group_sum[0],
        second[:HV],
        two_sum[0],
        grad_gate,
        grad_up,
        grad_down,
    )


def solution(mesh):
    placed = (
        P(("wide", "narrow"), None),
        P("wide", None),
        P(),
        P(None, "narrow"),
        P(None, "narrow"),
        P(None, "narrow"),
        P(None, "narrow"),
        P(),
        P(None, "narrow"),
        P("narrow"),
        P(),
        P("narrow", None),
        P(),
        P(None, "narrow"),
        P(None, "narrow"),
        P("narrow", None),
        P(("wide", "narrow"), None),
    )
    return jax.shard_map(
        functools.partial(body, mesh.shape["wide"]),
        mesh=mesh,
        in_specs=placed,
        out_specs=(
            P(("wide", "narrow"), None),
            P(("wide", "narrow"), None),
            P(),
            P(None, "narrow"),
            P(None, "narrow"),
            P(None, "narrow"),
            P(None, "narrow"),
            P(),
            P(None, "narrow"),
            P("narrow"),
            P(),
            P("narrow", None),
            P(),
            P(None, "narrow"),
            P(None, "narrow"),
            P("narrow", None),
        ),
        check_vma=False,
    )
```
